32 devices in a mesh: dp: 8 (over z, x), rep: 4 (over y, core).
Axes of the slice: x: 2, y: 2, z: 4, core: 2. Of those that a mesh axis runs over, the one named last changes fastest.
Arguments:
- tokens: bfloat16 [128, 256, 512], P(('dp', 'rep')), may hold values from -6 to 6
- cotangent: bfloat16 [128, 256, 512], P(('dp', 'rep')), may hold values from -6 to 6
- target_lengths: int32 [128], P(('dp', 'rep')), may hold values from 32 to 256, as said below
- task_mask: int32 [128, 256], P(('dp', 'rep')), may hold values 0 or 1
- memory_lengths: int32 [128], P(('dp', 'rep')), may hold values from 256 to 1024, as said below
- position_buckets: int32 [256, 256], replicated, may hold values from 0 to 510
- memory: bfloat16 [8, 16, 1024, 512], P(None, 'rep', 'dp'), may hold values from -6 to 6
- self_gain: float32 [512], replicated, may hold values from 0.25 to 1.75
- self_shift: float32 [512], replicated, may hold values from -1.75 to 1.75
- query_weight: bfloat16 [512, 512], replicated, may hold values from -0.25 to 0.25
- query_bias: float32 [512], replicated, may hold values from -1.75 to 1.75
- key_weight: bfloat16 [512, 512], replicated, may hold values from -0.25 to 0.25
- value_weight: bfloat16 [512, 512], replicated, may hold values from -0.25 to 0.25
- value_bias: float32 [512], replicated, may hold values from -1.75 to 1.75
- position_table: float32 [511, 8], replicated, may hold values from -6 to 6
- head_scale: float32 [8], replicated, may hold values from 0.5 to 1.5
- output_weight: bfloat16 [512, 512], replicated, may hold values from -1 to 1
- output_bias: float32 [512], replicated, may hold values from -1.75 to 1.75
- cross_gain: float32 [512], replicated, may hold values from 0.25 to 1.75
- cross_shift: float32 [512], replicated, may hold values from -1.75 to 1.75
- cross_query: bfloat16 [512, 512], replicated, may hold values from -0.25 to 0.25
- cross_query_bias: float32 [512], replicated, may hold values from -1.75 to 1.75
- cross_key: bfloat16 [512, 512], replicated, may hold values from -0.25 to 0.25
- cross_value: bfloat16 [512, 512], replicated, may hold values from -0.25 to 0.25
- cross_value_bias: float32 [512], replicated, may hold values from -1.75 to 1.75
- post_gain: float32 [512], replicated, may hold values from 0.25 to 1.75
- post_shift: float32 [512], replicated, may hold values from -1.75 to 1.75
- cross_output: bfloat16 [512, 512], replicated, may hold values from -0.25 to 0.25
- cross_output_bias: float32 [512], replicated, may hold values from -1.75 to 1.75
- feed_gain: float32 [512], replicated, may hold values from 0.25 to 1.75
- feed_shift: float32 [512], replicated, may hold values from -1.75 to 1.75
- inner_weight: bfloat16 [512, 2048], replicated, may hold values from -0.25 to 0.25
- inner_bias: float32 [2048], replicated, may hold values from -1.75 to 1.75
- inner_gain: float32 [2048], replicated, may hold values from 0.25 to 1.75
- inner_shift: float32 [2048], replicated, may hold values from -1.75 to 1.75
- outer_weight: bfloat16 [2048, 512], replicated, may hold values from -0.125 to 0.125
- outer_bias: float32 [512], replicated, may hold values from -1.75 to 1.75
Outputs:
- layer_output: bfloat16 [128, 256, 512], P(('dp', 'rep'))
- tokens_gradient: bfloat16 [128, 256, 512], P(('dp', 'rep'))
- memory_gradient: bfloat16 [8, 16, 1024, 512], P(None, 'rep', 'dp')
- gradient_self_gain: float32 [512], replicated
- gradient_self_shift: float32 [512], replicated
- gradient_query_weight: float32 [512, 512], replicated
- gradient_query_bias: float32 [512], replicated
- gradient_key_weight: float32 [512, 512], replicated
- gradient_value_weight: float32 [512, 512], replicated
- gradient_value_bias: float32 [512], replicated
- gradient_position_table: float32 [511, 8], replicated
- gradient_head_scale: float32 [8], replicated
- gradient_output_weight: float32 [512, 512], replicated
- gradient_output_bias: float32 [512], replicated
- gradient_cross_gain: float32 [512], replicated
- gradient_cross_shift: float32 [512], replicated
- gradient_cross_query: float32 [512, 512], replicated
- gradient_cross_query_bias: float32 [512], replicated
- gradient_cross_key: float32 [512, 512], replicated
- gradient_cross_value: float32 [512, 512], replicated
- gradient_cross_value_bias: float32 [512], replicated
- gradient_post_gain: float32 [512], replicated
- gradient_post_shift: float32 [512], replicated
- gradient_cross_output: float32 [512, 512], replicated
- gradient_cross_output_bias: float32 [512], replicated
- gradient_feed_gain: float32 [512], replicated
- gradient_feed_shift: float32 [512], replicated
- gradient_inner_weight: float32 [512, 2048], replicated
- gradient_inner_bias: float32 [2048], replicated
- gradient_inner_gain: float32 [2048], replicated
- gradient_inner_shift: float32 [2048], replicated
- gradient_outer_weight: float32 [2048, 512], replicated
- gradient_outer_bias: float32 [512], replicated
The draws below stay inside these ranges and needn't reach their ends.
Inputs may be any that keep to these rules, and one draw needn't show every extreme that they name: `target_lengths`: some sequence has 256 real tokens in every draw; later positions are padding. `memory_lengths`: some sequence has all 1024 memory positions real in every draw.
All inputs are finite; a program needn't handle non-finite values. No bound on the sum of `task_mask` on one device may be relied on, other than what follows from the above.
Results may differ from the reference program's by a relative error of at most 0.017.
Values may be sent and summed in bfloat16 or wider, within the bound.
A program may use at most 192 MiB of HBM per device.

```python
import jax
import jax.numpy as jnp
from jax import lax

D = 512
H = 8
FF = 2048
NB = 511
SEQ_DEV = 4
LEN = 256
MLEN = 1024
SEQS = 128
GROUPS = 8
LANES = 16


def draw_target_lengths(key, part):
    base_draw = jax.random.randint(key, (SEQS,), LEN // 8, LEN + 1)
    chosen = jax.random.randint(jax.random.fold_in(key, 7), (), 0, SEQS)
    return jnp.where(jnp.arange(SEQS) == chosen, LEN, base_draw).astype(jnp.int32)


def draw_memory_lengths(key, part):
    base_draw = jax.random.randint(key, (SEQS,), MLEN // 4, MLEN + 1)
    chosen = jax.random.randint(jax.random.fold_in(key, 11), (), 0, SEQS)
    return jnp.where(jnp.arange(SEQS) == chosen, MLEN, base_draw).astype(jnp.int32)


def set_ends(array, own_key, least, high):
    place = [jax.random.randint(jax.random.fold_in(own_key, axis), (), 0, length) for axis, length in enumerate(array.shape)]
    widest = array.shape.index(max(array.shape))
    beside = place[:widest] + [(place[widest] + 1) % array.shape[widest]] + place[widest + 1:]
    return array.at[tuple(place)].set(least).at[tuple(beside)].set(high)


def levels(stream_key, dims, shards, least, top_value):
    loudness, own = 1.0, jax.random.fold_in(stream_key, 6)
    for position, parts in shards:
        steps = jnp.exp(jax.random.uniform(jax.random.fold_in(own, position), (parts,), jnp.float32, least / len(shards), top_value / len(shards)))
        loudness = loudness * jnp.repeat(steps, dims[position] // parts).reshape([-1 if axis == position else 1 for axis in range(len(dims))])
    return loudness


def bell_draw(rng, extent, width, limit, cuts=(), dtype=jnp.bfloat16):
    array = width * jax.random.normal(rng, extent, jnp.float32)
    if cuts:
        array = array * levels(rng, extent, cuts, -0.22, 0.18)
    return jnp.clip(array, -limit, limit).astype(dtype)


def setup_inputs(seed: int = 0) -> dict:
    arg_keys = jax.random.split(jax.random.key(seed), 38)
    tokens = bell_draw(arg_keys[0], (SEQS, LEN, D), 1.0, 6.0, ((0, 32),))
    cotangent = bell_draw(arg_keys[1], (SEQS, LEN, D), 1.0, 6.0, ((0, 32),))
    target_lengths = draw_target_lengths(jax.random.fold_in(arg_keys[37], 71), 0)
    task_mask = set_ends((jax.random.randint(arg_keys[3], (SEQS, LEN), 0, 4) < 3).astype(jnp.int32), jax.random.fold_in(arg_keys[3], 1), 0, 1)
    memory_lengths = draw_memory_lengths(jax.random.fold_in(arg_keys[37], 71), 0)
    position_buckets = set_ends(jax.random.randint(arg_keys[5], (LEN, LEN), 0, NB), jax.random.fold_in(arg_keys[5], 1), 0, NB - 1).astype(jnp.int32)
    memory = bell_draw(arg_keys[6], (GROUPS, LANES, MLEN, D), 1.0, 6.0, ((1, 4), (2, 8)))
    self_gain = jnp.clip(1.0 + 0.15 * jax.random.normal(arg_keys[7], (D,), jnp.float32), 0.25, 1.75)
    self_shift = bell_draw(arg_keys[8], (D,), 0.3, 1.75, (), jnp.float32)
    query_weight = bell_draw(arg_keys[9], (D, D), D ** -0.5, 0.25)
    query_bias = bell_draw(arg_keys[10], (D,), 0.3, 1.75, (), jnp.float32)
    key_weight = bell_draw(arg_keys[11], (D, D), D ** -0.5, 0.25)
    value_weight = bell_draw(arg_keys[12], (D, D), D ** -0.5, 0.25)
    value_bias = bell_draw(arg_keys[13], (D,), 0.3, 1.75, (), jnp.float32)
    position_table = bell_draw(arg_keys[14], (NB, H), 1.0, 6.0, (), jnp.float32)
    head_scale = jnp.clip(jax.random.uniform(arg_keys[15], (H,), jnp.float32, 0.5, 1.5), 0.5, 1.5)
    output_weight = bell_draw(arg_keys[16], (D, D), (D // 16) ** -0.5, 1.0)
    output_bias = bell_draw(arg_keys[17], (D,), 0.3, 1.75, (), jnp.float32)
    cross_gain = jnp.clip(1.0 + 0.15 * jax.random.normal(arg_keys[18], (D,), jnp.float32), 0.25, 1.75)
    cross_shift = bell_draw(arg_keys[19], (D,), 0.3, 1.75, (), jnp.float32)
    cross_query = bell_draw(arg_keys[20], (D, D), D ** -0.5, 0.25)
    cross_query_bias = bell_draw(arg_keys[21], (D,), 0.3, 1.75, (), jnp.float32)
    cross_key = bell_draw(arg_keys[22], (D, D), D ** -0.5, 0.25)
    cross_value = bell_draw(arg_keys[23], (D, D), D ** -0.5, 0.25)
    cross_value_bias = bell_draw(arg_keys[24], (D,), 0.3, 1.75, (), jnp.float32)
    post_gain = jnp.clip(1.0 + 0.15 * jax.random.normal(arg_keys[25], (D,), jnp.float32), 0.25, 1.75)
    post_shift = bell_draw(arg_keys[26], (D,), 0.3, 1.75, (), jnp.float32)
    cross_output = bell_draw(arg_keys[27], (D, D), D ** -0.5, 0.25)
    cross_output_bias = bell_draw(arg_keys[28], (D,), 0.3, 1.75, (), jnp.float32)
    feed_gain = jnp.clip(1.0 + 0.15 * jax.random.normal(arg_keys[29], (D,), jnp.float32), 0.25, 1.75)
    feed_shift = bell_draw(arg_keys[30], (D,), 0.3, 1.75, (), jnp.float32)
    inner_weight = bell_draw(arg_keys[31], (D, FF), D ** -0.5, 0.25)
    inner_bias = bell_draw(arg_keys[32], (FF,), 0.3, 1.75, (), jnp.float32)
    inner_gain = jnp.clip(1.0 + 0.15 * jax.random.normal(arg_keys[33], (FF,), jnp.float32), 0.25, 1.75)
    inner_shift = bell_draw(arg_keys[34], (FF,), 0.3, 1.75, (), jnp.float32)
    outer_weight = bell_draw(arg_keys[35], (FF, D), FF ** -0.5, 0.125)
    outer_bias = bell_draw(arg_keys[36], (D,), 0.3, 1.75, (), jnp.float32)
    return dict(tokens=tokens, cotangent=cotangent, target_lengths=target_lengths, task_mask=task_mask, memory_lengths=memory_lengths, position_buckets=position_buckets, memory=memory, self_gain=self_gain, self_shift=self_shift, query_weight=query_weight, query_bias=query_bias, key_weight=key_weight, value_weight=value_weight, value_bias=value_bias, position_table=position_table, head_scale=head_scale, output_weight=output_weight, output_bias=output_bias, cross_gain=cross_gain, cross_shift=cross_shift, cross_query=cross_query, cross_query_bias=cross_query_bias, cross_key=cross_key, cross_value=cross_value, cross_value_bias=cross_value_bias, post_gain=post_gain, post_shift=post_shift, cross_output=cross_output, cross_output_bias=cross_output_bias, feed_gain=feed_gain, feed_shift=feed_shift, inner_weight=inner_weight, inner_bias=inner_bias, inner_gain=inner_gain, inner_shift=inner_shift, outer_weight=outer_weight, outer_bias=outer_bias)


@jax.custom_vjp
def low(v):
    return lax.optimization_barrier(v.astype(jnp.bfloat16)).astype(jnp.float32)

@jax.custom_vjp
def low_back(v):
    return v

def low_keep(v):
    return (low(v), None)

def low_pass(kept, grad):
    return (grad,)

def back_keep(v):
    return (v, None)

def back_low(kept, grad):
    return (low(grad),)
low.defvjp(low_keep, low_pass)
low_back.defvjp(back_keep, back_low)

def product(left_side, right_side):
    return jnp.matmul(left_side, right_side, precision=lax.Precision.HIGHEST)

def layer_norm(value_in, norm_gain, norm_shift):
    center = value_in - lax.optimization_barrier(jnp.mean(value_in, axis=-1, keepdims=True))
    spread = lax.optimization_barrier(jnp.mean(center * center, axis=-1, keepdims=True))
    return center * lax.rsqrt(spread + 1e-05) * norm_gain + norm_shift

def split_block(matrix, head_count):
    group_count, span, model_width = matrix.shape
    return matrix.reshape(group_count, span, head_count, model_width // head_count).transpose(0, 2, 1, 3)

def merge_block(stacked):
    group_count, head_count, span, head_size = stacked.shape
    return stacked.transpose(0, 2, 1, 3).reshape(group_count, span, head_count * head_size)

def attend(query_block, key_block, value_block, extra_bias, allowed):
    raw_scores = jnp.einsum('ghqd,ghkd->ghqk', query_block, key_block, precision=lax.Precision.HIGHEST) + extra_bias
    scores = low_back(jnp.where(allowed, raw_scores, -1e+30))
    weights = low(jax.nn.softmax(scores, axis=-1))
    return low_back(jnp.einsum('ghqk,ghkd->ghqd', weights, value_block, precision=lax.Precision.HIGHEST))

def block(params, bias_heads, stream_zero, memory_rows, seq_lengths, mem_lengths):
    self_gain, self_shift, query_weight, query_bias, key_weight, value_weight, value_bias, position_table, head_scale, output_weight, output_bias, cross_gain, cross_shift, cross_query, cross_query_bias, cross_key, cross_value, cross_value_bias, post_gain, post_shift, cross_output, cross_output_bias, feed_gain, feed_shift, inner_weight, inner_bias, inner_gain, inner_shift, outer_weight, outer_bias = params
    places = jnp.arange(LEN)
    causal = places[:, None] >= places[None, :]
    self_allowed = causal[None, None] & (places[None, None, None, :] < seq_lengths[:, None, None, None])
    cross_allowed = jnp.arange(MLEN)[None, None, None, :] < mem_lengths[:, None, None, None]
    normed_one = low(layer_norm(stream_zero, self_gain, self_shift))
    query_one = low_back(low((product(normed_one, query_weight) + query_bias) * 0.125))
    key_one = low_back(low(product(normed_one, key_weight)))
    value_one = low_back(low(product(normed_one, value_weight) + value_bias))
    attended = attend(split_block(query_one, H), split_block(key_one, H), split_block(value_one, H), bias_heads[None], self_allowed)
    mixed_one = low(merge_block(attended * head_scale[None, :, None, None]))
    stream_one = stream_zero + low_back(product(mixed_one, output_weight)) + output_bias
    normed_two = low(layer_norm(stream_one, cross_gain, cross_shift))
    query_two = low_back(low((product(normed_two, cross_query) + cross_query_bias) * 0.125))
    key_two = low_back(low(product(memory_rows, cross_key)))
    value_two = low_back(low(product(memory_rows, cross_value) + cross_value_bias))
    attended_two = merge_block(attend(split_block(query_two, H), split_block(key_two, H), split_block(value_two, H), 0.0, cross_allowed))
    post_two = low(layer_norm(attended_two, post_gain, post_shift))
    stream_two = stream_one + low_back(product(post_two, cross_output)) + cross_output_bias
    normed_three = low(layer_norm(stream_two, feed_gain, feed_shift))
    inner_pre = low_back(product(normed_three, inner_weight)) + inner_bias
    activated = low(layer_norm(jax.nn.gelu(inner_pre, approximate=False), inner_gain, inner_shift))
    stream_three = stream_two + low_back(product(activated, outer_weight)) + outer_bias
    return low(stream_three)

def reference(tokens, cotangent, target_lengths, task_mask, memory_lengths, position_buckets, memory, self_gain, self_shift, query_weight, query_bias, key_weight, value_weight, value_bias, position_table, head_scale, output_weight, output_bias, cross_gain, cross_shift, cross_query, cross_query_bias, cross_key, cross_value, cross_value_bias, post_gain, post_shift, cross_output, cross_output_bias, feed_gain, feed_shift, inner_weight, inner_bias, inner_gain, inner_shift, outer_weight, outer_bias):
    params = tuple((entry.astype(jnp.float32) for entry in (self_gain, self_shift, query_weight, query_bias, key_weight, value_weight, value_bias, position_table, head_scale, output_weight, output_bias, cross_gain, cross_shift, cross_query, cross_query_bias, cross_key, cross_value, cross_value_bias, post_gain, post_shift, cross_output, cross_output_bias, feed_gain, feed_shift, inner_weight, inner_bias, inner_gain, inner_shift, outer_weight, outer_bias)))
    group_total = SEQS // SEQ_DEV

    def forward_all(param_set, stream_in, memory_in):
        bias_heads = jnp.transpose(param_set[7][position_buckets], (2, 0, 1))
        pieces = (stream_in.reshape(group_total, SEQ_DEV, LEN, D), memory_in.reshape(group_total, SEQ_DEV, MLEN, D), target_lengths.reshape(group_total, SEQ_DEV), memory_lengths.reshape(group_total, SEQ_DEV))

        def step(carry, piece):
            return (carry, block(param_set, bias_heads, piece[0], piece[1], piece[2], piece[3]))
        carry_end, outputs = lax.scan(jax.checkpoint(step), jnp.float32(0.0), pieces)
        return outputs.reshape(SEQS, LEN, D)
    stream_in = tokens.astype(jnp.float32)
    memory_in = memory.astype(jnp.float32)
    outputs, pullback = jax.vjp(forward_all, params, stream_in, memory_in)
    keep = task_mask.astype(jnp.float32) * (jnp.arange(LEN)[None, :] < target_lengths[:, None]).astype(jnp.float32)
    grad_params, grad_tokens, grad_memory = pullback(cotangent.astype(jnp.float32) * keep[:, :, None])
    return (outputs.astype(jnp.bfloat16), grad_tokens.astype(jnp.bfloat16), grad_memory.astype(jnp.bfloat16), grad_params[0], grad_params[1], grad_params[2], grad_params[3], grad_params[4], grad_params[5], grad_params[6], grad_params[7], grad_params[8], grad_params[9], grad_params[10], grad_params[11], grad_params[12], grad_params[13], grad_params[14], grad_params[15], grad_params[16], grad_params[17], grad_params[18], grad_params[19], grad_params[20], grad_params[21], grad_params[22], grad_params[23], grad_params[24], grad_params[25], grad_params[26], grad_params[27], grad_params[28], grad_params[29])
```

```python
import functools

import jax
import jax.numpy as jnp
from jax import lax
from jax.experimental import pallas as pl
from jax.experimental.pallas import tpu as pltpu
from jax.sharding import PartitionSpec as P

NEG = -1e30
F32 = jnp.float32
BF16 = jnp.bfloat16
VMEM_LIMIT = 67043328

(
    SELF_GAIN,
    SELF_SHIFT,
    QUERY_BIAS,
    VALUE_BIAS,
    HEAD_SCALE,
    OUTPUT_BIAS,
    CROSS_GAIN,
    CROSS_SHIFT,
    CROSS_QUERY_BIAS,
    CROSS_VALUE_BIAS,
    POST_GAIN,
    POST_SHIFT,
    CROSS_OUTPUT_BIAS,
    FEED_GAIN,
    FEED_SHIFT,
    OUTER_BIAS,
) = range(16)


def mm(a, b):
    return jnp.dot(a, b, preferred_element_type=F32)


def mm_nt(a, b):
    return lax.dot_general(a, b, (((1,), (1,)), ((), ())), preferred_element_type=F32)


def mm_tn(a, b):
    return lax.dot_general(a, b, (((0,), (0,)), ((), ())), preferred_element_type=F32)


def normalize(x):
    center = x - jnp.mean(x, axis=-1, keepdims=True)
    spread = jnp.mean(center * center, axis=-1, keepdims=True)
    scale = lax.rsqrt(spread + 1e-05)
    return center * scale, scale


def norm_back(dy, hat, scale, gain):
    w = dy * gain
    first = jnp.mean(w, axis=-1, keepdims=True)
    second = jnp.mean(w * hat, axis=-1, keepdims=True)
    return (w - first - hat * second) * scale


def colsum(x):
    return jnp.sum(x, axis=0, keepdims=True)


def half_masks(rows):
    lane = lax.broadcasted_iota(jnp.int32, (rows, 128), 1)
    return (lane < 64, lane >= 64)


def pick(mask, x):
    return jnp.where(mask, x.astype(F32), 0.0).astype(BF16)


def pair_lanes(p):
    return pl.ds(pl.multiple_of(p * 128, 128), 128)


def head_rows(p, half):
    return pl.ds(pl.multiple_of(p * 128 + half * 64, 64), 64)


def bias_kernel(buckets_ref, table_ref, out_ref):
    length = buckets_ref.shape[0]
    chunks = table_ref.shape[2] // 128
    key_place = lax.broadcasted_iota(jnp.int32, (length, 128), 0)
    for tile in range(length // 128):
        lanes = pl.ds(tile * 128, 128)
        ids = buckets_ref[:, lanes]
        low, high = ids & 127, ids >> 7
        total = jnp.zeros((length, 128), F32)
        for c in range(chunks):
            row = jnp.broadcast_to(table_ref[0, :, pl.ds(c * 128, 128)], (length, 128))
            got = jnp.take_along_axis(row, low, axis=1, mode="promise_in_bounds")
            total = jnp.where(high == c, got, total)
        query_place = lax.broadcasted_iota(jnp.int32, (length, 128), 1) + tile * 128
        out_ref[0, :, lanes] = jnp.where(key_place <= query_place, total, NEG)


def position_bias(buckets_t, table_t):
    heads = table_t.shape[0]
    length = buckets_t.shape[0]
    return pl.pallas_call(
        bias_kernel,
        out_shape=jax.ShapeDtypeStruct((heads, length, length), F32),
        grid=(heads,),
        in_specs=[
            pl.BlockSpec(buckets_t.shape, lambda h: (0, 0)),
            pl.BlockSpec((1, 1, table_t.shape[2]), lambda h: (h, 0, 0)),
        ],
        out_specs=pl.BlockSpec((1, length, length), lambda h: (h, 0, 0)),
        name="position_bias",
    )(buckets_t, table_t)


def self_forward(s, tlen_ref, tok_ref, bias_ref, vec_ref, wq, wk, wv, wo, q_ref, k_ref, v_ref, lse_ref, ot_ref, x1_ref, vt_ref):
    length = tok_ref.shape[1]
    x0 = tok_ref[0].astype(F32)
    hat, _ = normalize(x0)
    h1 = (hat * vec_ref[SELF_GAIN : SELF_GAIN + 1] + vec_ref[SELF_SHIFT : SELF_SHIFT + 1]).astype(BF16)
    q_ref[0] = ((mm(h1, wq[...]) + vec_ref[QUERY_BIAS : QUERY_BIAS + 1]) * 0.125).astype(BF16)
    k_ref[0] = mm(h1, wk[...]).astype(BF16)
    value = (mm(h1, wv[...]) + vec_ref[VALUE_BIAS : VALUE_BIAS + 1]).astype(BF16)
    v_ref[0] = value
    vt_ref[:, pl.ds(0, length)] = value.T
    key_place = lax.broadcasted_iota(jnp.int32, (length, length), 0)
    outside = jnp.where(key_place < tlen_ref[s], 0.0, NEG)
    masks = half_masks(length)

    @pl.loop(0, q_ref.shape[2] // 128)
    def _(p):
        lanes = pair_lanes(p)
        kp, qp = k_ref[0, :, lanes], q_ref[0, :, lanes]
        for half in range(2):
            st = mm_nt(kp, pick(masks[half], qp)) + bias_ref[2 * p + half] + outside
            top = jnp.max(st, axis=0, keepdims=True)
            e = jnp.exp(st - top)
            total = colsum(e)
            ot = mm(vt_ref[head_rows(p, half), pl.ds(0, length)], e.astype(BF16))
            ot_ref[0, head_rows(p, half), :] = ot * (1.0 / total)
            lse_ref[0, 2 * p + half] = top + jnp.log(total)

    out = ot_ref[0].T
    c1 = (out * vec_ref[HEAD_SCALE : HEAD_SCALE + 1]).astype(BF16)
    x1_ref[...] = x0 + mm(c1, wo[...]) + vec_ref[OUTPUT_BIAS : OUTPUT_BIAS + 1]


def cross_forward(s, mlen_ref, mem_ref, vec_ref, x1, wcq, wck, wcv, q_ref, k_ref, v_ref, lse_ref, ot_ref, vt_ref, st_ref):
    length, mem_total = x1.shape[0], mem_ref.shape[0]
    hat, _ = normalize(x1)
    h2 = (hat * vec_ref[CROSS_GAIN : CROSS_GAIN + 1] + vec_ref[CROSS_SHIFT : CROSS_SHIFT + 1]).astype(BF16)
    q_ref[0] = ((mm(h2, wcq[...]) + vec_ref[CROSS_QUERY_BIAS : CROSS_QUERY_BIAS + 1]) * 0.125).astype(BF16)
    step = 256

    @pl.loop(0, mem_total // step)
    def _(c):
        rows = pl.ds(pl.multiple_of(c * step, step), step)
        part = mem_ref[rows, :]
        k_ref[0, rows, :] = mm(part, wck[...]).astype(BF16)
        v_ref[0, rows, :] = (mm(part, wcv[...]) + vec_ref[CROSS_VALUE_BIAS : CROSS_VALUE_BIAS + 1]).astype(BF16)

    for c in range(mem_total // step):
        vt_ref[:, pl.ds(c * step, step)] = v_ref[0, pl.ds(c * step, step), :].T
    masks = half_masks(length)
    place = lax.broadcasted_iota(jnp.int32, (step, length), 0)

    @pl.loop(0, q_ref.shape[2] // 128)
    def _(p):
        lanes = pair_lanes(p)
        qp = q_ref[0, :, lanes]
        for half in range(2):
            qm = pick(masks[half], qp)
            top = jnp.full((1, length), -jnp.inf, F32)
            for c in range(mem_total // step):
                rows = pl.ds(c * step, step)
                st = mm_nt(k_ref[0, rows, lanes], qm)
                st = st + jnp.where(place < mlen_ref[s] - c * step, 0.0, NEG)
                st_ref[half, rows, :] = st
                top = jnp.maximum(top, jnp.max(st, axis=0, keepdims=True))
            total = jnp.zeros((1, length), F32)
            ot = jnp.zeros((64, length), F32)
            for c in range(mem_total // step):
                e = jnp.exp(st_ref[half, pl.ds(c * step, step), :] - top)
                total = total + colsum(e)
                ot = ot + mm(vt_ref[head_rows(p, half), pl.ds(c * step, step)], e.astype(BF16))
            ot_ref[head_rows(p, half), :] = ot * (1.0 / total)
            lse_ref[0, 2 * p + half] = top + jnp.log(total)


def feed_both(x2, g3, vec_ref, wide_ref, w1, w2, out_ref, dw1_ref, dw2_ref, sums_ref, wide_sums_ref, u_ref, d_ref, df_ref, f_ref, eu_ref, r_ref):
    length, hidden = u_ref.shape
    hat3, scale3 = normalize(x2)
    gain3 = vec_ref[FEED_GAIN : FEED_GAIN + 1]
    h3 = (hat3 * gain3 + vec_ref[FEED_SHIFT : FEED_SHIFT + 1]).astype(BF16)
    u_ref[...] = mm(h3, w1[...])
    step = 16

    @pl.loop(0, length // step)
    def _(b):
        rows = pl.ds(pl.multiple_of(b * step, step), step)
        u = u_ref[rows, :] + wide_ref[0:1]
        below = 0.5 * (1.0 + lax.erf(u * 0.7071067811865476))
        d_ref[rows, :] = below + u * (jnp.exp(-0.5 * u * u) * 0.3989422804014327)
        hat, scale = normalize(u * below)
        u_ref[rows, :] = hat
        f_ref[rows, :] = (hat * wide_ref[1:2] + wide_ref[2:3]).astype(BF16)
        r_ref[rows, :] = jnp.broadcast_to(scale, (step, 128))

    x3 = x2 + mm(f_ref[...], w2[...]) + vec_ref[OUTER_BIAS : OUTER_BIAS + 1]
    out_ref[0] = x3.astype(BF16)
    sums_ref[0:1] += colsum(g3)
    e3 = g3.astype(BF16)
    dw2_ref[...] += mm_tn(f_ref[...], e3)
    df_ref[...] = mm_nt(e3, w2[...])

    @pl.loop(0, length // step)
    def _(b):
        rows = pl.ds(pl.multiple_of(b * step, step), step)
        dy, hat = df_ref[rows, :], u_ref[rows, :]
        part = dy * hat
        wide_sums_ref[0:8] += part[0:8] + part[8:16]
        wide_sums_ref[8:16] += dy[0:8] + dy[8:16]
        da = norm_back(dy, hat, r_ref[rows, 0:1], wide_ref[1:2])
        du = da * d_ref[rows, :]
        wide_sums_ref[16:24] += du[0:8] + du[8:16]
        eu_ref[rows, :] = du.astype(BF16)

    dw1_ref[...] += mm_tn(h3, eu_ref[...])
    dh3 = mm_nt(eu_ref[...], w1[...])
    sums_ref[1:2] += colsum(dh3 * hat3)
    sums_ref[2:3] += colsum(dh3)
    return g3 + norm_back(dh3, hat3, scale3, gain3)


def fwd_kernel(
    tlen_ref, mlen_ref,
    tok_ref, cot_ref, keep_ref, mem_ref, bias_ref, vec_ref, wide_ref,
    wq, wk, wv, wo, wcq, wck, wcv, wco, w1, w2,
    q1_ref, k1_ref, v1_ref, lse1_ref, ot1_ref,
    x1_ref, q2_ref, k2_ref, v2_ref, lse2_ref, delta2_ref, do2_ref, g2_ref, out_ref,
    dwco_ref, dw1_ref, dw2_ref, sums_ref, wide_out_ref,
    x1_scr, vt_scr, st_scr, ot_scr, u_scr, d_scr, df_scr, f_scr, eu_scr, r_scr, wide_scr,
):
    seqs = x1_scr.shape[0]
    t = pl.program_id(0)

    @pl.when(t == 0)
    def _():
        for ref in (dwco_ref, dw1_ref, dw2_ref, sums_ref, wide_scr):
            ref[...] = jnp.zeros_like(ref)

    @pl.when(t < seqs)
    def _():
        self_forward(
            t, tlen_ref, tok_ref, bias_ref, vec_ref, wq, wk, wv, wo,
            q1_ref, k1_ref, v1_ref, lse1_ref, ot1_ref, x1_scr.at[t], vt_scr,
        )

    @pl.when(t >= seqs)
    def _():
        s = t - seqs
        x1 = x1_scr[s]
        x1_ref[0] = x1
        cross_forward(
            s, mlen_ref, mem_ref.at[0], vec_ref, x1, wcq, wck, wcv,
            q2_ref, k2_ref, v2_ref, lse2_ref, ot_scr, vt_scr, st_scr,
        )
        hat, scale = normalize(ot_scr[...].T)
        gain = vec_ref[POST_GAIN : POST_GAIN + 1]
        c2 = (hat * gain + vec_ref[POST_SHIFT : POST_SHIFT + 1]).astype(BF16)
        x2 = x1 + mm(c2, wco[...]) + vec_ref[CROSS_OUTPUT_BIAS : CROSS_OUTPUT_BIAS + 1]
        g3 = cot_ref[0].astype(F32) * keep_ref[0]
        g2 = feed_both(
            x2, g3, vec_ref, wide_ref, w1, w2, out_ref, dw1_ref, dw2_ref, sums_ref, wide_scr,
            u_scr, d_scr, df_scr, f_scr, eu_scr, r_scr,
        )
        g2_ref[0] = g2
        sums_ref[3:4] += colsum(g2)
        e2 = g2.astype(BF16)
        dwco_ref[...] += mm_tn(c2, e2)
        dc2 = mm_nt(e2, wco[...])
        sums_ref[4:5] += colsum(dc2 * hat)
        sums_ref[5:6] += colsum(dc2)
        do2 = norm_back(dc2, hat, scale, gain)
        do2_ref[0] = do2.astype(BF16)
        prod = do2.astype(BF16).astype(F32).T * ot_scr[...]
        for h in range(lse2_ref.shape[1]):
            delta2_ref[0, h] = colsum(prod[h * 64 : (h + 1) * 64])

    @pl.when(t == 2 * seqs - 1)
    def _():
        for k in range(3):
            wide_out_ref[k : k + 1] = colsum(wide_scr[8 * k : 8 * k + 8])


def forward(tlen, mlen, tokens, cotangent, keep, mem, bias, vec, wide, weights):
    seqs, length, width = tokens.shape
    mem_total = mem.shape[1]
    heads = bias.shape[0]
    hidden = wide.shape[1]
    early = lambda t, *_: (jnp.minimum(t, seqs - 1), 0, 0)
    late = lambda t, *_: (jnp.maximum(t - seqs, 0), 0, 0)
    whole2 = lambda t, *_: (0, 0)
    const = lambda a: pl.BlockSpec(a.shape, lambda t, *_: (0,) * a.ndim, pipeline_mode=pl.Buffered(1))
    seq = lambda rows, cols, idx: pl.BlockSpec((1, rows, cols), idx)
    row = lambda idx: pl.BlockSpec((1, heads, 1, length), lambda t, *_: idx(t) + (0,))
    sds = jax.ShapeDtypeStruct
    outs = [
        (sds((seqs, length, width), BF16), seq(length, width, early)),
        (sds((seqs, length, width), BF16), seq(length, width, early)),
        (sds((seqs, length, width), BF16), seq(length, width, early)),
        (sds((seqs, heads, 1, length), F32), row(early)),
        (sds((seqs, width, length), F32), seq(width, length, early)),
        (sds((seqs, length, width), F32), seq(length, width, late)),
        (sds((seqs, length, width), BF16), seq(length, width, late)),
        (sds((seqs, mem_total, width), BF16), seq(mem_total, width, late)),
        (sds((seqs, mem_total, width), BF16), seq(mem_total, width, late)),
        (sds((seqs, heads, 1, length), F32), row(late)),
        (sds((seqs, heads, 1, length), F32), row(late)),
        (sds((seqs, length, width), BF16), seq(length, width, late)),
        (sds((seqs, length, width), F32), seq(length, width, late)),
        (sds((seqs, length, width), BF16), seq(length, width, late)),
        (sds((width, width), F32), pl.BlockSpec((width, width), whole2)),
        (sds((width, hidden), F32), pl.BlockSpec((width, hidden), whole2)),
        (sds((hidden, width), F32), pl.BlockSpec((hidden, width), whole2)),
        (sds((8, width), F32), pl.BlockSpec((8, width), whole2)),
        (sds((3, hidden), F32), pl.BlockSpec((3, hidden), whole2)),
    ]
    return pl.pallas_call(
        fwd_kernel,
        out_shape=[o[0] for o in outs],
        grid_spec=pltpu.PrefetchScalarGridSpec(
            num_scalar_prefetch=2,
            grid=(2 * seqs,),
            in_specs=[
                seq(length, width, early),
                seq(length, width, late),
                seq(length, 1, late),
                seq(mem_total, width, late),
                const(bias), const(vec), const(wide),
            ] + [const(w) for w in weights],
            out_specs=[o[1] for o in outs],
            scratch_shapes=[
                pltpu.VMEM((seqs, length, width), F32),
                pltpu.VMEM((width, mem_total), BF16),
                pltpu.VMEM((2, mem_total, length), F32),
                pltpu.VMEM((width, length), F32),
                pltpu.VMEM((length, hidden), F32),
                pltpu.VMEM((length, hidden), F32),
                pltpu.VMEM((length, hidden), F32),
                pltpu.VMEM((length, hidden), BF16),
                pltpu.VMEM((length, hidden), BF16),
                pltpu.VMEM((length, 128), F32),
                pltpu.VMEM((24, hidden), F32),
            ],
        ),
        compiler_params=pltpu.CompilerParams(vmem_limit_bytes=VMEM_LIMIT),
        name="forward",
    )(tlen, mlen, tokens, cotangent, keep, mem, bias, vec, wide, *weights)


def cross_backward(mlen, mem_ref, q_ref, k_ref, v_ref, lse_ref, delta_ref, do_ref, wck, wcv, dk_ref, dv_ref, dqt_ref, kt_ref, dmem_ref, dwck_ref, dwcv_ref, sums_ref):
    length, mem_total = q_ref.shape[0], mem_ref.shape[0]
    step = 256
    for c in range(mem_total // step):
        kt_ref[:, pl.ds(c * step, step)] = k_ref[pl.ds(c * step, step), :].T
    masks = half_masks(length)
    place = lax.broadcasted_iota(jnp.int32, (step, length), 0)

    @pl.loop(0, q_ref.shape[1] // 128)
    def _(p):
        lanes = pair_lanes(p)
        qp, dop = q_ref[:, lanes], do_ref[:, lanes]
        qms = [pick(masks[half], qp) for half in range(2)]
        doms = [pick(masks[half], dop) for half in range(2)]
        lse = [lse_ref[2 * p + half] for half in range(2)]
        delta = [delta_ref[2 * p + half] for half in range(2)]
        dqt = [jnp.zeros((64, length), F32) for half in range(2)]
        for c in range(mem_total // step):
            rows = pl.ds(c * step, step)
            kp, vp = k_ref[rows, lanes], v_ref[rows, lanes]
            outside = jnp.where(place < mlen - c * step, 0.0, NEG)
            dv = jnp.zeros((step, 128), F32)
            dk = jnp.zeros((step, 128), F32)
            for half in range(2):
                st = mm_nt(kp, qms[half]) + outside
                pt = jnp.exp(st - lse[half])
                dpt = mm_nt(vp, doms[half])
                dst = (pt * (dpt - delta[half])).astype(BF16)
                dqt[half] = dqt[half] + mm(kt_ref[head_rows(p, half), rows], dst)
                dv = dv + mm(pt.astype(BF16), doms[half])
                dk = dk + mm(dst, qms[half])
            dv_ref[rows, lanes] = dv.astype(BF16)
            dk_ref[rows, lanes] = dk.astype(BF16)
        for half in range(2):
            dqt_ref[head_rows(p, half), :] = dqt[half]

    @pl.loop(0, mem_total // step)
    def _(c):
        rows = pl.ds(pl.multiple_of(c * step, step), step)
        dk, dv = dk_ref[rows, :], dv_ref[rows, :]
        dmem_ref[rows, :] = (mm_nt(dk, wck[...]) + mm_nt(dv, wcv[...])).astype(BF16)
        sums_ref[8:9] += colsum(dv.astype(F32))

    dwck_ref[...] += mm_tn(mem_ref[...], dk_ref[...])
    dwcv_ref[...] += mm_tn(mem_ref[...], dv_ref[...])


def self_backward(tlen, bias_ref, q_ref, k_ref, v_ref, lse_ref, delta_ref, do_ref, dqt_ref, dk_ref, dv_ref, kt_ref, dbias_ref):
    length = q_ref.shape[0]
    kt_ref[:, pl.ds(0, length)] = k_ref[...].T
    key_place = lax.broadcasted_iota(jnp.int32, (length, length), 0)
    outside = jnp.where(key_place < tlen, 0.0, NEG)
    masks = half_masks(length)

    @pl.loop(0, q_ref.shape[1] // 128)
    def _(p):
        lanes = pair_lanes(p)
        qp, dop = q_ref[:, lanes], do_ref[:, lanes]
        kp, vp = k_ref[:, lanes], v_ref[:, lanes]
        dv = jnp.zeros((length, 128), F32)
        dk = jnp.zeros((length, 128), F32)
        for half in range(2):
            h = 2 * p + half
            qm, dom = pick(masks[half], qp), pick(masks[half], dop)
            st = mm_nt(kp, qm) + bias_ref[h] + outside
            pt = jnp.exp(st - lse_ref[h])
            dpt = mm_nt(vp, dom)
            dst = (pt * (dpt - delta_ref[h])).astype(BF16)
            rows = pl.ds(pl.multiple_of(h * length, length), length)
            wide_ds = dst.astype(F32)
            for tile in range(length // 128):
                dbias_ref[tile, rows, :] += wide_ds[:, tile * 128 : (tile + 1) * 128]
            dqt_ref[head_rows(p, half), :] = mm(kt_ref[head_rows(p, half), pl.ds(0, length)], dst)
            dv = dv + mm(pt.astype(BF16), dom)
            dk = dk + mm(dst, qm)
        dv_ref[:, lanes] = dv.astype(BF16)
        dk_ref[:, lanes] = dk.astype(BF16)


def bucket_totals(buckets_ref, dbias_ref, out_ref):
    length = buckets_ref.shape[0]
    heads = dbias_ref.shape[1] // length
    lo_places = lax.broadcasted_iota(jnp.int32, (32, length), 0)

    def body(b, acc):
        start = pl.multiple_of(b * 8, 8)
        rows = buckets_ref[pl.ds(start, 8), :]
        for k in range(8):
            ids = rows[k : k + 1]
            d = jnp.concatenate(
                [dbias_ref[tile, pl.ds(start + k, heads, stride=length), :] for tile in range(length // 128)], axis=1
            )
            rough = d.astype(BF16).astype(F32)
            fine = d - rough
            high = jnp.broadcast_to(ids >> 5, (heads, length))
            left = jnp.concatenate(
                [jnp.where(high == g, part, 0.0) for part in (rough, fine) for g in range(16)], axis=0
            ).astype(BF16)
            right = jnp.where(lo_places == (ids & 31), 1.0, 0.0).astype(BF16)
            acc = acc + mm_nt(left, right)
        return acc

    acc = lax.fori_loop(0, length // 8, body, jnp.zeros((2 * 16 * heads, 32), F32))
    acc = acc[: 16 * heads] + acc[16 * heads :]
    for g in range(16):
        out_ref[:, g * 32 : (g + 1) * 32] = acc[g * heads : (g + 1) * heads]


def bwd_kernel(
    tlen_ref, mlen_ref,
    tok_ref, mem_ref, bias_ref, buckets_ref, vec_ref, hs_ref,
    q1_ref, k1_ref, v1_ref, lse1_ref, ot1_ref,
    x1_ref, q2_ref, k2_ref, v2_ref, lse2_ref, delta2_ref, do2_ref, g2_ref,
    wq, wk, wv, wo, wcq, wck, wcv,
    dmem_ref, dtok_ref, dw_ref, sums_ref, table_ref,
    dk_scr, dv_scr, dqt_scr, kt_scr, dbias_scr, delta_scr, do_scr, hs_scr,
):
    t = pl.program_id(0)
    seqs = pl.num_programs(0)
    heads = lse1_ref.shape[1]
    length = tok_ref.shape[1]

    @pl.when(t == 0)
    def _():
        for ref in (dw_ref, sums_ref, dbias_scr, hs_scr):
            ref[...] = jnp.zeros_like(ref)

    cross_backward(
        mlen_ref[t], mem_ref.at[0], q2_ref.at[0], k2_ref.at[0], v2_ref.at[0], lse2_ref.at[0], delta2_ref.at[0],
        do2_ref.at[0], wck, wcv, dk_scr, dv_scr, dqt_scr, kt_scr, dmem_ref.at[0], dw_ref.at[5], dw_ref.at[6], sums_ref,
    )
    dq2 = (dqt_scr[...].T.astype(BF16).astype(F32) * 0.125).astype(BF16)
    hat2, scale2 = normalize(x1_ref[0])
    gain2 = vec_ref[CROSS_GAIN : CROSS_GAIN + 1]
    h2 = (hat2 * gain2 + vec_ref[CROSS_SHIFT : CROSS_SHIFT + 1]).astype(BF16)
    dw_ref[4] += mm_tn(h2, dq2)
    sums_ref[7:8] += colsum(dq2.astype(F32))
    dh2 = mm_nt(dq2, wcq[...])
    sums_ref[5:6] += colsum(dh2 * hat2)
    sums_ref[6:7] += colsum(dh2)
    g1 = g2_ref[0] + norm_back(dh2, hat2, scale2, gain2)
    sums_ref[4:5] += colsum(g1)
    e1 = g1.astype(BF16)
    c1t = (ot1_ref[0] * hs_ref[...]).astype(BF16)
    dw_ref[3] += mm(c1t, e1)
    dc1 = mm_nt(e1, wo[...])
    do_scr[...] = (dc1 * vec_ref[HEAD_SCALE : HEAD_SCALE + 1]).astype(BF16)
    dc1t = dc1.T
    do1t = (dc1t * hs_ref[...]).astype(BF16).astype(F32)
    for h in range(heads):
        rows = slice(h * 64, (h + 1) * 64)
        o = ot1_ref[0, rows, :]
        hs_scr[h : h + 1, :] += colsum(o * dc1t[rows])
        delta_scr[h] = colsum(o * do1t[rows])
    self_backward(
        tlen_ref[t], bias_ref, q1_ref.at[0], k1_ref.at[0], v1_ref.at[0], lse1_ref.at[0], delta_scr, do_scr,
        dqt_scr, dk_scr.at[pl.ds(0, length)], dv_scr.at[pl.ds(0, length)], kt_scr, dbias_scr,
    )
    dq1 = (dqt_scr[...].T.astype(BF16).astype(F32) * 0.125).astype(BF16)
    dk1 = dk_scr[pl.ds(0, length), :]
    dv1 = dv_scr[pl.ds(0, length), :]
    hat1, scale1 = normalize(tok_ref[0].astype(F32))
    gain1 = vec_ref[SELF_GAIN : SELF_GAIN + 1]
    h1 = (hat1 * gain1 + vec_ref[SELF_SHIFT : SELF_SHIFT + 1]).astype(BF16)
    dw_ref[0] += mm_tn(h1, dq1)
    dw_ref[1] += mm_tn(h1, dk1)
    dw_ref[2] += mm_tn(h1, dv1)
    sums_ref[2:3] += colsum(dq1.astype(F32))
    sums_ref[3:4] += colsum(dv1.astype(F32))
    dh1 = mm_nt(dq1, wq[...]) + mm_nt(dk1, wk[...]) + mm_nt(dv1, wv[...])
    sums_ref[0:1] += colsum(dh1 * hat1)
    sums_ref[1:2] += colsum(dh1)
    dtok_ref[0] = (g1 + norm_back(dh1, hat1, scale1, gain1)).astype(BF16)

    @pl.when(t == seqs - 1)
    def _():
        sums_ref[16 : 16 + heads] = jnp.broadcast_to(
            jnp.sum(hs_scr[...], axis=1, keepdims=True), (heads, sums_ref.shape[1])
        )
        bucket_totals(buckets_ref, dbias_scr, table_ref)


def backward(tlen, mlen, tokens, mem, bias, buckets_t, vec, hs_col, saved, weights):
    seqs, length, width = tokens.shape
    mem_total = mem.shape[1]
    heads = bias.shape[0]
    each = lambda t, *_: (t, 0, 0)
    const = lambda a: pl.BlockSpec(a.shape, lambda t, *_: (0,) * a.ndim, pipeline_mode=pl.Buffered(1))
    seq = lambda a: pl.BlockSpec((1,) + a.shape[1:], lambda t, *_: (t,) + (0,) * (a.ndim - 1))
    sds = jax.ShapeDtypeStruct
    whole = lambda shape: pl.BlockSpec(shape, lambda t, *_: (0,) * len(shape))
    return pl.pallas_call(
        bwd_kernel,
        out_shape=[
            sds((seqs, mem_total, width), BF16),
            sds((seqs, length, width), BF16),
            sds((7, width, width), F32),
            sds((24, width), F32),
            sds((heads, 512), F32),
        ],
        grid_spec=pltpu.PrefetchScalarGridSpec(
            num_scalar_prefetch=2,
            grid=(seqs,),
            in_specs=[seq(tokens), seq(mem), const(bias), const(buckets_t), const(vec), const(hs_col)]
            + [seq(a) for a in saved]
            + [const(w) for w in weights],
            out_specs=[
                pl.BlockSpec((1, mem_total, width), each),
                pl.BlockSpec((1, length, width), each),
                whole((7, width, width)),
                whole((24, width)),
                whole((heads, 512)),
            ],
            scratch_shapes=[
                pltpu.VMEM((mem_total, width), BF16),
                pltpu.VMEM((mem_total, width), BF16),
                pltpu.VMEM((width, length), F32),
                pltpu.VMEM((width, mem_total), BF16),
                pltpu.VMEM((length // 128, heads * length, 128), F32),
                pltpu.VMEM((heads, 1, length), F32),
                pltpu.VMEM((length, width), BF16),
                pltpu.VMEM((heads, length), F32),
            ],
        ),
        compiler_params=pltpu.CompilerParams(vmem_limit_bytes=VMEM_LIMIT),
        name="backward",
    )(tlen, mlen, tokens, mem, bias, buckets_t, vec, hs_col, *saved, *weights)


def local(
    tokens, cotangent, target_lengths, task_mask, memory_lengths, position_buckets, memory,
    self_gain, self_shift, query_weight, query_bias, key_weight, value_weight, value_bias, position_table, head_scale,
    output_weight, output_bias, cross_gain, cross_shift, cross_query, cross_query_bias, cross_key, cross_value,
    cross_value_bias, post_gain, post_shift, cross_output, cross_output_bias, feed_gain, feed_shift, inner_weight,
    inner_bias, inner_gain, inner_shift, outer_weight, outer_bias,
):
    seqs, length, width = tokens.shape
    heads = head_scale.shape[0]
    bucket_count = position_table.shape[0]
    buckets_t = position_buckets.T
    table_t = jnp.pad(position_table, ((0, 512 - bucket_count), (0, 0))).T[:, None, :]
    hs_lanes = jnp.repeat(head_scale, width // heads)
    vec = jnp.stack([
        self_gain, self_shift, query_bias, value_bias, hs_lanes, output_bias, cross_gain, cross_shift,
        cross_query_bias, cross_value_bias, post_gain, post_shift, cross_output_bias, feed_gain, feed_shift, outer_bias,
    ])
    wide = jnp.stack([inner_bias, inner_gain, inner_shift])
    keep = task_mask.astype(F32) * (jnp.arange(length)[None, :] < target_lengths[:, None]).astype(F32)
    bias = position_bias(buckets_t, table_t)
    mem = lax.all_to_all(memory, "dp", split_axis=0, concat_axis=2, tiled=True)[0]
    fwd = forward(
        target_lengths, memory_lengths, tokens, cotangent, keep[:, :, None], mem, bias, vec, wide,
        [query_weight, key_weight, value_weight, output_weight, cross_query, cross_key, cross_value, cross_output,
         inner_weight, outer_weight],
    )
    layer_output = fwd[13]
    dwco, dw1, dw2, sums_a, wide_sums = fwd[14:]
    dmem, dtok, dw, sums_b, table_sums = backward(
        target_lengths, memory_lengths, tokens, mem, bias, buckets_t, vec,
        jnp.broadcast_to(hs_lanes[:, None], (width, length)), fwd[:13],
        [query_weight, key_weight, value_weight, output_weight, cross_query, cross_key, cross_value],
    )
    memory_gradient = lax.all_to_all(dmem[None], "dp", split_axis=2, concat_axis=0, tiled=True)
    low = lambda a: a.astype(BF16)
    big = lax.psum((low(dw), low(dwco), low(dw1), low(dw2)), ("dp", "rep"))
    dw, dwco, dw1, dw2 = [a.astype(F32) for a in big]
    small = jnp.concatenate([sums_a, sums_b, table_sums, wide_sums.reshape(-1, width)], axis=0)
    small = lax.psum(small, ("dp", "rep"))
    a, b, tab, wid = small[:8], small[8:32], small[32:40], small[40:].reshape(3, -1)
    return (
        layer_output, dtok, memory_gradient,
        b[0], b[1], dw[0], b[2], dw[1], dw[2], b[3], tab[:, :bucket_count].T, b[16:24, 0],
        dw[3], b[4], b[5], b[6], dw[4], b[7], dw[5], dw[6], b[8],
        a[4], a[5], dwco, a[3], a[1], a[2], dw1, wid[2], wid[0], wid[1], dw2, a[0],
    )


def solution(mesh):
    per_seq3, per_seq2, per_seq1 = P(("dp", "rep"), None, None), P(("dp", "rep"), None), P(("dp", "rep"))
    spread = P(None, "rep", "dp", None)
    in_specs = (per_seq3, per_seq3, per_seq1, per_seq2, per_seq1, P(), spread) + (P(),) * 30
    out_specs = (per_seq3, per_seq3, spread) + (P(),) * 30
    return jax.shard_map(local, mesh=mesh, in_specs=in_specs, out_specs=out_specs, check_vma=False)
```

```python
import functools

import jax
import jax.numpy as jnp
from jax import lax
from jax.experimental import pallas as pl
from jax.experimental.pallas import tpu as pltpu
from jax.sharding import PartitionSpec as P

NEG = -1e30
F32 = jnp.float32
BF16 = jnp.bfloat16
VMEM_LIMIT = 67043328

(
    SELF_GAIN,
    SELF_SHIFT,
    QUERY_BIAS,
    VALUE_BIAS,
    HEAD_SCALE,
    OUTPUT_BIAS,
    CROSS_GAIN,
    CROSS_SHIFT,
    CROSS_QUERY_BIAS,
    CROSS_VALUE_BIAS,
    POST_GAIN,
    POST_SHIFT,
    CROSS_OUTPUT_BIAS,
    FEED_GAIN,
    FEED_SHIFT,
    OUTER_BIAS,
) = range(16)


def mm(a, b):
    return jnp.dot(a, b, preferred_element_type=F32)


def mm_nt(a, b):
    return lax.dot_general(a, b, (((1,), (1,)), ((), ())), preferred_element_type=F32)


def mm_tn(a, b):
    return lax.dot_general(a, b, (((0,), (0,)), ((), ())), preferred_element_type=F32)


def normalize(x):
    center = x - jnp.mean(x, axis=-1, keepdims=True)
    spread = jnp.mean(center * center, axis=-1, keepdims=True)
    scale = lax.rsqrt(spread + 1e-05)
    return center * scale, scale


def norm_back(dy, hat, scale, gain):
    w = dy * gain
    first = jnp.mean(w, axis=-1, keepdims=True)
    second = jnp.mean(w * hat, axis=-1, keepdims=True)
    return (w - first - hat * second) * scale


def colsum(x):
    return jnp.sum(x, axis=0, keepdims=True)


def half_masks(rows):
    lane = lax.broadcasted_iota(jnp.int32, (rows, 128), 1)
    return (lane < 64, lane >= 64)


def pick(mask, x):
    return jnp.where(mask, x.astype(F32), 0.0).astype(BF16)


def pair_lanes(p):
    return pl.ds(pl.multiple_of(p * 128, 128), 128)


def head_rows(p, half):
    return pl.ds(pl.multiple_of(p * 128 + half * 64, 64), 64)


def fill_bias(buckets, table_rows, out_ref):
    length = buckets.shape[0]
    chunks = table_rows.shape[2] // 128
    ids_t = buckets.T
    low, high = ids_t & 127, ids_t >> 7
    key_place = lax.broadcasted_iota(jnp.int32, (length, 128), 0)
    lane = lax.broadcasted_iota(jnp.int32, (length, 128), 1)

    @pl.loop(0, out_ref.shape[0])
    def _(h):
        rows = [jnp.broadcast_to(table_rows[h, :, pl.ds(c * 128, 128)], (length, 128)) for c in range(chunks)]
        for tile in range(length // 128):
            cols = slice(tile * 128, (tile + 1) * 128)
            total = jnp.zeros((length, 128), F32)
            for c in range(chunks):
                got = jnp.take_along_axis(rows[c], low[:, cols], axis=1, mode="promise_in_bounds")
                total = jnp.where(high[:, cols] == c, got, total)
            out_ref[h, :, pl.ds(tile * 128, 128)] = jnp.where(key_place <= lane + tile * 128, total, NEG)


def axis_bits(sizes):
    return [(axis, bit) for axis in ("rep", "dp") for bit in range(sizes[axis].bit_length() - 1)]


def stage_orders(sizes):
    plain = axis_bits(sizes)
    reps = sizes["rep"].bit_length() - 1
    swapped = list(plain)
    if reps >= 2 and len(plain) > reps:
        swapped = plain[: reps - 1] + [plain[reps], plain[reps - 1]] + plain[reps + 1 :]
    return plain, swapped


class Reduction:
    def __init__(self, buf, land, start, rows, land_start, stages, tile, send, recv, free):
        self.buf, self.land, self.tile, self.send, self.recv, self.free = buf, land, tile, send, recv, free
        self.plan = []
        base, span, at = start, rows, land_start
        for axis, bit in stages:
            place = lax.axis_index(axis)
            mine = (place // 2**bit) % 2
            peer = {axis: place + (1 - 2 * mine) * 2**bit}
            halve = span % (2 * tile) == 0
            size = span // 2 if halve else span
            keep = base + mine * size if halve else base
            give = base + (1 - mine) * size if halve else base
            mark = len(self.plan)
            self.plan.append(("fold", peer, give, keep, size, at, mark if halve else None))
            at += size
            if halve:
                self.plan.append(("spread", peer, keep, base, size, None, mark))
            base, span = keep, size
        folds = [p for p in self.plan if p[0] == "fold"]
        spreads = [p for p in self.plan if p[0] == "spread"]
        self.plan = folds + spreads[::-1]
        self.land_rows = at - land_start

    def __len__(self):
        return len(self.plan)

    def rows(self, start, size):
        return pl.ds(start if isinstance(start, int) else pl.multiple_of(start, self.tile), size)

    def copy(self, k):
        kind, peer, give, keep, size, at, mark = self.plan[k]
        source = self.buf.at[self.rows(give, size)]
        target = self.land.at[self.rows(at, size)] if kind == "fold" else source
        return pltpu.make_async_remote_copy(
            src_ref=source, dst_ref=target, send_sem=self.send.at[k], recv_sem=self.recv.at[k],
            device_id=peer, device_id_type=pl.DeviceIdType.MESH,
        )

    def start(self, k):
        if k < len(self):
            if self.plan[k][0] == "spread":
                pl.semaphore_wait(self.free.at[self.plan[k][6]], 1)
            self.copy(k).start()

    def finish(self, k):
        if k >= len(self):
            return
        kind, peer, give, keep, size, at, mark = self.plan[k]
        self.copy(k).wait()
        if kind == "fold":
            if mark is not None:
                pl.semaphore_signal(
                    self.free.at[mark], inc=1, device_id=peer, device_id_type=pl.DeviceIdType.MESH
                )
            step = next(c for c in (128, 64, 48, 32, 16, 8) if size % c == 0)

            @pl.loop(0, size // step)
            def _(b):
                kept = pl.ds(pl.multiple_of(keep + b * step, self.tile), step)
                came = pl.ds(pl.multiple_of(at + b * step, self.tile), step)
                total = self.buf[kept, :].astype(F32) + self.land[came, :].astype(F32)
                self.buf[kept, :] = total.astype(self.buf.dtype)

    def advance(self, k):
        if 0 < k <= len(self):
            self.finish(k - 1)
        self.start(k)


def land_rows(rows, stages, tile):
    span, total = rows, 0
    for _ in stages:
        span = span // 2 if span % (2 * tile) == 0 else span
        total += span
    return total


def meet(peers):
    barrier = pltpu.get_barrier_semaphore()
    for peer in peers:
        pl.semaphore_signal(barrier, inc=1, device_id=peer, device_id_type=pl.DeviceIdType.MESH)
    pl.semaphore_wait(barrier, len(peers))


def scaled_heads(value_t, hs_ref):
    return jnp.concatenate([value_t[h * 64 : (h + 1) * 64] * hs_ref[h] for h in range(value_t.shape[0] // 64)], axis=0)


def self_forward(s, tlen_ref, hs_ref, tok_ref, bias_ref, vec_ref, wq, wk, wv, wo, q_ref, k_ref, v_ref, lse_ref, ot_ref, x1_ref, vt_ref):
    length = tok_ref.shape[1]
    x0 = tok_ref[0].astype(F32)
    hat, _ = normalize(x0)
    h1 = (hat * vec_ref[SELF_GAIN][...] + vec_ref[SELF_SHIFT][...]).astype(BF16)
    q_ref[0] = ((mm(h1, wq[...]) + vec_ref[QUERY_BIAS][...]) * 0.125).astype(BF16)
    k_ref[0] = mm(h1, wk[...]).astype(BF16)
    value = (mm(h1, wv[...]) + vec_ref[VALUE_BIAS][...]).astype(BF16)
    v_ref[0] = value
    vt_ref[:, pl.ds(0, length)] = value.T
    key_place = lax.broadcasted_iota(jnp.int32, (length, length), 0)
    outside = jnp.where(key_place < tlen_ref[s], 0.0, NEG)
    masks = half_masks(length)

    @pl.loop(0, q_ref.shape[2] // 128)
    def _(p):
        lanes = pair_lanes(p)
        kp, qp = k_ref[0, :, lanes], q_ref[0, :, lanes]
        for half in range(2):
            st = mm_nt(kp, pick(masks[half], qp)) + bias_ref[2 * p + half] + outside
            top = jnp.max(st, axis=0, keepdims=True)
            e = jnp.exp(st - top)
            total = colsum(e)
            ot = mm(vt_ref[head_rows(p, half), pl.ds(0, length)], e.astype(BF16))
            ot_ref[0, head_rows(p, half), :] = ot * (1.0 / total)
            lse_ref[0, 2 * p + half] = top + jnp.log(total)

    c1 = scaled_heads(ot_ref[0], hs_ref).T.astype(BF16)
    x1_ref[...] = x0 + mm(c1, wo[...]) + vec_ref[OUTPUT_BIAS][...]


def cross_forward(s, mlen_ref, mem_ref, vec_ref, x1, wcq, wck, wcv, q_ref, k_ref, v_ref, lse_ref, ot_ref, vt_ref, st_ref):
    length, mem_total = x1.shape[0], mem_ref.shape[0]
    hat, _ = normalize(x1)
    h2 = (hat * vec_ref[CROSS_GAIN][...] + vec_ref[CROSS_SHIFT][...]).astype(BF16)
    q_ref[0] = ((mm(h2, wcq[...]) + vec_ref[CROSS_QUERY_BIAS][...]) * 0.125).astype(BF16)
    step = 256

    @pl.loop(0, mem_total // step)
    def _(c):
        rows = pl.ds(pl.multiple_of(c * step, step), step)
        part = mem_ref[rows, :]
        k_ref[0, rows, :] = mm(part, wck[...]).astype(BF16)
        v_ref[0, rows, :] = (mm(part, wcv[...]) + vec_ref[CROSS_VALUE_BIAS][...]).astype(BF16)

    for c in range(mem_total // step):
        vt_ref[:, pl.ds(c * step, step)] = v_ref[0, pl.ds(c * step, step), :].T
    masks = half_masks(length)
    place = lax.broadcasted_iota(jnp.int32, (step, length), 0)

    @pl.loop(0, q_ref.shape[2] // 128)
    def _(p):
        lanes = pair_lanes(p)
        qp = q_ref[0, :, lanes]
        for half in range(2):
            qm = pick(masks[half], qp)
            top = jnp.full((1, length), -jnp.inf, F32)
            for c in range(mem_total // step):
                rows = pl.ds(c * step, step)
                st = mm_nt(k_ref[0, rows, lanes], qm)
                st = st + jnp.where(place < mlen_ref[s] - c * step, 0.0, NEG)
                st_ref[half, rows, :] = st
                top = jnp.maximum(top, jnp.max(st, axis=0, keepdims=True))
            total = jnp.zeros((1, length), F32)
            ot = jnp.zeros((64, length), F32)
            for c in range(mem_total // step):
                e = jnp.exp(st_ref[half, pl.ds(c * step, step), :] - top)
                total = total + colsum(e)
                ot = ot + mm(vt_ref[head_rows(p, half), pl.ds(c * step, step)], e.astype(BF16))
            ot_ref[head_rows(p, half), :] = ot * (1.0 / total)
            lse_ref[0, 2 * p + half] = top + jnp.log(total)


def feed_both(x2, g3, vec_ref, wide_ref, w1, w2, out_ref, dw1_ref, dw2_ref, sums_ref, wide_sums_ref, u_ref, d_ref, df_ref, f_ref, eu_ref, r_ref):
    length, hidden = u_ref.shape
    hat3, scale3 = normalize(x2)
    gain3 = vec_ref[FEED_GAIN][...]
    h3 = (hat3 * gain3 + vec_ref[FEED_SHIFT][...]).astype(BF16)
    u_ref[...] = mm(h3, w1[...])
    step = 16

    @pl.loop(0, length // step)
    def _(b):
        rows = pl.ds(pl.multiple_of(b * step, step), step)
        u = u_ref[rows, :] + wide_ref[0][...]
        below = 0.5 * (1.0 + lax.erf(u * 0.7071067811865476))
        d_ref[rows, :] = below + u * (jnp.exp(-0.5 * u * u) * 0.3989422804014327)
        hat, scale = normalize(u * below)
        u_ref[rows, :] = hat
        f_ref[rows, :] = (hat * wide_ref[1][...] + wide_ref[2][...]).astype(BF16)
        r_ref[rows, :] = jnp.broadcast_to(scale, (step, 128))

    x3 = x2 + mm(f_ref[...], w2[...]) + vec_ref[OUTER_BIAS][...]
    out_ref[0] = x3.astype(BF16)
    sums_ref[0:1] += colsum(g3)
    e3 = g3.astype(BF16)
    dw2_ref[...] += mm_tn(f_ref[...], e3)
    df_ref[...] = mm_nt(e3, w2[...])

    @pl.loop(0, length // step)
    def _(b):
        rows = pl.ds(pl.multiple_of(b * step, step), step)
        dy, hat = df_ref[rows, :], u_ref[rows, :]
        part = dy * hat
        wide_sums_ref[0:8] += part[0:8] + part[8:16]
        wide_sums_ref[8:16] += dy[0:8] + dy[8:16]
        da = norm_back(dy, hat, r_ref[rows, 0:1], wide_ref[1][...])
        du = da * d_ref[rows, :]
        wide_sums_ref[16:24] += du[0:8] + du[8:16]
        eu_ref[rows, :] = du.astype(BF16)

    dw1_ref[...] += mm_tn(h3, eu_ref[...])
    dh3 = mm_nt(eu_ref[...], w1[...])
    sums_ref[1:2] += colsum(dh3 * hat3)
    sums_ref[2:3] += colsum(dh3)
    return g3 + norm_back(dh3, hat3, scale3, gain3)


def fwd_kernel(
    tlen_ref, mlen_ref, hs_ref,
    tok_ref, cot_ref, mask_ref, buckets_ref, table_ref, mem_hbm, *rest,
):
    vec_ref, wide_ref, rest = rest[:16], rest[16:19], rest[19:]
    wq, wk, wv, wo, wcq, wck, wcv, wco, w1, w2 = rest[:10]
    (
    q1_ref, k1_ref, v1_ref, lse1_ref, ot1_ref,
    x1_ref, q2_ref, k2_ref, v2_ref, lse2_ref, delta2_ref, do2_ref, g2_ref, out_ref,
    gathered_hbm, packed_hbm, bias_hbm, sums_ref, wide_out_ref,
    mem_scr, packed_scr, dwco_ref, dw1_ref, dw2_ref, bias_ref, table_scr,
    x1_scr, vt_scr, st_scr, ot_scr, u_scr, d_scr, df_scr, f_scr, eu_scr, r_scr, wide_scr,
    send_sem, recv_sem, own_sem, out_sem,
    ) = rest[10:]
    seqs = x1_scr.shape[0]
    t = pl.program_id(0)
    places, _, piece, _ = mem_hbm.shape[0], mem_hbm.shape[1], mem_hbm.shape[2], mem_hbm.shape[3]
    me = lax.axis_index("dp")
    mine = pl.ds(pl.multiple_of(me * piece, piece), piece)
    others = pl.ds(0, (places - 1) * piece)

    def own(s):
        return pltpu.make_async_copy(mem_hbm.at[me, s], mem_scr.at[s, mine], own_sem.at[s])

    def save(s):
        return pltpu.make_async_copy(mem_scr.at[s], gathered_hbm.at[s], out_sem.at[s])

    def pack():
        return pltpu.make_async_copy(packed_scr, packed_hbm, out_sem.at[seqs])

    def keep_bias():
        return pltpu.make_async_copy(bias_ref, bias_hbm, out_sem.at[seqs + 1])

    def to_peer(k, s):
        peer = lax.rem(me + k, places)
        return pltpu.make_async_remote_copy(
            src_ref=mem_hbm.at[peer, s], dst_ref=mem_scr.at[s, mine], send_sem=send_sem.at[s], recv_sem=recv_sem.at[s],
            device_id={"dp": peer}, device_id_type=pl.DeviceIdType.MESH,
        )

    def all_peers(s):
        return pltpu.make_async_remote_copy(
            src_ref=mem_scr.at[s, others], dst_ref=mem_scr.at[s, others], send_sem=send_sem.at[s],
            recv_sem=recv_sem.at[s], device_id={"dp": lax.rem(me + 1, places)}, device_id_type=pl.DeviceIdType.MESH,
        )

    @pl.when(t == 0)
    def _():
        for s in range(seqs):
            own(s).start()
        if places > 1:
            meet([{"dp": lax.rem(me + k, places)} for k in range(1, places)])
            for s in range(seqs):

                @pl.loop(1, places)
                def _(k):
                    to_peer(k, s).start()

    @pl.when(t == 0)
    def _():
        for ref in (dwco_ref, dw1_ref, dw2_ref, sums_ref, wide_scr):
            ref[...] = jnp.zeros_like(ref)
        for h in range(table_scr.shape[0]):
            table_scr[h] = table_ref[h : h + 1, :]
        fill_bias(buckets_ref[...], table_scr, bias_ref)
        keep_bias().start()

    @pl.when(t < seqs)
    def _():
        self_forward(
            t, tlen_ref, hs_ref, tok_ref, bias_ref, vec_ref, wq, wk, wv, wo,
            q1_ref, k1_ref, v1_ref, lse1_ref, ot1_ref, x1_scr.at[t], vt_scr,
        )

    @pl.when(t >= seqs)
    def _():
        s = t - seqs
        own(s).wait()
        if places > 1:
            all_peers(s).wait_recv()
        save(s).start()
        x1 = x1_scr[s]
        x1_ref[0] = x1
        cross_forward(
            s, mlen_ref, mem_scr.at[s], vec_ref, x1, wcq, wck, wcv,
            q2_ref, k2_ref, v2_ref, lse2_ref, ot_scr, vt_scr, st_scr,
        )
        hat, scale = normalize(ot_scr[...].T)
        gain = vec_ref[POST_GAIN][...]
        c2 = (hat * gain + vec_ref[POST_SHIFT][...]).astype(BF16)
        x2 = x1 + mm(c2, wco[...]) + vec_ref[CROSS_OUTPUT_BIAS][...]
        length = cot_ref.shape[1]
        here = lax.broadcasted_iota(jnp.int32, mask_ref.shape, 0) == s
        row = jnp.sum(jnp.where(here, mask_ref[...], 0), axis=0, keepdims=True).astype(F32)
        row = jnp.where(lax.broadcasted_iota(jnp.int32, (1, length), 1) < tlen_ref[s], row, 0.0)
        keep = jnp.broadcast_to(row, (8, length)).T[:, 0:1]
        g3 = cot_ref[0].astype(F32) * keep
        g2 = feed_both(
            x2, g3, vec_ref, wide_ref, w1, w2, out_ref, dw1_ref, dw2_ref, sums_ref, wide_scr,
            u_scr, d_scr, df_scr, f_scr, eu_scr, r_scr,
        )
        g2_ref[0] = g2
        sums_ref[3:4] += colsum(g2)
        e2 = g2.astype(BF16)
        dwco_ref[...] += mm_tn(c2, e2)
        dc2 = mm_nt(e2, wco[...])
        sums_ref[4:5] += colsum(dc2 * hat)
        sums_ref[5:6] += colsum(dc2)
        do2 = norm_back(dc2, hat, scale, gain)
        do2_ref[0] = do2.astype(BF16)
        prod = do2.astype(BF16).astype(F32).T * ot_scr[...]
        for h in range(lse2_ref.shape[1]):
            delta2_ref[0, h] = colsum(prod[h * 64 : (h + 1) * 64])

    @pl.when(t == 2 * seqs - 1)
    def _():
        width, hidden = dw1_ref.shape
        for k in range(3):
            wide_out_ref[k : k + 1] = colsum(wide_scr[8 * k : 8 * k + 8])
        for c in range(hidden // width):
            packed_scr[pl.ds(c * width, width), :] = dw1_ref[:, pl.ds(c * width, width)].astype(BF16)
        packed_scr[pl.ds(hidden, hidden), :] = dw2_ref[...].astype(BF16)
        packed_scr[pl.ds(2 * hidden, width), :] = dwco_ref[...].astype(BF16)
        pack().start()
        for s in range(seqs):
            if places > 1:
                all_peers(s).wait_send()
            save(s).wait()
        pack().wait()
        keep_bias().wait()


def forward(tlen, mlen, head_scale, tokens, cotangent, mask, buckets, table, mem, vecs, wides, weights):
    seqs, length, width = tokens.shape
    mem_total = mem.shape[0] * mem.shape[2]
    heads = head_scale.shape[0]
    hidden = wides[0].shape[1]
    early = lambda t, *_: (jnp.minimum(t, seqs - 1), 0, 0)
    late = lambda t, *_: (jnp.maximum(t - seqs, 0), 0, 0)
    whole2 = lambda t, *_: (0, 0)
    const = lambda a: pl.BlockSpec(a.shape, lambda t, *_: (0,) * a.ndim, pipeline_mode=pl.Buffered(1))
    seq = lambda rows, cols, idx: pl.BlockSpec((1, rows, cols), idx)
    row = lambda idx: pl.BlockSpec((1, heads, 1, length), lambda t, *_: idx(t) + (0,))
    sds = jax.ShapeDtypeStruct
    outs = [
        (sds((seqs, length, width), BF16), seq(length, width, early)),
        (sds((seqs, length, width), BF16), seq(length, width, early)),
        (sds((seqs, length, width), BF16), seq(length, width, early)),
        (sds((seqs, heads, 1, length), F32), row(early)),
        (sds((seqs, width, length), F32), seq(width, length, early)),
        (sds((seqs, length, width), F32), seq(length, width, late)),
        (sds((seqs, length, width), BF16), seq(length, width, late)),
        (sds((seqs, mem_total, width), BF16), seq(mem_total, width, late)),
        (sds((seqs, mem_total, width), BF16), seq(mem_total, width, late)),
        (sds((seqs, heads, 1, length), F32), row(late)),
        (sds((seqs, heads, 1, length), F32), row(late)),
        (sds((seqs, length, width), BF16), seq(length, width, late)),
        (sds((seqs, length, width), F32), seq(length, width, late)),
        (sds((seqs, length, width), BF16), seq(length, width, late)),
        (sds((seqs, mem_total, width), BF16), pl.BlockSpec(memory_space=pl.ANY)),
        (sds((2 * hidden + width, width), BF16), pl.BlockSpec(memory_space=pl.ANY)),
        (sds((heads, length, length), F32), pl.BlockSpec(memory_space=pl.ANY)),
        (sds((8, width), F32), pl.BlockSpec((8, width), whole2)),
        (sds((3, hidden), F32), pl.BlockSpec((3, hidden), whole2)),
    ]
    return pl.pallas_call(
        fwd_kernel,
        out_shape=[o[0] for o in outs],
        grid_spec=pltpu.PrefetchScalarGridSpec(
            num_scalar_prefetch=3,
            grid=(2 * seqs,),
            in_specs=[
                seq(length, width, early),
                seq(length, width, late),
                const(mask), const(buckets), const(table),
                pl.BlockSpec(memory_space=pl.ANY),
            ] + [const(a) for a in vecs + wides + weights],
            out_specs=[o[1] for o in outs],
            scratch_shapes=[
                pltpu.VMEM((seqs, mem_total, width), BF16),
                pltpu.VMEM((2 * hidden + width, width), BF16),
                pltpu.VMEM((width, width), F32),
                pltpu.VMEM((width, hidden), F32),
                pltpu.VMEM((hidden, width), F32),
                pltpu.VMEM((heads, length, length), F32),
                pltpu.VMEM((heads, 1, table.shape[1]), F32),
                pltpu.VMEM((seqs, length, width), F32),
                pltpu.VMEM((width, mem_total), BF16),
                pltpu.VMEM((2, mem_total, length), F32),
                pltpu.VMEM((width, length), F32),
                pltpu.VMEM((length, hidden), F32),
                pltpu.VMEM((length, hidden), F32),
                pltpu.VMEM((length, hidden), F32),
                pltpu.VMEM((length, hidden), BF16),
                pltpu.VMEM((length, hidden), BF16),
                pltpu.VMEM((length, 128), F32),
                pltpu.VMEM((24, hidden), F32),
                pltpu.SemaphoreType.DMA((seqs,)),
                pltpu.SemaphoreType.DMA((seqs,)),
                pltpu.SemaphoreType.DMA((seqs,)),
                pltpu.SemaphoreType.DMA((seqs + 2,)),
            ],
        ),
        compiler_params=pltpu.CompilerParams(
            vmem_limit_bytes=VMEM_LIMIT, collective_id=0 if mem.shape[0] > 1 else None, has_side_effects=True
        ),
        name="forward",
    )(tlen, mlen, head_scale, tokens, cotangent, mask, buckets, table, mem, *vecs, *wides, *weights)


def cross_backward(mlen, mem_ref, q_ref, k_ref, v_ref, lse_ref, delta_ref, do_ref, wck, wcv, dk_ref, dv_ref, dqt_ref, kt_ref, dmem_ref, dwck_ref, dwcv_ref, sums_ref, middle):
    length, mem_total = q_ref.shape[0], mem_ref.shape[0]
    step = 256
    for c in range(mem_total // step):
        kt_ref[:, pl.ds(c * step, step)] = k_ref[pl.ds(c * step, step), :].T
    masks = half_masks(length)
    place = lax.broadcasted_iota(jnp.int32, (step, length), 0)

    @pl.loop(0, q_ref.shape[1] // 128)
    def _(p):
        lanes = pair_lanes(p)
        qp, dop = q_ref[:, lanes], do_ref[:, lanes]
        qms = [pick(masks[half], qp) for half in range(2)]
        doms = [pick(masks[half], dop) for half in range(2)]
        lse = [lse_ref[2 * p + half] for half in range(2)]
        delta = [delta_ref[2 * p + half] for half in range(2)]
        dqt = [jnp.zeros((64, length), F32) for half in range(2)]
        for c in range(mem_total // step):
            rows = pl.ds(c * step, step)
            kp, vp = k_ref[rows, lanes], v_ref[rows, lanes]
            outside = jnp.where(place < mlen - c * step, 0.0, NEG)
            dv = jnp.zeros((step, 128), F32)
            dk = jnp.zeros((step, 128), F32)
            for half in range(2):
                st = mm_nt(kp, qms[half]) + outside
                pt = jnp.exp(st - lse[half])
                dpt = mm_nt(vp, doms[half])
                dst = (pt * (dpt - delta[half])).astype(BF16)
                dqt[half] = dqt[half] + mm(kt_ref[head_rows(p, half), rows], dst)
                dv = dv + mm(pt.astype(BF16), doms[half])
                dk = dk + mm(dst, qms[half])
            dv_ref[rows, lanes] = dv.astype(BF16)
            dk_ref[rows, lanes] = dk.astype(BF16)
        for half in range(2):
            dqt_ref[head_rows(p, half), :] = dqt[half]

    middle()

    @pl.loop(0, mem_total // step)
    def _(c):
        rows = pl.ds(pl.multiple_of(c * step, step), step)
        dk, dv = dk_ref[rows, :], dv_ref[rows, :]
        dmem_ref[rows, :] = (mm_nt(dk, wck[...]) + mm_nt(dv, wcv[...])).astype(BF16)
        sums_ref[8:9] += colsum(dv.astype(F32))

    dwck_ref[...] += mm_tn(mem_ref[...], dk_ref[...])
    dwcv_ref[...] += mm_tn(mem_ref[...], dv_ref[...])


def self_backward(tlen, bias_ref, q_ref, k_ref, v_ref, lse_ref, delta_ref, do_ref, dqt_ref, dk_ref, dv_ref, kt_ref, dbias_ref):
    length = q_ref.shape[0]
    kt_ref[:, pl.ds(0, length)] = k_ref[...].T
    key_place = lax.broadcasted_iota(jnp.int32, (length, length), 0)
    outside = jnp.where(key_place < tlen, 0.0, NEG)
    masks = half_masks(length)

    @pl.loop(0, q_ref.shape[1] // 128)
    def _(p):
        lanes = pair_lanes(p)
        qp, dop = q_ref[:, lanes], do_ref[:, lanes]
        kp, vp = k_ref[:, lanes], v_ref[:, lanes]
        dv = jnp.zeros((length, 128), F32)
        dk = jnp.zeros((length, 128), F32)
        for half in range(2):
            h = 2 * p + half
            qm, dom = pick(masks[half], qp), pick(masks[half], dop)
            st = mm_nt(kp, qm) + bias_ref[h] + outside
            pt = jnp.exp(st - lse_ref[h])
            dpt = mm_nt(vp, dom)
            dst = (pt * (dpt - delta_ref[h])).astype(BF16)
            rows = pl.ds(pl.multiple_of(h * length, length), length)
            wide_ds = dst.astype(F32)
            for tile in range(length // 128):
                dbias_ref[tile, rows, :] += wide_ds[:, tile * 128 : (tile + 1) * 128]
            dqt_ref[head_rows(p, half), :] = mm(kt_ref[head_rows(p, half), pl.ds(0, length)], dst)
            dv = dv + mm(pt.astype(BF16), dom)
            dk = dk + mm(dst, qm)
        dv_ref[:, lanes] = dv.astype(BF16)
        dk_ref[:, lanes] = dk.astype(BF16)


def bucket_totals(buckets_t, dbias_ref, out_ref):
    length = buckets_t.shape[0]
    heads = dbias_ref.shape[1] // length
    lo_places = lax.broadcasted_iota(jnp.int32, (32, 128), 0)
    group = 8

    def block(start, tiles, acc):
        rows = buckets_t[pl.ds(start, group), :]
        lefts, rights = [], []
        for k in range(group):
            for tile in tiles:
                ids = rows[k : k + 1, tile * 128 : (tile + 1) * 128]
                d = dbias_ref[tile, pl.ds(start + k, heads, stride=length), :]
                high = jnp.broadcast_to(ids >> 5, (heads, 128))
                lefts.append(jnp.concatenate([jnp.where(high == g, d, 0.0) for g in range(16)], axis=0).astype(BF16))
                rights.append(jnp.where(lo_places == (ids & 31), 1.0, 0.0).astype(BF16))
        return acc + mm_nt(jnp.concatenate(lefts, axis=1), jnp.concatenate(rights, axis=1))

    acc = jnp.zeros((16 * heads, 32), F32)
    tiles = length // 128
    for band in range(tiles):
        live = range(band, tiles)

        def body(b, acc):
            return block(pl.multiple_of(band * 128 + b * group, group), live, acc)

        acc = lax.fori_loop(0, 128 // group, body, acc)
    for g in range(16):
        out_ref[:, g * 32 : (g + 1) * 32] = acc[g * heads : (g + 1) * heads]


FIRST_POINTS = (0, 1, 2, 3, 5, 7, 9, 11, 12, 14, 15)
SECOND_POINTS = (1, 2, 4, 5, 7, 9, 11, 13, 14)
THIRD_POINTS = (8, 9, 11, 13, 15)


def bwd_kernel(
    sizes, groups,
    tlen_ref, mlen_ref,
    hs_ref, tok_ref, mem_ref, bias_ref, buckets_ref, sg_ref, ss_ref, cg_ref, cs_ref, packed_hbm, sums_a_ref, wide_a_ref,
    q1_ref, k1_ref, v1_ref, lse1_ref, ot1_ref,
    x1_ref, q2_ref, k2_ref, v2_ref, lse2_ref, delta2_ref, do2_ref, g2_ref,
    wq, wk, wv, wo, wcq, wck, wcv,
    dtok_ref, dmem_hbm, grads_hbm, small_hbm,
    dmem_scr, g1_scr, grads, land, small, small_land, dw_ref,
    dk_scr, dv_scr, dqt_scr, kt_scr, dbias_scr, delta_scr, do_scr, hs_scr,
    send_sem, recv_sem, own_sem, io_sem, group_send, group_recv, free_sem, buckets_t_scr,
):
    t = pl.program_id(0)
    seqs, heads, length, width = dmem_scr.shape[0], lse1_ref.shape[1], tok_ref.shape[1], tok_ref.shape[2]
    sums_ref = small.at[pl.ds(24, 24)]
    places, piece = dmem_hbm.shape[0], dmem_hbm.shape[2]
    me = lax.axis_index("dp")
    rows_mine = pl.ds(pl.multiple_of(me * piece, piece), piece)

    plain, swapped = stage_orders(sizes)
    reductions = []
    at = 0
    for k, (start, rows) in enumerate(groups):
        order = swapped if k % 2 else plain
        reductions.append(Reduction(grads, land, start, rows, at, order, 16, group_send.at[k], group_recv.at[k], free_sem.at[k]))
        at += reductions[-1].land_rows
    last = len(groups)
    reductions.append(
        Reduction(small, small_land, 0, small.shape[0], 0, plain, 8, group_send.at[last], group_recv.at[last], free_sem.at[last])
    )
    def own(s):
        return pltpu.make_async_copy(dmem_scr.at[s, rows_mine], dmem_hbm.at[me, s], own_sem.at[s])

    def to_peer(k, s):
        peer = lax.rem(me + k, places)
        rows = pl.ds(pl.multiple_of(peer * piece, piece), piece)
        return pltpu.make_async_remote_copy(
            src_ref=dmem_scr.at[s, rows], dst_ref=dmem_hbm.at[me, s], send_sem=send_sem.at[s], recv_sem=recv_sem.at[s],
            device_id={"dp": peer}, device_id_type=pl.DeviceIdType.MESH,
        )

    def all_peers(s):
        some = dmem_hbm.at[pl.ds(0, places - 1), s]
        return pltpu.make_async_remote_copy(
            src_ref=some, dst_ref=some, send_sem=send_sem.at[s], recv_sem=recv_sem.at[s],
            device_id={"dp": lax.rem(me + 1, places)}, device_id_type=pl.DeviceIdType.MESH,
        )

    points = 4 * seqs
    timing = [FIRST_POINTS, FIRST_POINTS, SECOND_POINTS, SECOND_POINTS, THIRD_POINTS, THIRD_POINTS]
    acts = {p: [] for p in range(points)}
    moved = [0] * len(reductions)
    for r, when in enumerate(timing):
        for p in when:
            if p < points and moved[r] <= len(reductions[r]):
                acts[p].append((r, moved[r]))
                moved[r] += 1
    pieces = [(s, k) for s in range(seqs) for k in range(1, places)]
    quota = -(-len(pieces) // (points - 2))
    sends = {p: [] for p in range(points)}
    for p in range(2, points):
        for _ in range(quota):
            if pieces and 2 * (pieces[0][0] + 1) <= p:
                s, k = pieces.pop(0)
                if sends[p] and sends[p][-1][0] == s:
                    sends[p][-1][2] = k + 1
                else:
                    sends[p].append([s, k, k + 1])

    def send(s, first, end):
        @pl.loop(first, end)
        def _(k):
            to_peer(k, s).start()

    def point(half):
        for step in range(2 * seqs):
            p = 2 * step + half
            if acts[p] or sends[p]:

                @pl.when(t == step)
                def _():
                    for r, k in acts[p]:
                        reductions[r].advance(k)
                    for s, first, end in sends[p]:
                        send(s, first, end)

    @pl.when(t == 0)
    def _():
        early = packed_hbm.shape[0]
        load = pltpu.make_async_copy(packed_hbm, grads.at[pl.ds(0, early)], io_sem.at[0])
        load.start()
        for ref in (dw_ref, dbias_scr, hs_scr, small):
            ref[...] = jnp.zeros_like(ref)
        buckets_t_scr[...] = buckets_ref[...].T
        small[0:8] = sums_a_ref[...]
        hidden = wide_a_ref.shape[1]
        for k in range(3):
            for c in range(hidden // width):
                row = 8 + k * (hidden // width) + c
                small[row : row + 1] = wide_a_ref[k : k + 1, c * width : (c + 1) * width]
        peers = [{"dp": lax.rem(me + k, places)} for k in range(1, places)]
        rep = lax.axis_index("rep")
        for bit in range(sizes["rep"].bit_length() - 1):
            peers.append({"rep": rep + (1 - 2 * ((rep // 2**bit) % 2)) * 2**bit})
        if peers:
            meet(peers)
        load.wait()

    point(0)

    @pl.when(t < seqs)
    def _():
        cross_backward(
            mlen_ref[t], mem_ref.at[0], q2_ref.at[0], k2_ref.at[0], v2_ref.at[0], lse2_ref.at[0], delta2_ref.at[0],
            do2_ref.at[0], wck, wcv, dk_scr, dv_scr, dqt_scr, kt_scr, dmem_scr.at[t], dw_ref.at[5], dw_ref.at[6],
            sums_ref, lambda: point(1),
        )
        own(t).start()
        dq2 = (dqt_scr[...].T.astype(BF16).astype(F32) * 0.125).astype(BF16)
        hat2, scale2 = normalize(x1_ref[0])
        gain2 = cg_ref[...]
        h2 = (hat2 * gain2 + cs_ref[...]).astype(BF16)
        dw_ref[4] += mm_tn(h2, dq2)
        sums_ref[7:8] += colsum(dq2.astype(F32))
        dh2 = mm_nt(dq2, wcq[...])
        sums_ref[5:6] += colsum(dh2 * hat2)
        sums_ref[6:7] += colsum(dh2)
        g1 = g2_ref[0] + norm_back(dh2, hat2, scale2, gain2)
        g1_scr[t] = g1
        sums_ref[4:5] += colsum(g1)
        e1 = g1.astype(BF16)
        c1t = scaled_heads(ot1_ref[0], hs_ref).astype(BF16)
        dw_ref[3] += mm(c1t, e1)

    @pl.when(t == seqs - 1)
    def _():
        for k in range(4):
            grads[pl.ds(groups[4][0] + k * width, width), :] = dw_ref[3 + k].astype(BF16)

    @pl.when(t >= seqs)
    def _():
        s = t - seqs
        g1 = g1_scr[s]
        dc1 = mm_nt(g1.astype(BF16), wo[...])
        dc1t = dc1.T
        do1t = scaled_heads(dc1t, hs_ref).astype(BF16)
        do_scr[...] = do1t.T
        for h in range(heads):
            rows = slice(h * 64, (h + 1) * 64)
            o = ot1_ref[0, rows, :]
            hs_scr[h : h + 1, :] += colsum(o * dc1t[rows])
            delta_scr[h] = colsum(o * do1t[rows].astype(F32))
        self_backward(
            tlen_ref[s], bias_ref, q1_ref.at[0], k1_ref.at[0], v1_ref.at[0], lse1_ref.at[0], delta_scr, do_scr,
            dqt_scr, dk_scr.at[pl.ds(0, length)], dv_scr.at[pl.ds(0, length)], kt_scr, dbias_scr,
        )
        point(1)
        dq1 = (dqt_scr[...].T.astype(BF16).astype(F32) * 0.125).astype(BF16)
        dk1 = dk_scr[pl.ds(0, length), :]
        dv1 = dv_scr[pl.ds(0, length), :]
        hat1, scale1 = normalize(tok_ref[0].astype(F32))
        gain1 = sg_ref[...]
        h1 = (hat1 * gain1 + ss_ref[...]).astype(BF16)
        dw_ref[0] += mm_tn(h1, dq1)
        dw_ref[1] += mm_tn(h1, dk1)
        dw_ref[2] += mm_tn(h1, dv1)
        sums_ref[2:3] += colsum(dq1.astype(F32))
        sums_ref[3:4] += colsum(dv1.astype(F32))
        dh1 = mm_nt(dq1, wq[...]) + mm_nt(dk1, wk[...]) + mm_nt(dv1, wv[...])
        sums_ref[0:1] += colsum(dh1 * hat1)
        sums_ref[1:2] += colsum(dh1)
        dtok_ref[0] = (g1 + norm_back(dh1, hat1, scale1, gain1)).astype(BF16)

    @pl.when(t == 2 * seqs - 1)
    def _():
        for k in range(3):
            grads[pl.ds(groups[6][0] + k * width, width), :] = dw_ref[k].astype(BF16)
        sums_ref[16 : 16 + heads] = jnp.broadcast_to(jnp.sum(hs_scr[...], axis=1, keepdims=True), (heads, width))
        late = [6, 7] + [r for r in range(6)]
        for r in (6, 7):
            reductions[r].advance(0)
            moved[r] = 1
        bucket_totals(buckets_t_scr, dbias_scr, small.at[pl.ds(48, 8)])
        late.append(last)
        while any(moved[r] <= len(reductions[r]) for r in late):
            for r in late:
                reductions[r].advance(moved[r])
                moved[r] += 1
        for s, k in pieces:
            send(s, k, k + 1)
        stores = [pltpu.make_async_copy(grads, grads_hbm, io_sem.at[0]), pltpu.make_async_copy(small, small_hbm, io_sem.at[1])]
        for c in stores:
            c.start()
        for s in range(seqs):
            own(s).wait()
            if places > 1:
                all_peers(s).wait_send()
                all_peers(s).wait_recv()
        for c in stores:
            c.wait()


def backward(sizes, tlen, mlen, head_scale, tokens, mem, bias, buckets, vecs, packed, sums_a, wide_a, saved, weights):
    seqs, length, width = tokens.shape
    mem_total = mem.shape[1]
    heads = bias.shape[0]
    places = sizes["dp"]
    early = packed.shape[0]
    quarter = early // (9 * width) * 2 * width
    groups = [(k * quarter, quarter) for k in range(2)]
    groups += [(2 * quarter, early - 3 * quarter), (early - quarter, quarter)]
    groups += [(early, 2 * width), (early + 2 * width, 2 * width)]
    groups += [(early + 4 * width, 2 * width), (early + 6 * width, width)]
    total = early + 7 * width
    plain, _ = stage_orders(sizes)
    land = max(sum(land_rows(rows, plain, 16) for _, rows in groups), 16)
    small_rows = 64
    small_land = max(land_rows(small_rows, plain, 8), 8)
    late = lambda t, *_: jnp.maximum(t - seqs, 0)
    soon = lambda t, *_: jnp.minimum(t, seqs - 1)
    both = lambda t, *_: jnp.where(t < seqs, t, t - seqs)
    const = lambda a: pl.BlockSpec(a.shape, lambda t, *_: (0,) * a.ndim, pipeline_mode=pl.Buffered(1))
    seq = lambda a, idx: pl.BlockSpec((1,) + a.shape[1:], lambda t, *_: (idx(t),) + (0,) * (a.ndim - 1))
    sds = jax.ShapeDtypeStruct
    anywhere = pl.BlockSpec(memory_space=pl.ANY)
    when = [late, late, late, late, both] + [soon] * 8
    slots = max(2 * len(plain), 1)
    several = places > 1 or sizes["rep"] > 1
    return pl.pallas_call(
        functools.partial(bwd_kernel, sizes, groups),
        out_shape=[
            sds((seqs, length, width), BF16),
            sds((places, seqs, mem_total // places, width), BF16),
            sds((total, width), BF16),
            sds((small_rows, width), F32),
        ],
        grid_spec=pltpu.PrefetchScalarGridSpec(
            num_scalar_prefetch=3,
            grid=(2 * seqs,),
            in_specs=[seq(tokens, late), seq(mem, soon), const(bias), const(buckets)] + [const(v) for v in vecs]
            + [anywhere, const(sums_a), const(wide_a)]
            + [seq(a, idx) for a, idx in zip(saved, when)]
            + [const(w) for w in weights],
            out_specs=[seq(tokens, late), anywhere, anywhere, anywhere],
            scratch_shapes=[
                pltpu.VMEM((seqs, mem_total, width), BF16),
                pltpu.VMEM((seqs, length, width), F32),
                pltpu.VMEM((total, width), BF16),
                pltpu.VMEM((land, width), BF16),
                pltpu.VMEM((small_rows, width), F32),
                pltpu.VMEM((small_land, width), F32),
                pltpu.VMEM((7, width, width), F32),
                pltpu.VMEM((mem_total, width), BF16),
                pltpu.VMEM((mem_total, width), BF16),
                pltpu.VMEM((width, length), F32),
                pltpu.VMEM((width, mem_total), BF16),
                pltpu.VMEM((length // 128, heads * length, 128), F32),
                pltpu.VMEM((heads, 1, length), F32),
                pltpu.VMEM((length, width), BF16),
                pltpu.VMEM((heads, length), F32),
                pltpu.SemaphoreType.DMA((seqs,)),
                pltpu.SemaphoreType.DMA((seqs,)),
                pltpu.SemaphoreType.DMA((seqs,)),
                pltpu.SemaphoreType.DMA((2,)),
                pltpu.SemaphoreType.DMA((len(groups) + 1, slots)),
                pltpu.SemaphoreType.DMA((len(groups) + 1, slots)),
                pltpu.SemaphoreType.REGULAR((len(groups) + 1, slots)),
                pltpu.VMEM((length, length), jnp.int32),
            ],
        ),
        compiler_params=pltpu.CompilerParams(
            vmem_limit_bytes=VMEM_LIMIT, collective_id=1 if several else None, has_side_effects=True
        ),
        name="backward",
    )(tlen, mlen, head_scale, tokens, mem, bias, buckets, *vecs, packed, sums_a, wide_a, *saved, *weights)


def unpack_kernel(grads_ref, small_ref, *refs):
    big, vectors, (table_ref, scale_ref, slots, sem) = refs[:10], refs[10:-4], refs[-4:]
    dw1, dw2, rest = big[0], big[1], big[2:]
    width = grads_ref.shape[0]
    parts = dw1.shape[1] // width
    targets = [dw1.at[:, pl.ds(c * width, width)] for c in range(parts)]
    targets += [dw2.at[pl.ds(c * width, width)] for c in range(parts)] + list(rest)
    t = pl.program_id(0)
    depth = slots.shape[0]
    slot = lax.rem(t, depth)

    def settle(k):
        pltpu.make_async_copy(slots.at[k], rest[0], sem.at[k]).wait()

    @pl.when(t >= depth)
    def _():
        settle(slot)

    slots[slot] = grads_ref[...].astype(F32)
    for k, target in enumerate(targets):

        @pl.when(t == k)
        def _():
            pltpu.make_async_copy(slots.at[k % depth], target, sem.at[k % depth]).start()

    @pl.when(t == 0)
    def _():
        for row, ref in zip(VECTOR_ROWS, vectors):
            for c in range(ref.shape[1] // width):
                ref[:, c * width : (c + 1) * width] = small_ref[row + c : row + c + 1]
        heads = scale_ref.shape[1]
        buckets = table_ref.shape[0]
        table_ref[...] = small_ref[48 : 48 + heads].T[:buckets]
        block = small_ref[40 : 40 + heads]
        diagonal = lax.broadcasted_iota(jnp.int32, block.shape, 0) == lax.broadcasted_iota(jnp.int32, block.shape, 1)
        scale_ref[...] = colsum(jnp.where(diagonal, block, 0.0))[:, :heads]

    @pl.when(t == len(targets) - 1)
    def _():
        for k in range(depth):
            settle(k)


VECTOR_ROWS = (24, 25, 26, 27, 28, 29, 30, 31, 32, 4, 5, 3, 1, 2, 0, 16, 8, 12)


def unpack(grads, small, hidden, heads, buckets):
    width = grads.shape[1]
    sds = jax.ShapeDtypeStruct
    big = [sds((width, hidden), F32), sds((hidden, width), F32)] + [sds((width, width), F32)] * 8
    vectors = [sds((1, width), F32)] * 15 + [sds((1, hidden), F32)] * 3
    tail = [sds((buckets, heads), F32), sds((1, heads), F32)]
    whole = lambda a: pl.BlockSpec(a.shape, lambda t: (0,) * len(a.shape))
    steps = grads.shape[0] // width
    return pl.pallas_call(
        unpack_kernel,
        out_shape=big + vectors + tail,
        grid=(steps,),
        in_specs=[pl.BlockSpec((width, width), lambda t: (t, 0)), whole(small)],
        out_specs=[pl.BlockSpec(memory_space=pl.ANY)] * 10 + [whole(a) for a in vectors + tail],
        scratch_shapes=[pltpu.VMEM((4, width, width), F32), pltpu.SemaphoreType.DMA((4,))],
        name="unpack",
    )(grads, small)


def local(
    tokens, cotangent, target_lengths, task_mask, memory_lengths, position_buckets, memory,
    self_gain, self_shift, query_weight, query_bias, key_weight, value_weight, value_bias, position_table, head_scale,
    output_weight, output_bias, cross_gain, cross_shift, cross_query, cross_query_bias, cross_key, cross_value,
    cross_value_bias, post_gain, post_shift, cross_output, cross_output_bias, feed_gain, feed_shift, inner_weight,
    inner_bias, inner_gain, inner_shift, outer_weight, outer_bias,
):
    heads = head_scale.shape[0]
    bucket_count = position_table.shape[0]
    hidden = inner_weight.shape[1]
    table_t = jnp.pad(position_table.T, ((0, 0), (0, 512 - bucket_count)))
    row = lambda v: v.reshape(1, -1)
    vecs = [row(v) for v in (
        self_gain, self_shift, query_bias, value_bias, output_bias, output_bias, cross_gain, cross_shift,
        cross_query_bias, cross_value_bias, post_gain, post_shift, cross_output_bias, feed_gain, feed_shift, outer_bias,
    )]
    wides = [row(v) for v in (inner_bias, inner_gain, inner_shift)]
    sizes = {"dp": lax.axis_size("dp"), "rep": lax.axis_size("rep")}
    fwd = forward(
        target_lengths, memory_lengths, head_scale, tokens, cotangent, task_mask, position_buckets, table_t, memory,
        vecs, wides,
        [query_weight, key_weight, value_weight, output_weight, cross_query, cross_key, cross_value, cross_output,
         inner_weight, outer_weight],
    )
    layer_output, gathered, packed, bias, sums_a, wide_a = fwd[13:]
    dtok, memory_gradient, grads, small = backward(
        sizes, target_lengths, memory_lengths, head_scale, tokens, gathered, bias, position_buckets,
        [vecs[k] for k in (SELF_GAIN, SELF_SHIFT, CROSS_GAIN, CROSS_SHIFT)], packed, sums_a, wide_a, fwd[:13],
        [query_weight, key_weight, value_weight, output_weight, cross_query, cross_key, cross_value],
    )
    outs = unpack(grads, small, hidden, heads, bucket_count)
    dw1, dw2, dwco, dwo, dwcq, dwck, dwcv, dwq, dwk, dwv = outs[:10]
    (
        d_self_gain, d_self_shift, d_query_bias, d_value_bias, d_output_bias, d_cross_gain, d_cross_shift,
        d_cross_query_bias, d_cross_value_bias, d_post_gain, d_post_shift, d_cross_output_bias, d_feed_gain,
        d_feed_shift, d_outer_bias, d_inner_bias, d_inner_gain, d_inner_shift,
    ) = [v.reshape(-1) for v in outs[10:28]]
    d_table, d_scale = outs[28], outs[29].reshape(-1)
    return (
        layer_output, dtok, memory_gradient,
        d_self_gain, d_self_shift, dwq, d_query_bias, dwk, dwv, d_value_bias, d_table, d_scale,
        dwo, d_output_bias, d_cross_gain, d_cross_shift, dwcq, d_cross_query_bias, dwck, dwcv, d_cross_value_bias,
        d_post_gain, d_post_shift, dwco, d_cross_output_bias, d_feed_gain, d_feed_shift, dw1, d_inner_bias,
        d_inner_gain, d_inner_shift, dw2, d_outer_bias,
    )


def solution(mesh):
    per_seq3, per_seq2, per_seq1 = P(("dp", "rep"), None, None), P(("dp", "rep"), None), P(("dp", "rep"))
    spread = P(None, "rep", "dp", None)
    in_specs = (per_seq3, per_seq3, per_seq1, per_seq2, per_seq1, P(), spread) + (P(),) * 30
    out_specs = (per_seq3, per_seq3, spread) + (P(),) * 30
    return jax.shard_map(local, mesh=mesh, in_specs=in_specs, out_specs=out_specs, check_vma=False)
```

```python
import functools

import jax
import jax.numpy as jnp
from jax import lax
from jax.experimental import pallas as pl
from jax.experimental.pallas import tpu as pltpu
from jax.sharding import PartitionSpec as P

NEG = -1e30
F32 = jnp.float32
BF16 = jnp.bfloat16
VMEM_LIMIT = 67043328

(
    SELF_GAIN,
    SELF_SHIFT,
    QUERY_BIAS,
    VALUE_BIAS,
    HEAD_SCALE,
    OUTPUT_BIAS,
    CROSS_GAIN,
    CROSS_SHIFT,
    CROSS_QUERY_BIAS,
    CROSS_VALUE_BIAS,
    POST_GAIN,
    POST_SHIFT,
    CROSS_OUTPUT_BIAS,
    FEED_GAIN,
    FEED_SHIFT,
    OUTER_BIAS,
) = range(16)


def mm(a, b):
    return jnp.dot(a, b, preferred_element_type=F32)


def mm_nt(a, b):
    return lax.dot_general(a, b, (((1,), (1,)), ((), ())), preferred_element_type=F32)


def mm_tn(a, b):
    return lax.dot_general(a, b, (((0,), (0,)), ((), ())), preferred_element_type=F32)


def normalize(x):
    center = x - jnp.mean(x, axis=-1, keepdims=True)
    spread = jnp.mean(center * center, axis=-1, keepdims=True)
    scale = lax.rsqrt(spread + 1e-05)
    return center * scale, scale


def norm_back(dy, hat, scale, gain):
    w = dy * gain
    first = jnp.mean(w, axis=-1, keepdims=True)
    second = jnp.mean(w * hat, axis=-1, keepdims=True)
    return (w - first - hat * second) * scale


def colsum(x):
    return jnp.sum(x, axis=0, keepdims=True)


def half_masks(rows):
    lane = lax.broadcasted_iota(jnp.int32, (rows, 128), 1)
    return (lane < 64, lane >= 64)


def pick(mask, x):
    return jnp.where(mask, x.astype(F32), 0.0).astype(BF16)


def pair_lanes(p):
    return pl.ds(pl.multiple_of(p * 128, 128), 128)


def head_rows(p, half):
    return pl.ds(pl.multiple_of(p * 128 + half * 64, 64), 64)


def fill_bias(buckets, table_rows, out_ref):
    length = buckets.shape[0]
    chunks = table_rows.shape[2] // 128
    low, high = buckets & 127, buckets >> 7
    key_place = lax.broadcasted_iota(jnp.int32, (length, 128), 0)
    lane = lax.broadcasted_iota(jnp.int32, (length, 128), 1)

    @pl.loop(0, out_ref.shape[0])
    def _(h):
        rows = [jnp.broadcast_to(table_rows[h, :, pl.ds(c * 128, 128)], (length, 128)) for c in range(chunks)]
        for tile in range(length // 128):
            cols = slice(tile * 128, (tile + 1) * 128)
            total = jnp.zeros((length, 128), F32)
            for c in range(chunks):
                got = jnp.take_along_axis(rows[c], low[:, cols], axis=1, mode="promise_in_bounds")
                total = jnp.where(high[:, cols] == c, got, total)
            out_ref[h, :, pl.ds(tile * 128, 128)] = jnp.where(key_place <= lane + tile * 128, total, NEG)


def axis_bits(sizes):
    return [(axis, bit) for axis in ("rep", "dp") for bit in range(sizes[axis].bit_length() - 1)]


def stage_orders(sizes):
    plain = axis_bits(sizes)
    reps = sizes["rep"].bit_length() - 1
    swapped = list(plain)
    if reps >= 2 and len(plain) > reps:
        swapped = plain[: reps - 1] + [plain[reps], plain[reps - 1]] + plain[reps + 1 :]
    return plain, swapped


def flip(axis, bit):
    place = lax.axis_index(axis)
    return {axis: place + (1 - 2 * ((place // 2**bit) % 2)) * 2**bit}


def fold_sizes(rows, stages, tile):
    sizes, span = [], rows
    for _ in stages:
        span = span // 2 if span % (2 * tile) == 0 else span
        sizes.append(span)
    return sizes


class Reduction:
    def __init__(self, buf, start, rows, out, out_start, stages, tile, lands, send, recv, store):
        self.buf, self.out, self.tile, self.lands = buf, out, tile, lands
        self.send, self.recv, self.shift = send, recv, out_start - start
        folds, spreads = [], []
        base, span = start, rows
        for (axis, bit), size in zip(stages, fold_sizes(rows, stages, tile)):
            mine = (lax.axis_index(axis) // 2**bit) % 2
            peer = flip(axis, bit)
            halve = size < span
            keep = base + mine * size if halve else base
            give = base + (1 - mine) * size if halve else base
            folds.append((peer, give, keep, size))
            if halve:
                spreads.insert(0, (peer, keep, size))
            base, span = keep, size
        self.folds, self.spreads, self.own = folds, spreads, (base, span)
        self.store = pltpu.make_async_copy(self.part(buf, base, span), self.part(out, base + self.shift, span), store)

    def __len__(self):
        return len(self.folds) + len(self.spreads)

    def part(self, ref, start, size):
        return ref.at[pl.ds(start if isinstance(start, int) else pl.multiple_of(start, self.tile), size)]

    def copy(self, k):
        n = len(self.folds)
        if k < n:
            peer, give, keep, size = self.folds[k]
            land, at = self.lands[k]
            source, target = self.part(self.buf, give, size), land.at[pl.ds(at, size)]
        else:
            peer, base, size = self.spreads[k - n]
            target = self.part(self.out, base + self.shift, size)
            source = self.part(self.buf, base, size) if k == n else target
        return pltpu.make_async_remote_copy(
            src_ref=source, dst_ref=target, send_sem=self.send.at[k], recv_sem=self.recv.at[k],
            device_id=peer, device_id_type=pl.DeviceIdType.MESH,
        )

    def start(self, k):
        if k == len(self.folds):
            self.store.start()
        if k == min(len(self.folds) + 1, len(self)):
            self.store.wait()
        if k < len(self):
            self.copy(k).start()

    def finish(self, k):
        self.copy(k).wait()
        if k < len(self.folds):
            peer, give, keep, size = self.folds[k]
            land, at = self.lands[k]
            step = next(c for c in (128, 64, 48, 32, 16, 8) if size % c == 0)

            @pl.loop(0, size // step)
            def _(b):
                kept = pl.ds(pl.multiple_of(keep + b * step, self.tile), step)
                came = pl.ds(pl.multiple_of(at + b * step, self.tile), step)
                total = self.buf[kept, :].astype(F32) + land[came, :].astype(F32)
                self.buf[kept, :] = total.astype(self.buf.dtype)

    def advance(self, k):
        if 0 < k <= len(self):
            self.finish(k - 1)
        if k <= len(self):
            self.start(k)


def signal_all(sem, peers):
    for peer in peers:
        pl.semaphore_signal(sem, inc=1, device_id=peer, device_id_type=pl.DeviceIdType.MESH)


def scaled_heads(value_t, hs_ref):
    return jnp.concatenate([value_t[h * 64 : (h + 1) * 64] * hs_ref[h] for h in range(value_t.shape[0] // 64)], axis=0)


def self_forward(
    tlen, hs_ref, tok, bias_ref, vec_ref, wq, wk, wv, wo, q_ref, k_ref, v_ref, lse_ref, ot_ref, x1_ref, vt_ref
):
    length = tok.shape[0]
    x0 = tok.astype(F32)
    hat, _ = normalize(x0)
    h1 = (hat * vec_ref[SELF_GAIN][...] + vec_ref[SELF_SHIFT][...]).astype(BF16)
    q_ref[...] = ((mm(h1, wq[...]) + vec_ref[QUERY_BIAS][...]) * 0.125).astype(BF16)
    k_ref[...] = mm(h1, wk[...]).astype(BF16)
    value = (mm(h1, wv[...]) + vec_ref[VALUE_BIAS][...]).astype(BF16)
    v_ref[...] = value
    vt_ref[:, pl.ds(0, length)] = value.T
    key_place = lax.broadcasted_iota(jnp.int32, (length, length), 0)
    outside = jnp.where(key_place < tlen, 0.0, NEG)
    masks = half_masks(length)

    @pl.loop(0, q_ref.shape[1] // 128)
    def _(p):
        lanes = pair_lanes(p)
        kp, qp = k_ref[:, lanes], q_ref[:, lanes]
        for half in range(2):
            st = mm_nt(kp, pick(masks[half], qp)) + bias_ref[2 * p + half] + outside
            top = jnp.max(st, axis=0, keepdims=True)
            e = jnp.exp(st - top)
            total = colsum(e)
            ot = mm(vt_ref[head_rows(p, half), pl.ds(0, length)], e.astype(BF16))
            ot_ref[head_rows(p, half), :] = ot * (1.0 / total)
            lse_ref[2 * p + half] = top + jnp.log(total)

    c1 = scaled_heads(ot_ref[...], hs_ref).T.astype(BF16)
    x1_ref[...] = x0 + mm(c1, wo[...]) + vec_ref[OUTPUT_BIAS][...]


def cross_forward(mlen, mem_ref, vec_ref, x1, wcq, wck, wcv, q_ref, k_ref, v_ref, lse_ref, ot_ref, vt_ref, st_ref):
    length, mem_total = x1.shape[0], mem_ref.shape[0]
    hat, _ = normalize(x1)
    h2 = (hat * vec_ref[CROSS_GAIN][...] + vec_ref[CROSS_SHIFT][...]).astype(BF16)
    q_ref[...] = ((mm(h2, wcq[...]) + vec_ref[CROSS_QUERY_BIAS][...]) * 0.125).astype(BF16)
    step = 256

    @pl.loop(0, mem_total // step)
    def _(c):
        rows = pl.ds(pl.multiple_of(c * step, step), step)
        part = mem_ref[rows, :]
        k_ref[rows, :] = mm(part, wck[...]).astype(BF16)
        v_ref[rows, :] = (mm(part, wcv[...]) + vec_ref[CROSS_VALUE_BIAS][...]).astype(BF16)

    for c in range(mem_total // step):
        vt_ref[:, pl.ds(c * step, step)] = v_ref[pl.ds(c * step, step), :].T
    masks = half_masks(length)
    place = lax.broadcasted_iota(jnp.int32, (step, length), 0)
    tiles = length // 128

    @pl.loop(0, q_ref.shape[1] // 128)
    def _(p):
        lanes = pair_lanes(p)
        qp = q_ref[:, lanes]
        for half in range(2):
            qm = pick(masks[half], qp)
            top = jnp.full((1, length), -jnp.inf, F32)
            for c in range(mem_total // step):
                st = mm_nt(k_ref[pl.ds(c * step, step), lanes], qm)
                st = st + jnp.where(place < mlen - c * step, 0.0, NEG)
                for tile in range(tiles):
                    st_ref[tile, pl.ds(half * mem_total + c * step, step), :] = st[:, tile * 128 : (tile + 1) * 128]
                top = jnp.maximum(top, jnp.max(st, axis=0, keepdims=True))
            total = jnp.zeros((1, length), F32)
            ot = jnp.zeros((64, length), F32)
            for c in range(mem_total // step):
                rows = pl.ds(half * mem_total + c * step, step)
                st = jnp.concatenate([st_ref[tile, rows, :] for tile in range(tiles)], axis=1)
                e = jnp.exp(st - top)
                total = total + colsum(e)
                ot = ot + mm(vt_ref[head_rows(p, half), pl.ds(c * step, step)], e.astype(BF16))
            ot_ref[head_rows(p, half), :] = ot * (1.0 / total)
            lse_ref[2 * p + half] = top + jnp.log(total)


def feed_both(x2, g3, vec_ref, wide_ref, w1, w2, out_ref, acc, sums_ref, wide_sums_ref, u_ref, d_ref, df_ref, f_ref, r_ref, middle):
    length, hidden = u_ref.shape
    width = x2.shape[1]
    parts = hidden // width
    hat3, scale3 = normalize(x2)
    gain3 = vec_ref[FEED_GAIN][...]
    h3 = (hat3 * gain3 + vec_ref[FEED_SHIFT][...]).astype(BF16)
    cols = [pl.ds(c * width, width) for c in range(parts)]
    chunk = [pl.ds(c * length, length) for c in range(parts)]
    for c in range(parts):
        u_ref[:, cols[c]] = mm(h3, w1[cols[c], :])
    step = 16
    tiles = hidden // 128
    halves = d_ref.shape[0]

    def d_place(b, k):
        return k % halves, pl.ds(pl.multiple_of((k // halves) * length + b * step, step), step)

    @pl.loop(0, length // step)
    def _(b):
        rows = pl.ds(pl.multiple_of(b * step, step), step)
        u = u_ref[rows, :] + wide_ref[0][...]
        below = 0.5 * (1.0 + lax.erf(u * 0.7071067811865476))
        d = below + u * (jnp.exp(-0.5 * u * u) * 0.3989422804014327)
        for k in range(tiles):
            tile, place = d_place(b, k)
            d_ref[tile, place, :] = d[:, k * 128 : (k + 1) * 128]
        hat, scale = normalize(u * below)
        u_ref[rows, :] = hat
        f = (hat * wide_ref[1][...] + wide_ref[2][...]).astype(BF16)
        for c in range(parts):
            f_ref[pl.ds(pl.multiple_of(c * length + b * step, step), step), :] = f[:, c * width : (c + 1) * width]
        r_ref[rows, :] = jnp.broadcast_to(scale, (step, 128))

    x3 = x2 + vec_ref[OUTER_BIAS][...]
    for c in range(parts):
        x3 = x3 + mm(f_ref[chunk[c], :], w2[cols[c], :])
    out_ref[0] = x3.astype(BF16)
    sums_ref[0:1] += colsum(g3)
    e3 = g3.astype(BF16)
    for c in range(parts):
        acc[pl.ds(hidden + c * width, width), :] += mm_tn(f_ref[chunk[c], :], e3)
        df_ref[:, cols[c]] = mm_nt(e3, w2[cols[c], :])
    middle()

    @pl.loop(0, length // step)
    def _(b):
        rows = pl.ds(pl.multiple_of(b * step, step), step)
        dy, hat = df_ref[rows, :], u_ref[rows, :]
        part = dy * hat
        wide_sums_ref[0:8] += part[0:8] + part[8:16]
        wide_sums_ref[8:16] += dy[0:8] + dy[8:16]
        da = norm_back(dy, hat, r_ref[rows, 0:1], wide_ref[1][...])
        pieces = []
        for k in range(tiles):
            tile, place = d_place(b, k)
            pieces.append(d_ref[tile, place, :])
        du = da * jnp.concatenate(pieces, axis=1)
        wide_sums_ref[16:24] += du[0:8] + du[8:16]
        eu = du.astype(BF16)
        for c in range(parts):
            f_ref[pl.ds(pl.multiple_of(c * length + b * step, step), step), :] = eu[:, c * width : (c + 1) * width]

    dh3 = jnp.zeros(x2.shape, F32)
    h3t = h3.T
    for c in range(parts):
        acc[cols[c], :] += mm(h3t, f_ref[chunk[c], :])
        dh3 = dh3 + mm_nt(f_ref[chunk[c], :], w1[cols[c], :])
    sums_ref[1:2] += colsum(dh3 * hat3)
    sums_ref[2:3] += colsum(dh3)
    return g3 + norm_back(dh3, hat3, scale3, gain3)


def cross_backward(
    mlen, mem_ref, q_ref, k_ref, v_ref, lse_ref, delta_ref, do_ref, wck, wcv, dk_ref, dv_ref, dqt_ref, kt_ref,
    acc_key, acc_value, sums_ref, points,
):
    length, mem_total = q_ref.shape[0], mem_ref.shape[0]
    step = 256
    for c in range(mem_total // step):
        kt_ref[:, pl.ds(c * step, step)] = k_ref[pl.ds(c * step, step), :].T
    masks = half_masks(length)
    place = lax.broadcasted_iota(jnp.int32, (step, length), 0)
    pairs = q_ref.shape[1] // 128

    @pl.loop(0, pairs)
    def _(p):
        @pl.when(p == pairs // 2)
        def _():
            points[0]()

        lanes = pair_lanes(p)
        qp, dop = q_ref[:, lanes], do_ref[:, lanes]
        qms = [pick(masks[half], qp) for half in range(2)]
        doms = [pick(masks[half], dop) for half in range(2)]
        lse = [lse_ref[2 * p + half] for half in range(2)]
        delta = [delta_ref[2 * p + half] for half in range(2)]
        dqt = [jnp.zeros((64, length), F32) for half in range(2)]
        for c in range(mem_total // step):
            rows = pl.ds(c * step, step)
            kp, vp = k_ref[rows, lanes], v_ref[rows, lanes]
            outside = jnp.where(place < mlen - c * step, 0.0, NEG)
            dv = jnp.zeros((step, 128), F32)
            dk = jnp.zeros((step, 128), F32)
            for half in range(2):
                st = mm_nt(kp, qms[half]) + outside
                pt = jnp.exp(st - lse[half])
                dpt = mm_nt(vp, doms[half])
                dst = (pt * (dpt - delta[half])).astype(BF16)
                dqt[half] = dqt[half] + mm(kt_ref[head_rows(p, half), rows], dst)
                dv = dv + mm(pt.astype(BF16), doms[half])
                dk = dk + mm(dst, qms[half])
            dv_ref[rows, lanes] = dv.astype(BF16)
            dk_ref[rows, lanes] = dk.astype(BF16)
        for half in range(2):
            dqt_ref[head_rows(p, half), :] = dqt[half]

    points[1]()
    acc_key[...] += mm_tn(mem_ref[...], dk_ref[...])
    acc_value[...] += mm_tn(mem_ref[...], dv_ref[...])

    @pl.loop(0, mem_total // step)
    def _(c):
        rows = pl.ds(pl.multiple_of(c * step, step), step)
        dk, dv = dk_ref[rows, :], dv_ref[rows, :]
        mem_ref[rows, :] = (mm_nt(dk, wck[...]) + mm_nt(dv, wcv[...])).astype(BF16)
        sums_ref[8:9] += colsum(dv.astype(F32))


def self_backward(tlen, bias_ref, q_ref, k_ref, v_ref, lse_ref, delta_ref, do_ref, dqt_ref, dk_ref, dv_ref, kt_ref, dbias_ref):
    length = q_ref.shape[0]
    kt_ref[:, pl.ds(0, length)] = k_ref[...].T
    key_place = lax.broadcasted_iota(jnp.int32, (length, length), 0)
    outside = jnp.where(key_place < tlen, 0.0, NEG)
    masks = half_masks(length)

    @pl.loop(0, q_ref.shape[1] // 128)
    def _(p):
        lanes = pair_lanes(p)
        qp, dop = q_ref[:, lanes], do_ref[:, lanes]
        kp, vp = k_ref[:, lanes], v_ref[:, lanes]
        dv = jnp.zeros((length, 128), F32)
        dk = jnp.zeros((length, 128), F32)
        for half in range(2):
            h = 2 * p + half
            qm, dom = pick(masks[half], qp), pick(masks[half], dop)
            st = mm_nt(kp, qm) + bias_ref[h] + outside
            pt = jnp.exp(st - lse_ref[h])
            dpt = mm_nt(vp, dom)
            dst = (pt * (dpt - delta_ref[h])).astype(BF16)
            rows = pl.ds(pl.multiple_of(h * length, length), length)
            wide_ds = dst.astype(F32)
            for tile in range(length // 128):
                dbias_ref[tile, rows, :] += wide_ds[:, tile * 128 : (tile + 1) * 128]
            dqt_ref[head_rows(p, half), :] = mm(kt_ref[head_rows(p, half), pl.ds(0, length)], dst)
            dv = dv + mm(pt.astype(BF16), dom)
            dk = dk + mm(dst, qm)
        dv_ref[:, lanes] = dv.astype(BF16)
        dk_ref[:, lanes] = dk.astype(BF16)


def bucket_totals(buckets_t, dbias_ref, out_ref):
    length = buckets_t.shape[0]
    heads = dbias_ref.shape[1] // length
    lo_places = lax.broadcasted_iota(jnp.int32, (32, 128), 0)
    group = 8

    def block(start, tiles, acc):
        rows = buckets_t[pl.ds(start, group), :]
        lefts, rights = [], []
        for k in range(group):
            for tile in tiles:
                ids = rows[k : k + 1, tile * 128 : (tile + 1) * 128]
                d = dbias_ref[tile, pl.ds(start + k, heads, stride=length), :]
                high = jnp.broadcast_to(ids >> 5, (heads, 128))
                lefts.append(jnp.concatenate([jnp.where(high == g, d, 0.0) for g in range(16)], axis=0).astype(BF16))
                rights.append(jnp.where(lo_places == (ids & 31), 1.0, 0.0).astype(BF16))
        return acc + mm_nt(jnp.concatenate(lefts, axis=1), jnp.concatenate(rights, axis=1))

    acc = jnp.zeros((16 * heads, 32), F32)
    tiles = length // 128
    for band in range(tiles):
        live = range(band, tiles)

        def body(b, acc):
            return block(pl.multiple_of(band * 128 + b * group, group), live, acc)

        acc = lax.fori_loop(0, 128 // group, body, acc)
    for g in range(16):
        out_ref[:, g * 32 : (g + 1) * 32] = acc[g * heads : (g + 1) * heads]


SMALL_ROWS = 64
SUMS_B = 24
HEAD_ROWS = 40
TABLE_ROWS = 48


def piece_order(places):
    far, near = list(range(max(places // 2, 1), places)), list(range(1, places // 2))
    order = []
    for k in range(len(far)):
        order.append(far[k])
        if k < len(near):
            order.append(near[k])
    return order


def partner(me, places, k):
    if places & (places - 1):
        return lax.rem(me + k, places)
    for bit in range(places.bit_length() - 1):
        if (k >> bit) & 1:
            me = me + (1 - 2 * ((me // 2**bit) % 2)) * 2**bit
    return me


def layer_kernel(sizes, layout, tlen_ref, mlen_ref, hs_ref, tok_ref, cot_ref, mask_ref, buckets_ref, table_ref, *rest):
    mem_hbm, w1_hbm, w2_hbm = rest[:3]
    vec_ref, wide_ref = rest[3:19], rest[19:22]
    wq, wk, wv, wo, wcq, wck, wcv, wco = rest[22:30]
    out_ref, dtok_ref, dmem_hbm, grads_hbm, small_hbm = rest[30:35]
    (
        mem_scr, w1s, w2s, acc, bias_ref, st_scr,
        q1_scr, k1_scr, v1_scr, lse1_scr, ot1_scr, x1_scr,
        kv_scr, q2_scr, do_scr, lse2_scr, delta_scr,
        vt_scr, ot_scr, u_scr, df_scr, r_scr, dk_scr, dv_scr,
        grads, land, small, small_land, wide_scr, hs_scr, table_scr, buckets_t_scr,
        load_sem, send_sem, recv_sem, own_sem, back_send, back_recv, back_own, group_send, group_recv, store_sem, ready_sem,
    ) = rest[35:]
    seqs, mem_total, width = mem_scr.shape
    length, hidden, heads = tok_ref.shape[1], u_scr.shape[1], bias_ref.shape[0]
    places, piece = mem_hbm.shape[0], mem_hbm.shape[2]
    t = pl.program_id(0)
    me = lax.axis_index("dp")
    mine = pl.ds(pl.multiple_of(me * piece, piece), piece)
    k2_scr, v2_scr = kv_scr.at[pl.ds(0, mem_total)], kv_scr.at[pl.ds(mem_total, mem_total)]
    sums_a, sums_b = small.at[pl.ds(0, 8)], small.at[pl.ds(SUMS_B, 24)]
    base = 2 * hidden
    acc_at = lambda k: acc.at[pl.ds(base + k * width, width)]
    CROSS_OUT, OUT, QUERY, KEY, VALUE = range(5)
    order = piece_order(places)

    def own_in(s):
        return pltpu.make_async_copy(mem_hbm.at[me, s], mem_scr.at[s, mine], own_sem.at[s])

    def own_back(s):
        return pltpu.make_async_copy(mem_scr.at[s, mine], dmem_hbm.at[me, s], back_own.at[s])

    def loads():
        copies = []
        for c in range(hidden // width):
            cols = pl.ds(c * width, width)
            copies.append(pltpu.make_async_copy(w1_hbm.at[:, cols], w1s.at[cols], load_sem.at[c]))
        copies.append(pltpu.make_async_copy(w2_hbm, w2s, load_sem.at[hidden // width]))
        return copies

    def remote(source, target, send, recv, peer):
        return pltpu.make_async_remote_copy(
            src_ref=source, dst_ref=target, send_sem=send, recv_sem=recv, device_id={"dp": peer},
            device_id_type=pl.DeviceIdType.MESH,
        )

    def send_in(s, k):
        peer = partner(me, places, k)
        remote(mem_hbm.at[peer, s], mem_scr.at[s, mine], send_sem.at[s], recv_sem.at[s], peer).start()

    def send_back(s, k):
        peer = partner(me, places, k)
        rows = pl.ds(pl.multiple_of(peer * piece, piece), piece)
        remote(mem_scr.at[s, rows], dmem_hbm.at[me, s], back_send.at[s], back_recv.at[s], peer).start()

    def all_in(s):
        some = mem_scr.at[s, pl.ds(0, (places - 1) * piece)]
        return remote(some, some, send_sem.at[s], recv_sem.at[s], partner(me, places, 1))

    def all_back(s):
        some = dmem_hbm.at[pl.ds(0, places - 1), s]
        return remote(some, some, back_send.at[s], back_recv.at[s], partner(me, places, 1))

    plain, swapped = stage_orders(sizes)
    pools = {"first": w2s, "second": w1s, "land": land}
    buffers = {"grads": grads, "kv": kv_scr}
    reductions = []
    for r, (buf, start, rows, out_start, lands) in enumerate(layout):
        reductions.append(Reduction(
            buffers[buf], start, rows, grads_hbm, out_start, swapped if r % 2 else plain, 16,
            [(pools[name], at) for name, at in lands], group_send.at[r], group_recv.at[r], store_sem.at[r],
        ))
    last = len(layout)
    at, lands = 0, []
    for size in fold_sizes(SMALL_ROWS, plain, 8):
        lands.append((small_land, at))
        at += size
    reductions.append(Reduction(
        small, 0, SMALL_ROWS, small_hbm, 0, plain, 8, lands, group_send.at[last], group_recv.at[last], store_sem.at[last],
    ))
    first = [r for r, item in enumerate(layout) if item[0] == "grads" and item[1] < base]
    second = [r for r, item in enumerate(layout) if item[0] == "grads" and item[1] >= base]
    third = [r for r, item in enumerate(layout) if item[0] == "kv"]
    flips = [flip(axis, bit) for axis, bit in plain]

    steps = 4 * seqs
    begin_first, begin_second = 3 * (3 * seqs - 1), 3 * 3 * seqs
    acts = {p: [] for p in range(3 * steps)}
    moved = [0] * len(reductions)
    for group, begin, table in ((first, begin_first, FIRST_POINTS), (second, begin_second, SECOND_POINTS)):
        for n, r in enumerate(group):
            for p in table[n % len(table)]:
                if begin + p < 3 * steps and moved[r] <= len(reductions[r]):
                    acts[begin + p].append((r, moved[r]))
                    moved[r] += 1
    queue = [(s, k) for s in range(seqs) for k in order]
    sends = {p: [] for p in range(3 * steps)}
    for p in range(3 * steps):
        quota = -(-len(order) * PIECES[p % len(PIECES)] // 7)
        while quota and queue and p >= 3 * (seqs + 2 * queue[0][0] + 2):
            sends[p].append(queue.pop(0))
            quota -= 1

    def point(part, low, high):
        for step in range(low, high):
            p = 3 * step + part
            if acts[p] or sends[p] or (p == begin_first and flips):

                @pl.when(t == step)
                def _():
                    if p == begin_first and flips:
                        pl.semaphore_wait(ready_sem, len(flips))
                    for r, k in acts[p]:
                        reductions[r].advance(k)
                    for s, k in sends[p]:
                        send_back(s, k)

    @pl.when(t == 0)
    def _():
        bucket_load = pltpu.make_async_copy(buckets_ref, buckets_t_scr, load_sem.at[hidden // width + 1])
        bucket_load.start()
        for s in range(seqs):
            own_in(s).start()
        peers = [{"dp": partner(me, places, k)} for k in range(1, places)]
        peers += [flip(axis, bit) for axis, bit in plain if axis == "rep"]
        if peers:
            barrier = pltpu.get_barrier_semaphore()
            signal_all(barrier, peers)
            pl.semaphore_wait(barrier, len(peers))
        for s in range(seqs):
            for k in order:
                send_in(s, k)
        for c in loads():
            c.start()
        for ref in (acc, small, wide_scr, hs_scr):
            ref[...] = jnp.zeros_like(ref)
        for h in range(heads):
            table_scr[h] = table_ref[h : h + 1, :]
        bucket_load.wait()
        buckets_t_scr[...] = buckets_t_scr[...].T
        fill_bias(buckets_t_scr[...], table_scr, bias_ref)

    @pl.when(t < seqs)
    def _():
        self_forward(
            tlen_ref[t], hs_ref, tok_ref[0], bias_ref, vec_ref, wq, wk, wv, wo,
            q1_scr.at[t], k1_scr.at[t], v1_scr.at[t], lse1_scr.at[t], ot1_scr.at[t], x1_scr.at[t], vt_scr,
        )

    @pl.when(t == seqs)
    def _():
        for c in loads():
            c.wait()

    inner = t - seqs
    s = inner // 2

    @pl.when((t >= seqs) & (t < 3 * seqs) & (inner % 2 == 0))
    def _():
        own_in(s).wait()
        if places > 1:
            all_in(s).wait_recv()
        point(0, seqs, 3 * seqs)
        x1 = x1_scr[s]
        cross_forward(
            mlen_ref[s], mem_scr.at[s], vec_ref, x1, wcq, wck, wcv,
            q2_scr, k2_scr, v2_scr, lse2_scr, ot_scr, vt_scr, st_scr,
        )
        point(1, seqs, 3 * seqs)
        hat, scale = normalize(ot_scr[...].T)
        gain = vec_ref[POST_GAIN][...]
        c2 = (hat * gain + vec_ref[POST_SHIFT][...]).astype(BF16)
        x2 = x1 + mm(c2, wco[...]) + vec_ref[CROSS_OUTPUT_BIAS][...]
        here = lax.broadcasted_iota(jnp.int32, mask_ref.shape, 0) == s
        row = jnp.sum(jnp.where(here, mask_ref[...], 0), axis=0, keepdims=True).astype(F32)
        row = jnp.where(lax.broadcasted_iota(jnp.int32, (1, length), 1) < tlen_ref[s], row, 0.0)
        g3 = cot_ref[0].astype(F32) * jnp.broadcast_to(row, (8, length)).T[:, 0:1]
        g2 = feed_both(
            x2, g3, vec_ref, wide_ref, w1s, w2s, out_ref, acc, sums_a, wide_scr,
            u_scr, st_scr, df_scr, dk_scr, r_scr, lambda: point(2, seqs, 3 * seqs),
        )
        df_scr[:, pl.ds(0, width)] = g2
        sums_a[3:4] += colsum(g2)
        e2 = g2.astype(BF16)
        acc_at(CROSS_OUT)[...] += mm_tn(c2, e2)
        dc2 = mm_nt(e2, wco[...])
        sums_a[4:5] += colsum(dc2 * hat)
        sums_a[5:6] += colsum(dc2)
        do2 = norm_back(dc2, hat, scale, gain).astype(BF16)
        do_scr[...] = do2
        prod = do2.astype(F32).T * ot_scr[...]
        for h in range(heads):
            delta_scr[h] = colsum(prod[h * 64 : (h + 1) * 64])

    @pl.when(t == 3 * seqs - 2)
    def _():
        signal_all(ready_sem, flips)
        for k in range(3):
            total = colsum(wide_scr[8 * k : 8 * k + 8])
            for c in range(hidden // width):
                row = 8 + k * (hidden // width) + c
                small[row : row + 1] = total[:, c * width : (c + 1) * width]

        @pl.loop(0, base // 256)
        def _(b):
            rows = pl.ds(pl.multiple_of(b * 256, 256), 256)
            grads[rows, :] = acc[rows, :].astype(BF16)

    @pl.when((t >= seqs) & (t < 3 * seqs) & (inner % 2 == 1))
    def _():
        point(0, seqs, 3 * seqs)
        cross_backward(
            mlen_ref[s], mem_scr.at[s], q2_scr, k2_scr, v2_scr, lse2_scr, delta_scr, do_scr, wck, wcv,
            dk_scr, dv_scr, ot_scr, vt_scr, acc_at(KEY), acc_at(VALUE), sums_b,
            [lambda: point(1, seqs, 3 * seqs), lambda: point(2, seqs, 3 * seqs)],
        )
        own_back(s).start()
        dq2 = (ot_scr[...].T.astype(BF16).astype(F32) * 0.125).astype(BF16)
        hat2, scale2 = normalize(x1_scr[s])
        gain2 = vec_ref[CROSS_GAIN][...]
        h2 = (hat2 * gain2 + vec_ref[CROSS_SHIFT][...]).astype(BF16)
        acc_at(QUERY)[...] += mm_tn(h2, dq2)
        sums_b[7:8] += colsum(dq2.astype(F32))
        dh2 = mm_nt(dq2, wcq[...])
        sums_b[5:6] += colsum(dh2 * hat2)
        sums_b[6:7] += colsum(dh2)
        g1 = df_scr[:, pl.ds(0, width)] + norm_back(dh2, hat2, scale2, gain2)
        x1_scr[s] = g1
        sums_b[4:5] += colsum(g1)
        c1t = scaled_heads(ot1_scr[s], hs_ref).astype(BF16)
        acc_at(OUT)[...] += mm(c1t, g1.astype(BF16))

    @pl.when(t == 3 * seqs - 1)
    def _():
        @pl.loop(0, 5 * width // 256)
        def _(b):
            rows = pl.ds(pl.multiple_of(base + b * 256, 256), 256)
            grads[rows, :] = acc[rows, :].astype(BF16)

        st_scr[...] = jnp.zeros_like(st_scr)
        acc[pl.ds(0, 3 * width), :] = jnp.zeros((3 * width, width), F32)

    @pl.when(t >= 3 * seqs)
    def _():
        point(0, 3 * seqs, steps)
        s = t - 3 * seqs
        g1 = x1_scr[s]
        dc1t = mm_nt(g1.astype(BF16), wo[...]).T
        do1t = scaled_heads(dc1t, hs_ref).astype(BF16)
        do_scr[...] = do1t.T
        for h in range(heads):
            rows = slice(h * 64, (h + 1) * 64)
            o = ot1_scr[s, rows, :]
            hs_scr[h : h + 1, :] += colsum(o * dc1t[rows])
            delta_scr[h] = colsum(o * do1t[rows].astype(F32))
        dk_ref, dv_ref = dk_scr.at[pl.ds(0, length)], dv_scr.at[pl.ds(0, length)]
        self_backward(
            tlen_ref[s], bias_ref, q1_scr.at[s], k1_scr.at[s], v1_scr.at[s], lse1_scr.at[s], delta_scr, do_scr,
            ot_scr, dk_ref, dv_ref, vt_scr, st_scr,
        )
        point(1, 3 * seqs, steps)
        dq1 = (ot_scr[...].T.astype(BF16).astype(F32) * 0.125).astype(BF16)
        dk1, dv1 = dk_ref[...], dv_ref[...]
        hat1, scale1 = normalize(tok_ref[0].astype(F32))
        gain1 = vec_ref[SELF_GAIN][...]
        h1t = (hat1 * gain1 + vec_ref[SELF_SHIFT][...]).astype(BF16).T
        for k, d in enumerate((dq1, dk1, dv1)):
            acc[pl.ds(k * width, width), :] += mm(h1t, d)
        point(2, 3 * seqs, steps)
        sums_b[2:3] += colsum(dq1.astype(F32))
        sums_b[3:4] += colsum(dv1.astype(F32))
        dh1 = mm_nt(dq1, wq[...]) + mm_nt(dk1, wk[...]) + mm_nt(dv1, wv[...])
        sums_b[0:1] += colsum(dh1 * hat1)
        sums_b[1:2] += colsum(dh1)
        dtok_ref[0] = (g1 + norm_back(dh1, hat1, scale1, gain1)).astype(BF16)

    @pl.when(t == steps - 1)
    def _():
        @pl.loop(0, 3 * width // 256)
        def _(b):
            rows = pl.ds(pl.multiple_of(b * 256, 256), 256)
            kv_scr[rows, :] = acc[rows, :].astype(BF16)

        small[HEAD_ROWS : HEAD_ROWS + heads] = jnp.broadcast_to(
            jnp.sum(hs_scr[...], axis=1, keepdims=True), (heads, width)
        )
        for r in third:
            reductions[r].advance(0)
            moved[r] = 1
        for r in first + second:
            reductions[r].advance(moved[r])
            moved[r] += 1
        bucket_totals(buckets_t_scr, st_scr, small.at[pl.ds(TABLE_ROWS, heads)])
        left = third + [last] + second + first
        while any(moved[r] <= len(reductions[r]) for r in left):
            for r in left:
                reductions[r].advance(moved[r])
                moved[r] += 1
            for _ in range(-(-len(order) * 2 // 7)):
                if queue:
                    send_back(*queue.pop(0))
        for s, k in queue:
            send_back(s, k)
        for s in range(seqs):
            own_back(s).wait()
            if places > 1:
                all_in(s).wait_send()
                all_back(s).wait_send()
                all_back(s).wait_recv()


FIRST_POINTS = ((0, 1, 2, 4, 6, 8, 10, 12), (0, 1, 2, 4, 6, 8, 10, 12), (1, 2, 3, 5, 7, 9, 11, 13), (1, 2, 3, 5, 7, 9, 11, 13))
SECOND_POINTS = ((1, 3, 5, 7, 9), (1, 3, 5, 7, 9), (2, 4, 6, 8, 10), (2, 4, 6, 8, 10))
PIECES = (2, 2, 2)


def reduction_layout(sizes, width, hidden):
    plain, _ = stage_orders(sizes)
    base = 2 * hidden
    members = [("grads", k * hidden // 2, hidden // 2, k * hidden // 2) for k in range(4)]
    members += [("grads", base, 2 * width, base), ("grads", base + 2 * width, 2 * width, base + 2 * width)]
    members += [("grads", base + 4 * width, width, base + 4 * width)]
    members += [("kv", 0, width, base + 5 * width), ("kv", width, width, base + 6 * width)]
    members += [("kv", 2 * width, width, base + 7 * width)]
    used = {"first": 0, "second": 0, "land": 0}
    layout = []
    for buf, start, rows, out_start in members:
        lands = []
        for size in fold_sizes(rows, plain, 16):
            name = "land"
            if buf == "grads":
                name = next((n for n in ("first", "second") if used[n] + size <= hidden), "land")
            lands.append((name, used[name]))
            used[name] += size
        layout.append((buf, start, rows, out_start, lands))
    return layout, max(used["land"], 16)


def whole_layer(sizes, tlen, mlen, head_scale, tokens, cotangent, mask, buckets, table, memory, w1, w2, vecs, wides, weights):
    seqs, length, width = tokens.shape
    places, _, piece, _ = memory.shape
    mem_total = places * piece
    heads, hidden = head_scale.shape[0], w1.shape[1]
    layout, land = reduction_layout(sizes, width, hidden)
    plain, _ = stage_orders(sizes)
    small_land = max(sum(fold_sizes(SMALL_ROWS, plain, 8)), 8)
    slots = max(2 * len(plain), 1)
    several = places > 1 or sizes["rep"] > 1
    sds = jax.ShapeDtypeStruct
    anywhere = pl.BlockSpec(memory_space=pl.ANY)
    const = lambda a: pl.BlockSpec(a.shape, lambda t, *_: (0,) * a.ndim, pipeline_mode=pl.Buffered(1))
    seq = lambda idx: pl.BlockSpec((1, length, width), lambda t, *_: (idx(t), 0, 0))
    ends = lambda t: jnp.where(t < 3 * seqs, jnp.minimum(t, seqs - 1), t - 3 * seqs)
    middle = lambda t: jnp.clip((t - seqs) // 2, 0, seqs - 1)
    late = lambda t: jnp.maximum(t - 3 * seqs, 0)
    tall = heads * length
    scratch = [
        ((seqs, mem_total, width), BF16), ((hidden, width), BF16), ((hidden, width), BF16),
        ((2 * hidden + 5 * width, width), F32), ((heads, length, length), F32),
        ((length // 128, max(tall, 2 * mem_total, hidden * length * 128 // (length * 128)), 128), F32),
        ((seqs, length, width), BF16), ((seqs, length, width), BF16), ((seqs, length, width), BF16),
        ((seqs, heads, 1, length), F32), ((seqs, width, length), F32), ((seqs, length, width), F32),
        ((2 * mem_total, width), BF16), ((length, width), BF16), ((length, width), BF16),
        ((heads, 1, length), F32), ((heads, 1, length), F32),
        ((width, mem_total), BF16), ((width, length), F32), ((length, hidden), F32), ((length, hidden), F32),
        ((length, 128), F32), ((max(mem_total, hidden // width * length), width), BF16), ((mem_total, width), BF16),
        ((2 * hidden + 5 * width, width), BF16), ((land, width), BF16), ((SMALL_ROWS, width), F32), ((small_land, width), F32),
        ((24, hidden), F32), ((heads, length), F32), ((heads, 1, table.shape[1]), F32), ((length, length), jnp.int32),
    ]
    dma = pltpu.SemaphoreType.DMA
    groups = len(layout) + 1
    return pl.pallas_call(
        functools.partial(layer_kernel, sizes, layout),
        out_shape=[
            sds(tokens.shape, BF16), sds(tokens.shape, BF16), sds(memory.shape, BF16),
            sds((2 * hidden + 8 * width, width), BF16), sds((SMALL_ROWS, width), F32),
        ],
        grid_spec=pltpu.PrefetchScalarGridSpec(
            num_scalar_prefetch=3,
            grid=(4 * seqs,),
            in_specs=[seq(ends), seq(middle), const(mask), anywhere, const(table), anywhere, anywhere, anywhere]
            + [const(a) for a in vecs + wides + weights],
            out_specs=[seq(middle), seq(late), anywhere, anywhere, anywhere],
            scratch_shapes=[pltpu.VMEM(shape, dtype) for shape, dtype in scratch] + [
                dma((hidden // width + 2,)), dma((seqs,)), dma((seqs,)), dma((seqs,)), dma((seqs,)), dma((seqs,)),
                dma((seqs,)), dma((groups, slots)), dma((groups, slots)), dma((groups,)), pltpu.SemaphoreType.REGULAR,
            ],
        ),
        compiler_params=pltpu.CompilerParams(
            vmem_limit_bytes=VMEM_LIMIT, collective_id=0 if several else None, has_side_effects=True
        ),
        name="layer",
    )(tlen, mlen, head_scale, tokens, cotangent, mask, buckets, table, memory, w1, w2, *vecs, *wides, *weights)


def unpack_kernel(grads_ref, small_ref, *refs):
    big, vectors, (table_ref, scale_ref, slots, sem) = refs[:10], refs[10:-4], refs[-4:]
    dw1, dw2, rest = big[0], big[1], big[2:]
    width = grads_ref.shape[0]
    parts = dw1.shape[1] // width
    targets = [dw1.at[:, pl.ds(c * width, width)] for c in range(parts)]
    targets += [dw2.at[pl.ds(c * width, width)] for c in range(parts)] + list(rest)
    t = pl.program_id(0)
    depth = slots.shape[0]
    slot = lax.rem(t, depth)

    def settle(k):
        pltpu.make_async_copy(slots.at[k], rest[0], sem.at[k]).wait()

    @pl.when(t >= depth)
    def _():
        settle(slot)

    slots[slot] = grads_ref[...].astype(F32)
    for k, target in enumerate(targets):

        @pl.when(t == k)
        def _():
            pltpu.make_async_copy(slots.at[k % depth], target, sem.at[k % depth]).start()

    @pl.when(t == 0)
    def _():
        for row, ref in zip(VECTOR_ROWS, vectors):
            for c in range(ref.shape[1] // width):
                ref[:, c * width : (c + 1) * width] = small_ref[row + c : row + c + 1]
        heads = scale_ref.shape[1]
        buckets = table_ref.shape[0]
        table_ref[...] = small_ref[48 : 48 + heads].T[:buckets]
        block = small_ref[40 : 40 + heads]
        diagonal = lax.broadcasted_iota(jnp.int32, block.shape, 0) == lax.broadcasted_iota(jnp.int32, block.shape, 1)
        scale_ref[...] = colsum(jnp.where(diagonal, block, 0.0))[:, :heads]

    @pl.when(t == len(targets) - 1)
    def _():
        for k in range(depth):
            settle(k)


VECTOR_ROWS = (24, 25, 26, 27, 28, 29, 30, 31, 32, 4, 5, 3, 1, 2, 0, 16, 8, 12)


def unpack(grads, small, hidden, heads, buckets):
    width = grads.shape[1]
    sds = jax.ShapeDtypeStruct
    big = [sds((width, hidden), F32), sds((hidden, width), F32)] + [sds((width, width), F32)] * 8
    vectors = [sds((1, width), F32)] * 15 + [sds((1, hidden), F32)] * 3
    tail = [sds((buckets, heads), F32), sds((1, heads), F32)]
    whole = lambda a: pl.BlockSpec(a.shape, lambda t: (0,) * len(a.shape))
    steps = grads.shape[0] // width
    return pl.pallas_call(
        unpack_kernel,
        out_shape=big + vectors + tail,
        grid=(steps,),
        in_specs=[pl.BlockSpec((width, width), lambda t: (t, 0)), whole(small)],
        out_specs=[pl.BlockSpec(memory_space=pl.ANY)] * 10 + [whole(a) for a in vectors + tail],
        scratch_shapes=[pltpu.VMEM((4, width, width), F32), pltpu.SemaphoreType.DMA((4,))],
        name="unpack",
    )(grads, small)


def local(
    tokens, cotangent, target_lengths, task_mask, memory_lengths, position_buckets, memory,
    self_gain, self_shift, query_weight, query_bias, key_weight, value_weight, value_bias, position_table, head_scale,
    output_weight, output_bias, cross_gain, cross_shift, cross_query, cross_query_bias, cross_key, cross_value,
    cross_value_bias, post_gain, post_shift, cross_output, cross_output_bias, feed_gain, feed_shift, inner_weight,
    inner_bias, inner_gain, inner_shift, outer_weight, outer_bias,
):
    heads = head_scale.shape[0]
    bucket_count = position_table.shape[0]
    hidden = inner_weight.shape[1]
    table_t = jnp.pad(position_table.T, ((0, 0), (0, 512 - bucket_count)))
    row = lambda v: v.reshape(1, -1)
    vecs = [row(v) for v in (
        self_gain, self_shift, query_bias, value_bias, output_bias, output_bias, cross_gain, cross_shift,
        cross_query_bias, cross_value_bias, post_gain, post_shift, cross_output_bias, feed_gain, feed_shift, outer_bias,
    )]
    wides = [row(v) for v in (inner_bias, inner_gain, inner_shift)]
    sizes = {"dp": lax.axis_size("dp"), "rep": lax.axis_size("rep")}
    layer_output, dtok, memory_gradient, grads, small = whole_layer(
        sizes, target_lengths, memory_lengths, head_scale, tokens, cotangent, task_mask, position_buckets, table_t,
        memory, inner_weight, outer_weight, vecs, wides,
        [query_weight, key_weight, value_weight, output_weight, cross_query, cross_key, cross_value, cross_output],
    )
    outs = unpack(grads, small, hidden, heads, bucket_count)
    dw1, dw2, dwco, dwo, dwcq, dwck, dwcv, dwq, dwk, dwv = outs[:10]
    (
        d_self_gain, d_self_shift, d_query_bias, d_value_bias, d_output_bias, d_cross_gain, d_cross_shift,
        d_cross_query_bias, d_cross_value_bias, d_post_gain, d_post_shift, d_cross_output_bias, d_feed_gain,
        d_feed_shift, d_outer_bias, d_inner_bias, d_inner_gain, d_inner_shift,
    ) = [v.reshape(-1) for v in outs[10:28]]
    d_table, d_scale = outs[28], outs[29].reshape(-1)
    return (
        layer_output, dtok, memory_gradient,
        d_self_gain, d_self_shift, dwq, d_query_bias, dwk, dwv, d_value_bias, d_table, d_scale,
        dwo, d_output_bias, d_cross_gain, d_cross_shift, dwcq, d_cross_query_bias, dwck, dwcv, d_cross_value_bias,
        d_post_gain, d_post_shift, dwco, d_cross_output_bias, d_feed_gain, d_feed_shift, dw1, d_inner_bias,
        d_inner_gain, d_inner_shift, dw2, d_outer_bias,
    )


def solution(mesh):
    per_seq3, per_seq2, per_seq1 = P(("dp", "rep"), None, None), P(("dp", "rep"), None), P(("dp", "rep"))
    spread = P(None, "rep", "dp", None)
    in_specs = (per_seq3, per_seq3, per_seq1, per_seq2, per_seq1, P(), spread) + (P(),) * 30
    out_specs = (per_seq3, per_seq3, spread) + (P(),) * 30
    return jax.shard_map(local, mesh=mesh, in_specs=in_specs, out_specs=out_specs, check_vma=False)
```

```python
import functools

import jax
import jax.numpy as jnp
from jax import lax
from jax.experimental import pallas as pl
from jax.experimental.pallas import tpu as pltpu
from jax.sharding import PartitionSpec as P

NEG = -1e30
F32 = jnp.float32
BF16 = jnp.bfloat16
VMEM_LIMIT = 67043328

(
    SELF_GAIN,
    SELF_SHIFT,
    QUERY_BIAS,
    VALUE_BIAS,
    HEAD_SCALE,
    OUTPUT_BIAS,
    CROSS_GAIN,
    CROSS_SHIFT,
    CROSS_QUERY_BIAS,
    CROSS_VALUE_BIAS,
    POST_GAIN,
    POST_SHIFT,
    CROSS_OUTPUT_BIAS,
    FEED_GAIN,
    FEED_SHIFT,
    OUTER_BIAS,
) = range(16)


def mm(a, b):
    return jnp.dot(a, b, preferred_element_type=F32)


def mm_nt(a, b):
    return lax.dot_general(a, b, (((1,), (1,)), ((), ())), preferred_element_type=F32)


def mm_tn(a, b):
    return lax.dot_general(a, b, (((0,), (0,)), ((), ())), preferred_element_type=F32)


def normalize(x):
    center = x - jnp.mean(x, axis=-1, keepdims=True)
    spread = jnp.mean(center * center, axis=-1, keepdims=True)
    scale = lax.rsqrt(spread + 1e-05)
    return center * scale, scale


def norm_back(dy, hat, scale, gain):
    w = dy * gain
    first = jnp.mean(w, axis=-1, keepdims=True)
    second = jnp.mean(w * hat, axis=-1, keepdims=True)
    return (w - first - hat * second) * scale


def colsum(x):
    return jnp.sum(x, axis=0, keepdims=True)


def eight_rows(x):
    total = x[0:8]
    for k in range(8, x.shape[0], 8):
        total = total + x[k : k + 8]
    return total


def half_masks(rows):
    lane = lax.broadcasted_iota(jnp.int32, (rows, 128), 1)
    return (lane < 64, lane >= 64)


def pick(mask, x):
    return jnp.where(mask, x.astype(F32), 0.0).astype(BF16)


def pair_lanes(p):
    return pl.ds(pl.multiple_of(p * 128, 128), 128)


def head_rows(p, half):
    return pl.ds(pl.multiple_of(p * 128 + half * 64, 64), 64)


def fill_bias(buckets, table_rows, out_ref):
    length = buckets.shape[0]
    chunks = table_rows.shape[2] // 128
    low, high = buckets & 127, buckets >> 7
    key_place = lax.broadcasted_iota(jnp.int32, (length, 128), 0)
    lane = lax.broadcasted_iota(jnp.int32, (length, 128), 1)

    @pl.loop(0, out_ref.shape[0])
    def _(h):
        rows = [jnp.broadcast_to(table_rows[h, :, pl.ds(c * 128, 128)], (length, 128)) for c in range(chunks)]
        for tile in range(length // 128):
            cols, live = slice(tile * 128, (tile + 1) * 128), (tile + 1) * 128
            total = jnp.zeros((live, 128), F32)
            for c in range(chunks):
                got = jnp.take_along_axis(rows[c][:live], low[:live, cols], axis=1, mode="promise_in_bounds")
                total = jnp.where(high[:live, cols] == c, got, total)
            seen = jnp.where(key_place[:live] <= lane[:live] + tile * 128, total, NEG)
            out_ref[h, pl.ds(0, live), pl.ds(tile * 128, 128)] = seen
            if live < length:
                out_ref[h, pl.ds(live, length - live), pl.ds(tile * 128, 128)] = jnp.full((length - live, 128), NEG, F32)


def axis_bits(sizes):
    return [(axis, bit) for axis in ("rep", "dp") for bit in range(sizes[axis].bit_length() - 1)]


def stage_orders(sizes):
    plain = axis_bits(sizes)
    reps = sizes["rep"].bit_length() - 1
    swapped = list(plain)
    if reps >= 2 and len(plain) > reps:
        swapped = plain[: reps - 1] + [plain[reps], plain[reps - 1]] + plain[reps + 1 :]
    return plain, swapped


def flip(axis, bit):
    place = lax.axis_index(axis)
    return {axis: place + (1 - 2 * ((place // 2**bit) % 2)) * 2**bit}


def fold_sizes(rows, stages, tile):
    sizes, span = [], rows
    for _ in stages:
        span = span // 2 if span % (2 * tile) == 0 else span
        sizes.append(span)
    return sizes


class Reduction:
    def __init__(self, buf, start, rows, out, out_start, stages, tile, lands, send, recv, store):
        self.buf, self.out, self.tile, self.lands = buf, out, tile, lands
        self.send, self.recv, self.shift = send, recv, out_start - start
        folds, spreads = [], []
        base, span = start, rows
        for (axis, bit), size in zip(stages, fold_sizes(rows, stages, tile)):
            mine = (lax.axis_index(axis) // 2**bit) % 2
            peer = flip(axis, bit)
            halve = size < span
            keep = base + mine * size if halve else base
            give = base + (1 - mine) * size if halve else base
            folds.append((peer, give, keep, size))
            if halve:
                spreads.insert(0, (peer, keep, size))
            base, span = keep, size
        self.folds, self.spreads, self.own = folds, spreads, (base, span)
        self.store = pltpu.make_async_copy(self.part(buf, base, span), self.part(out, base + self.shift, span), store)

    def __len__(self):
        return len(self.folds) + len(self.spreads)

    def part(self, ref, start, size):
        return ref.at[pl.ds(start if isinstance(start, int) else pl.multiple_of(start, self.tile), size)]

    def copy(self, k):
        n = len(self.folds)
        if k < n:
            peer, give, keep, size = self.folds[k]
            land, at = self.lands[k]
            source, target = self.part(self.buf, give, size), land.at[pl.ds(at, size)]
        else:
            peer, base, size = self.spreads[k - n]
            target = self.part(self.out, base + self.shift, size)
            source = self.part(self.buf, base, size) if k == n else target
        return pltpu.make_async_remote_copy(
            src_ref=source, dst_ref=target, send_sem=self.send.at[k], recv_sem=self.recv.at[k],
            device_id=peer, device_id_type=pl.DeviceIdType.MESH,
        )

    def start(self, k):
        if k == len(self.folds):
            self.store.start()
        if k == min(len(self.folds) + 1, len(self)):
            self.store.wait()
        if k < len(self):
            self.copy(k).start()

    def finish(self, k):
        self.copy(k).wait()
        if k < len(self.folds):
            peer, give, keep, size = self.folds[k]
            land, at = self.lands[k]
            step = next(c for c in (128, 64, 48, 32, 16, 8) if size % c == 0)

            @pl.loop(0, size // step)
            def _(b):
                kept = pl.ds(pl.multiple_of(keep + b * step, self.tile), step)
                came = pl.ds(pl.multiple_of(at + b * step, self.tile), step)
                total = self.buf[kept, :].astype(F32) + land[came, :].astype(F32)
                self.buf[kept, :] = total.astype(self.buf.dtype)

    def advance(self, k):
        if 0 < k <= len(self):
            self.finish(k - 1)
        if k <= len(self):
            self.start(k)


def signal_all(sem, peers):
    for peer in peers:
        pl.semaphore_signal(sem, inc=1, device_id=peer, device_id_type=pl.DeviceIdType.MESH)


def scaled_heads(value_t, hs_ref):
    return jnp.concatenate([value_t[h * 64 : (h + 1) * 64] * hs_ref[h] for h in range(value_t.shape[0] // 64)], axis=0)


def self_forward(
    tlen, hs_ref, tok, bias_ref, vec_ref, wq, wk, wv, wo, q_ref, k_ref, v_ref, lse_ref, ot_ref, x1_ref, vt_ref
):
    length = tok.shape[0]
    x0 = tok.astype(F32)
    hat, _ = normalize(x0)
    h1 = (hat * vec_ref[SELF_GAIN][...] + vec_ref[SELF_SHIFT][...]).astype(BF16)
    q_ref[...] = ((mm(h1, wq[...]) + vec_ref[QUERY_BIAS][...]) * 0.125).astype(BF16)
    k_ref[...] = mm(h1, wk[...]).astype(BF16)
    value = (mm(h1, wv[...]) + vec_ref[VALUE_BIAS][...]).astype(BF16)
    v_ref[...] = value
    vt_ref[:, pl.ds(0, length)] = value.T
    key_place = lax.broadcasted_iota(jnp.int32, (length, length), 0)
    outside = jnp.where(key_place < tlen, 0.0, NEG)
    masks = half_masks(length)

    @pl.loop(0, q_ref.shape[1] // 128, unroll=4)
    def _(p):
        lanes = pair_lanes(p)
        kp, qp = k_ref[:, lanes], q_ref[:, lanes]
        for half in range(2):
            st = mm_nt(kp, pick(masks[half], qp)) + bias_ref[2 * p + half] + outside
            top = jnp.max(st, axis=0, keepdims=True)
            e = jnp.exp(st - top)
            total = colsum(e)
            ot = mm(vt_ref[head_rows(p, half), pl.ds(0, length)], e.astype(BF16))
            ot_ref[head_rows(p, half), :] = ot * (1.0 / total)
            lse_ref[2 * p + half] = top + jnp.log(total)

    c1 = scaled_heads(ot_ref[...], hs_ref).T.astype(BF16)
    x1_ref[...] = x0 + mm(c1, wo[...]) + vec_ref[OUTPUT_BIAS][...]


def cross_forward(mlen, mem_ref, vec_ref, x1, wcq, wck, wcv, q_ref, k_ref, v_ref, lse_ref, ot_ref, vt_ref, st_ref):
    length, mem_total = x1.shape[0], mem_ref.shape[0]
    hat, _ = normalize(x1)
    h2 = (hat * vec_ref[CROSS_GAIN][...] + vec_ref[CROSS_SHIFT][...]).astype(BF16)
    q_ref[...] = ((mm(h2, wcq[...]) + vec_ref[CROSS_QUERY_BIAS][...]) * 0.125).astype(BF16)
    step = 256

    @pl.loop(0, mem_total // step, unroll=4)
    def _(c):
        rows = pl.ds(pl.multiple_of(c * step, step), step)
        part = mem_ref[rows, :]
        k_ref[rows, :] = mm(part, wck[...]).astype(BF16)
        v_ref[rows, :] = (mm(part, wcv[...]) + vec_ref[CROSS_VALUE_BIAS][...]).astype(BF16)

    for c in range(mem_total // step):
        vt_ref[:, pl.ds(c * step, step)] = v_ref[pl.ds(c * step, step), :].T
    masks = half_masks(length)
    place = lax.broadcasted_iota(jnp.int32, (step, length), 0)
    tiles = length // 128

    @pl.loop(0, q_ref.shape[1] // 128, unroll=2)
    def _(p):
        lanes = pair_lanes(p)
        qp = q_ref[:, lanes]
        for half in range(2):
            qm = pick(masks[half], qp)
            top = jnp.full((1, length), -jnp.inf, F32)
            for c in range(mem_total // step):
                st = mm_nt(k_ref[pl.ds(c * step, step), lanes], qm)
                st = st + jnp.where(place < mlen - c * step, 0.0, NEG)
                for tile in range(tiles):
                    st_ref[tile, pl.ds(half * mem_total + c * step, step), :] = st[:, tile * 128 : (tile + 1) * 128]
                top = jnp.maximum(top, jnp.max(st, axis=0, keepdims=True))
            total = jnp.zeros((1, length), F32)
            ot = jnp.zeros((64, length), F32)
            for c in range(mem_total // step):
                rows = pl.ds(half * mem_total + c * step, step)
                st = jnp.concatenate([st_ref[tile, rows, :] for tile in range(tiles)], axis=1)
                e = jnp.exp(st - top)
                total = total + colsum(e)
                ot = ot + mm(vt_ref[head_rows(p, half), pl.ds(c * step, step)], e.astype(BF16))
            ot_ref[head_rows(p, half), :] = ot * (1.0 / total)
            lse_ref[2 * p + half] = top + jnp.log(total)


def feed_both(x2, g3, vec_ref, wide_ref, w1, w2, out_ref, acc, sums_ref, wide_sums_ref, u_ref, d_ref, df_ref, f_ref, r_ref, middle):
    length, hidden = u_ref.shape
    width = x2.shape[1]
    parts = hidden // width
    hat3, scale3 = normalize(x2)
    gain3 = vec_ref[FEED_GAIN][...]
    h3 = (hat3 * gain3 + vec_ref[FEED_SHIFT][...]).astype(BF16)
    cols = [pl.ds(c * width, width) for c in range(parts)]
    chunk = [pl.ds(c * length, length) for c in range(parts)]
    for c in range(parts):
        u_ref[:, cols[c]] = mm(h3, w1[cols[c], :])
    step = 64
    tiles = hidden // 128
    halves = d_ref.shape[0]

    def d_place(b, k):
        return k % halves, pl.ds(pl.multiple_of((k // halves) * length + b * step, step), step)

    @pl.loop(0, length // step)
    def _(b):
        rows = pl.ds(pl.multiple_of(b * step, step), step)
        u = u_ref[rows, :] + wide_ref[0][...]
        below = 0.5 * (1.0 + lax.erf(u * 0.7071067811865476))
        d = below + u * (jnp.exp(-0.5 * u * u) * 0.3989422804014327)
        for k in range(tiles):
            tile, place = d_place(b, k)
            d_ref[tile, place, :] = d[:, k * 128 : (k + 1) * 128]
        hat, scale = normalize(u * below)
        u_ref[rows, :] = hat
        f = (hat * wide_ref[1][...] + wide_ref[2][...]).astype(BF16)
        for c in range(parts):
            f_ref[pl.ds(pl.multiple_of(c * length + b * step, step), step), :] = f[:, c * width : (c + 1) * width]
        r_ref[rows, :] = jnp.broadcast_to(scale, (step, 128))

    x3 = x2 + vec_ref[OUTER_BIAS][...]
    for c in range(parts):
        x3 = x3 + mm(f_ref[chunk[c], :], w2[cols[c], :])
    out_ref[0] = x3.astype(BF16)
    sums_ref[0:1] += colsum(g3)
    e3 = g3.astype(BF16)
    for c in range(parts):
        acc[pl.ds(hidden + c * width, width), :] += mm_tn(f_ref[chunk[c], :], e3)
        df_ref[:, cols[c]] = mm_nt(e3, w2[cols[c], :])
    middle()

    @pl.loop(0, length // step)
    def _(b):
        rows = pl.ds(pl.multiple_of(b * step, step), step)
        dy, hat = df_ref[rows, :], u_ref[rows, :]
        part = dy * hat
        wide_sums_ref[0:8] += eight_rows(part)
        wide_sums_ref[8:16] += eight_rows(dy)
        da = norm_back(dy, hat, r_ref[rows, 0:1], wide_ref[1][...])
        pieces = []
        for k in range(tiles):
            tile, place = d_place(b, k)
            pieces.append(d_ref[tile, place, :])
        du = da * jnp.concatenate(pieces, axis=1)
        wide_sums_ref[16:24] += eight_rows(du)
        eu = du.astype(BF16)
        for c in range(parts):
            f_ref[pl.ds(pl.multiple_of(c * length + b * step, step), step), :] = eu[:, c * width : (c + 1) * width]

    dh3 = jnp.zeros(x2.shape, F32)
    h3t = h3.T
    for c in range(parts):
        acc[cols[c], :] += mm(h3t, f_ref[chunk[c], :])
        dh3 = dh3 + mm_nt(f_ref[chunk[c], :], w1[cols[c], :])
    sums_ref[1:2] += colsum(dh3 * hat3)
    sums_ref[2:3] += colsum(dh3)
    return g3 + norm_back(dh3, hat3, scale3, gain3)


def cross_backward(
    mlen, mem_ref, q_ref, k_ref, v_ref, lse_ref, delta_ref, do_ref, wck, wcv, dk_ref, dv_ref, dqt_ref, kt_ref,
    acc_key, acc_value, sums_ref, stage_ref, points,
):
    length, mem_total = q_ref.shape[0], mem_ref.shape[0]
    step = 256
    for c in range(mem_total // step):
        kt_ref[:, pl.ds(c * step, step)] = k_ref[pl.ds(c * step, step), :].T
    masks = half_masks(length)
    place = lax.broadcasted_iota(jnp.int32, (step, length), 0)
    pairs, chunks = q_ref.shape[1] // 128, mem_total // step

    @pl.loop(0, pairs)
    def _(p):
        @pl.when(p == pairs // 2)
        def _():
            points[0]()

        lanes = pair_lanes(p)
        qp, dop = q_ref[:, lanes], do_ref[:, lanes]
        qms = [pick(masks[half], qp) for half in range(2)]
        doms = [pick(masks[half], dop) for half in range(2)]
        lse = [lse_ref[2 * p + half] for half in range(2)]
        delta = [delta_ref[2 * p + half] for half in range(2)]
        for c in range(mem_total // step):
            rows = pl.ds(c * step, step)
            kp, vp = k_ref[rows, lanes], v_ref[rows, lanes]
            outside = jnp.where(place < mlen - c * step, 0.0, NEG)
            dv = jnp.zeros((step, 128), F32)
            dk = jnp.zeros((step, 128), F32)
            for half in range(2):
                st = mm_nt(kp, qms[half]) + outside
                pt = jnp.exp(st - lse[half])
                dpt = mm_nt(vp, doms[half])
                dst = (pt * (dpt - delta[half])).astype(BF16)
                stage_ref[:, pl.ds((half * chunks + c) * length, length)] = dst.astype(F32)
                dv = dv + mm(pt.astype(BF16), doms[half])
                dk = dk + mm(dst, qms[half])
            dv_ref[rows, lanes] = dv.astype(BF16)
            dk_ref[rows, lanes] = dk.astype(BF16)
        for half in range(2):
            staged = [stage_ref[:, pl.ds((half * chunks + c) * length, length)] for c in range(chunks)]
            dst = jnp.concatenate(staged, axis=0).astype(BF16)
            dqt_ref[head_rows(p, half), :] = mm(kt_ref[head_rows(p, half), :], dst)

    points[1]()
    acc_key[...] += mm_tn(mem_ref[...], dk_ref[...])
    acc_value[...] += mm_tn(mem_ref[...], dv_ref[...])

    @pl.loop(0, mem_total // step, unroll=4)
    def _(c):
        rows = pl.ds(pl.multiple_of(c * step, step), step)
        dk, dv = dk_ref[rows, :], dv_ref[rows, :]
        mem_ref[rows, :] = (mm_nt(dk, wck[...]) + mm_nt(dv, wcv[...])).astype(BF16)
        sums_ref[8:9] += colsum(dv.astype(F32))


def self_backward(tlen, bias_ref, q_ref, k_ref, v_ref, lse_ref, delta_ref, do_ref, dqt_ref, dk_ref, dv_ref, kt_ref, dbias_ref):
    length = q_ref.shape[0]
    kt_ref[:, pl.ds(0, length)] = k_ref[...].T
    key_place = lax.broadcasted_iota(jnp.int32, (length, length), 0)
    outside = jnp.where(key_place < tlen, 0.0, NEG)
    masks = half_masks(length)

    @pl.loop(0, q_ref.shape[1] // 128, unroll=4)
    def _(p):
        lanes = pair_lanes(p)
        qp, dop = q_ref[:, lanes], do_ref[:, lanes]
        kp, vp = k_ref[:, lanes], v_ref[:, lanes]
        dv = jnp.zeros((length, 128), F32)
        dk = jnp.zeros((length, 128), F32)
        for half in range(2):
            h = 2 * p + half
            qm, dom = pick(masks[half], qp), pick(masks[half], dop)
            st = mm_nt(kp, qm) + bias_ref[h] + outside
            pt = jnp.exp(st - lse_ref[h])
            dpt = mm_nt(vp, dom)
            dst = (pt * (dpt - delta_ref[h])).astype(BF16)
            rows = pl.ds(pl.multiple_of(h * length, length), length)
            wide_ds = dst.astype(F32)
            for tile in range(length // 128):
                dbias_ref[tile, rows, :] += wide_ds[:, tile * 128 : (tile + 1) * 128]
            dqt_ref[head_rows(p, half), :] = mm(kt_ref[head_rows(p, half), pl.ds(0, length)], dst)
            dv = dv + mm(pt.astype(BF16), dom)
            dk = dk + mm(dst, qm)
        dv_ref[:, lanes] = dv.astype(BF16)
        dk_ref[:, lanes] = dk.astype(BF16)


def bucket_totals(buckets_t, dbias_ref, out_ref, between):
    length = buckets_t.shape[0]
    heads = dbias_ref.shape[1] // length
    lo_places = lax.broadcasted_iota(jnp.int32, (32, 128), 0)
    group = 8

    def block(start, tiles, acc):
        rows = buckets_t[pl.ds(start, group), :]
        lefts, rights = [], []
        for k in range(group):
            for tile in tiles:
                ids = rows[k : k + 1, tile * 128 : (tile + 1) * 128]
                d = dbias_ref[tile, pl.ds(start + k, heads, stride=length), :]
                high = jnp.broadcast_to(ids >> 5, (heads, 128))
                lefts.append(jnp.concatenate([jnp.where(high == g, d, 0.0) for g in range(16)], axis=0).astype(BF16))
                rights.append(jnp.where(lo_places == (ids & 31), 1.0, 0.0).astype(BF16))
        return acc + mm_nt(jnp.concatenate(lefts, axis=1), jnp.concatenate(rights, axis=1))

    acc = jnp.zeros((16 * heads, 32), F32)
    tiles = length // 128
    for band in range(tiles):
        if band:
            between()
        live = range(band, tiles)

        def body(b, acc):
            return block(pl.multiple_of(band * 128 + b * group, group), live, acc)

        acc = lax.fori_loop(0, 128 // group, body, acc)
    for g in range(16):
        out_ref[:, g * 32 : (g + 1) * 32] = acc[g * heads : (g + 1) * heads]


SMALL_ROWS = 64
SUMS_B = 24
HEAD_ROWS = 40
TABLE_ROWS = 48


def piece_order(places):
    far, near = list(range(max(places // 2, 1), places)), list(range(1, places // 2))
    order = []
    for k in range(len(far)):
        order.append(far[k])
        if k < len(near):
            order.append(near[k])
    return order


def partner(me, places, k):
    if places & (places - 1):
        return lax.rem(me + k, places)
    for bit in range(places.bit_length() - 1):
        if (k >> bit) & 1:
            me = me + (1 - 2 * ((me // 2**bit) % 2)) * 2**bit
    return me


def layer_kernel(sizes, layout, tlen_ref, mlen_ref, hs_ref, tok_ref, cot_ref, mask_ref, buckets_ref, table_ref, *rest):
    mem_hbm, w1_hbm, w2_hbm = rest[:3]
    vec_ref, wide_ref = rest[3:19], rest[19:22]
    wq, wk, wv, wo, wcq, wck, wcv, wco = rest[22:30]
    out_ref, dtok_ref, dmem_hbm, grads_hbm, small_hbm = rest[30:35]
    (
        mem_scr, w1s, w2s, acc, bias_ref, st_scr,
        q1_scr, k1_scr, v1_scr, lse1_scr, ot1_scr, x1_scr,
        kv_scr, q2_scr, do_scr, lse2_scr, delta_scr,
        vt_scr, ot_scr, u_scr, df_scr, r_scr, dk_scr, dv_scr,
        grads, land, small, small_land, wide_scr, hs_scr, table_scr, buckets_t_scr,
        load_sem, send_sem, recv_sem, own_sem, back_send, back_recv, back_own, group_send, group_recv, store_sem, ready_sem, late_sem,
    ) = rest[35:]
    seqs, mem_total, width = mem_scr.shape
    length, hidden, heads = tok_ref.shape[1], u_scr.shape[1], bias_ref.shape[0]
    places, piece = mem_hbm.shape[0], mem_hbm.shape[2]
    t = pl.program_id(0)
    me = lax.axis_index("dp")
    mine = pl.ds(pl.multiple_of(me * piece, piece), piece)
    k2_scr, v2_scr = kv_scr.at[pl.ds(0, mem_total)], kv_scr.at[pl.ds(mem_total, mem_total)]
    sums_a, sums_b = small.at[pl.ds(0, 8)], small.at[pl.ds(SUMS_B, 24)]
    base = 2 * hidden
    acc_at = lambda k: acc.at[pl.ds(base + k * width, width)]
    CROSS_OUT, OUT, QUERY, KEY, VALUE = range(5)
    order = piece_order(places)

    def own_in(s):
        return pltpu.make_async_copy(mem_hbm.at[me, s], mem_scr.at[s, mine], own_sem.at[s])

    def own_back(s):
        return pltpu.make_async_copy(mem_scr.at[s, mine], dmem_hbm.at[me, s], back_own.at[s])

    def loads():
        copies = []
        for c in range(hidden // width):
            cols = pl.ds(c * width, width)
            copies.append(pltpu.make_async_copy(w1_hbm.at[:, cols], w1s.at[cols], load_sem.at[c]))
        copies.append(pltpu.make_async_copy(w2_hbm, w2s, load_sem.at[hidden // width]))
        return copies

    def remote(source, target, send, recv, peer):
        return pltpu.make_async_remote_copy(
            src_ref=source, dst_ref=target, send_sem=send, recv_sem=recv, device_id={"dp": peer},
            device_id_type=pl.DeviceIdType.MESH,
        )

    def send_in(s, k):
        peer = partner(me, places, k)
        remote(mem_hbm.at[peer, s], mem_scr.at[s, mine], send_sem.at[s], recv_sem.at[s], peer).start()

    def send_back(s, k):
        peer = partner(me, places, k)
        rows = pl.ds(pl.multiple_of(peer * piece, piece), piece)
        remote(mem_scr.at[s, rows], dmem_hbm.at[me, s], back_send.at[s], back_recv.at[s], peer).start()

    def all_in(s):
        some = mem_scr.at[s, pl.ds(0, (places - 1) * piece)]
        return remote(some, some, send_sem.at[s], recv_sem.at[s], partner(me, places, 1))

    def all_back(s):
        some = dmem_hbm.at[pl.ds(0, places - 1), s]
        return remote(some, some, back_send.at[s], back_recv.at[s], partner(me, places, 1))

    plain, swapped = stage_orders(sizes)
    spare = pl.ds(length, mem_total - length)
    pools = {"first": w2s, "second": w1s, "key": dk_scr.at[spare], "value": dv_scr.at[spare], "land": land}
    buffers = {"grads": grads, "kv": kv_scr}
    reductions = []
    for r, (buf, start, rows, out_start, lands, color) in enumerate(layout):
        reductions.append(Reduction(
            buffers[buf], start, rows, grads_hbm, out_start, swapped if color == 1 else plain, 16,
            [(pools[name], at) for name, at in lands], group_send.at[r], group_recv.at[r], store_sem.at[r],
        ))
    last = len(layout)
    at, lands = 0, []
    for size in fold_sizes(SMALL_ROWS, plain, 8):
        lands.append((small_land, at))
        at += size
    reductions.append(Reduction(
        small, 0, SMALL_ROWS, small_hbm, 0, plain, 8, lands, group_send.at[last], group_recv.at[last], store_sem.at[last],
    ))
    first = [r for r, item in enumerate(layout) if item[0] == "grads" and item[1] < base]
    second = [r for r, item in enumerate(layout) if item[0] == "grads" and item[1] >= base]
    third = [r for r, item in enumerate(layout) if item[0] == "kv"]
    flips = [flip(axis, bit) for axis, bit in plain]

    steps = 4 * seqs
    begin_first, begin_second = 3 * (3 * seqs - 1), 3 * 3 * seqs
    planned = len(plain) == 5 and places == 8 and seqs == 4
    acts = {p: [] for p in range(3 * steps)}
    sends = {p: [] for p in range(3 * steps)}
    moved = [0] * len(reductions)
    queue = [(s, k) for s in range(seqs) for k in order]
    for p in range(3 * seqs, 3 * steps):
        if planned:
            count = SENDS[p - 3 * seqs]
        else:
            count = -(-len(order) * 2 // 7)
        while count and queue and p >= 3 * (seqs + 2 * queue[0][0] + 2):
            sends[p].append(queue.pop(0))
            count -= 1
        for r in ACTS[p - 3 * seqs] if planned else ():
            acts[p].append((r, moved[r]))
            moved[r] += 1

    def point(part, low, high):
        for step in range(low, high):
            p = 3 * step + part
            if acts[p] or sends[p] or (p == begin_first and flips):

                @pl.when(t == step)
                def _():
                    if p == begin_first and flips:
                        pl.semaphore_wait(ready_sem, len(flips))
                    for r, k in acts[p]:
                        reductions[r].advance(k)
                    for s, k in sends[p]:
                        send_back(s, k)

    @pl.when(t == 0)
    def _():
        bucket_load = pltpu.make_async_copy(buckets_ref, buckets_t_scr, load_sem.at[hidden // width + 1])
        bucket_load.start()
        for s in range(seqs):
            own_in(s).start()
        peers = [{"dp": partner(me, places, k)} for k in range(1, places)]
        peers += [flip(axis, bit) for axis, bit in plain if axis == "rep"]
        if peers:
            barrier = pltpu.get_barrier_semaphore()
            signal_all(barrier, peers)
            pl.semaphore_wait(barrier, len(peers))
        for s in range(seqs):
            for k in order:
                send_in(s, k)
        for c in loads():
            c.start()
        for ref in (acc, small, wide_scr, hs_scr):
            ref[...] = jnp.zeros_like(ref)
        for h in range(heads):
            table_scr[h] = jnp.zeros(table_scr.shape[1:], F32)
            table_scr[h, :, : table_ref.shape[1]] = table_ref[h : h + 1, :]
        bucket_load.wait()
        buckets_t_scr[...] = buckets_t_scr[...].T
        fill_bias(buckets_t_scr[...], table_scr, bias_ref)

    @pl.when(t < seqs)
    def _():
        self_forward(
            tlen_ref[t], hs_ref, tok_ref[0], bias_ref, vec_ref, wq, wk, wv, wo,
            q1_scr.at[t], k1_scr.at[t], v1_scr.at[t], lse1_scr.at[t], ot1_scr.at[t], x1_scr.at[t], vt_scr,
        )

    @pl.when(t == seqs)
    def _():
        for c in loads():
            c.wait()

    inner = t - seqs
    s = inner // 2

    @pl.when((t >= seqs) & (t < 3 * seqs) & (inner % 2 == 0))
    def _():
        own_in(s).wait()
        if places > 1:
            all_in(s).wait_recv()
        point(0, seqs, 3 * seqs)
        x1 = x1_scr[s]
        cross_forward(
            mlen_ref[s], mem_scr.at[s], vec_ref, x1, wcq, wck, wcv,
            q2_scr, k2_scr, v2_scr, lse2_scr, ot_scr, vt_scr, st_scr,
        )
        point(1, seqs, 3 * seqs)
        hat, scale = normalize(ot_scr[...].T)
        gain = vec_ref[POST_GAIN][...]
        c2 = (hat * gain + vec_ref[POST_SHIFT][...]).astype(BF16)
        x2 = x1 + mm(c2, wco[...]) + vec_ref[CROSS_OUTPUT_BIAS][...]
        here = lax.broadcasted_iota(jnp.int32, mask_ref.shape, 0) == s
        row = jnp.sum(jnp.where(here, mask_ref[...], 0), axis=0, keepdims=True).astype(F32)
        row = jnp.where(lax.broadcasted_iota(jnp.int32, (1, length), 1) < tlen_ref[s], row, 0.0)
        g3 = cot_ref[0].astype(F32) * jnp.broadcast_to(row, (8, length)).T[:, 0:1]
        g2 = feed_both(
            x2, g3, vec_ref, wide_ref, w1s, w2s, out_ref, acc, sums_a, wide_scr,
            u_scr, st_scr, df_scr, dk_scr, r_scr, lambda: point(2, seqs, 3 * seqs),
        )
        df_scr[:, pl.ds(0, width)] = g2
        sums_a[3:4] += colsum(g2)
        e2 = g2.astype(BF16)
        acc_at(CROSS_OUT)[...] += mm_tn(c2, e2)
        dc2 = mm_nt(e2, wco[...])
        sums_a[4:5] += colsum(dc2 * hat)
        sums_a[5:6] += colsum(dc2)
        do2 = norm_back(dc2, hat, scale, gain).astype(BF16)
        do_scr[...] = do2
        prod = do2.astype(F32).T * ot_scr[...]
        for h in range(heads):
            delta_scr[h] = colsum(prod[h * 64 : (h + 1) * 64])

    @pl.when(t == 3 * seqs - 2)
    def _():
        signal_all(ready_sem, flips)
        for k in range(3):
            total = colsum(wide_scr[8 * k : 8 * k + 8])
            for c in range(hidden // width):
                row = 8 + k * (hidden // width) + c
                small[row : row + 1] = total[:, c * width : (c + 1) * width]

        @pl.loop(0, base // 256)
        def _(b):
            rows = pl.ds(pl.multiple_of(b * 256, 256), 256)
            grads[rows, :] = acc[rows, :].astype(BF16)

    @pl.when((t >= seqs) & (t < 3 * seqs) & (inner % 2 == 1))
    def _():
        point(0, seqs, 3 * seqs)
        cross_backward(
            mlen_ref[s], mem_scr.at[s], q2_scr, k2_scr, v2_scr, lse2_scr, delta_scr, do_scr, wck, wcv,
            dk_scr, dv_scr, ot_scr, vt_scr, acc_at(KEY), acc_at(VALUE), sums_b, u_scr,
            [lambda: point(1, seqs, 3 * seqs), lambda: point(2, seqs, 3 * seqs)],
        )
        own_back(s).start()
        dq2 = (ot_scr[...].T.astype(BF16).astype(F32) * 0.125).astype(BF16)
        hat2, scale2 = normalize(x1_scr[s])
        gain2 = vec_ref[CROSS_GAIN][...]
        h2 = (hat2 * gain2 + vec_ref[CROSS_SHIFT][...]).astype(BF16)
        acc_at(QUERY)[...] += mm_tn(h2, dq2)
        sums_b[7:8] += colsum(dq2.astype(F32))
        dh2 = mm_nt(dq2, wcq[...])
        sums_b[5:6] += colsum(dh2 * hat2)
        sums_b[6:7] += colsum(dh2)
        g1 = df_scr[:, pl.ds(0, width)] + norm_back(dh2, hat2, scale2, gain2)
        x1_scr[s] = g1
        sums_b[4:5] += colsum(g1)
        c1t = scaled_heads(ot1_scr[s], hs_ref).astype(BF16)
        acc_at(OUT)[...] += mm(c1t, g1.astype(BF16))

    @pl.when(t == 3 * seqs - 1)
    def _():
        @pl.loop(0, 5 * width // 256)
        def _(b):
            rows = pl.ds(pl.multiple_of(base + b * 256, 256), 256)
            grads[rows, :] = acc[rows, :].astype(BF16)

        signal_all(late_sem, flips)
        st_scr[...] = jnp.zeros_like(st_scr)
        acc[pl.ds(0, 3 * width), :] = jnp.zeros((3 * width, width), F32)

    @pl.when(t >= 3 * seqs)
    def _():
        point(0, 3 * seqs, steps)
        s = t - 3 * seqs
        g1 = x1_scr[s]
        dc1t = mm_nt(g1.astype(BF16), wo[...]).T
        do1t = scaled_heads(dc1t, hs_ref).astype(BF16)
        do_scr[...] = do1t.T
        for h in range(heads):
            rows = slice(h * 64, (h + 1) * 64)
            o = ot1_scr[s, rows, :]
            hs_scr[h : h + 1, :] += colsum(o * dc1t[rows])
            delta_scr[h] = colsum(o * do1t[rows].astype(F32))
        dk_ref, dv_ref = dk_scr.at[pl.ds(0, length)], dv_scr.at[pl.ds(0, length)]
        self_backward(
            tlen_ref[s], bias_ref, q1_scr.at[s], k1_scr.at[s], v1_scr.at[s], lse1_scr.at[s], delta_scr, do_scr,
            ot_scr, dk_ref, dv_ref, vt_scr, st_scr,
        )
        point(1, 3 * seqs, steps)
        dq1 = (ot_scr[...].T.astype(BF16).astype(F32) * 0.125).astype(BF16)
        dk1, dv1 = dk_ref[...], dv_ref[...]
        hat1, scale1 = normalize(tok_ref[0].astype(F32))
        gain1 = vec_ref[SELF_GAIN][...]
        h1t = (hat1 * gain1 + vec_ref[SELF_SHIFT][...]).astype(BF16).T
        for k, d in enumerate((dq1, dk1, dv1)):
            acc[pl.ds(k * width, width), :] += mm(h1t, d)
        point(2, 3 * seqs, steps)
        sums_b[2:3] += colsum(dq1.astype(F32))
        sums_b[3:4] += colsum(dv1.astype(F32))
        dh1 = mm_nt(dq1, wq[...]) + mm_nt(dk1, wk[...]) + mm_nt(dv1, wv[...])
        sums_b[0:1] += colsum(dh1 * hat1)
        sums_b[1:2] += colsum(dh1)
        dtok_ref[0] = (g1 + norm_back(dh1, hat1, scale1, gain1)).astype(BF16)

    @pl.when(t == steps - 1)
    def _():
        @pl.loop(0, 3 * width // 256)
        def _(b):
            rows = pl.ds(pl.multiple_of(b * 256, 256), 256)
            kv_scr[rows, :] = acc[rows, :].astype(BF16)

        small[HEAD_ROWS : HEAD_ROWS + heads] = jnp.broadcast_to(
            jnp.sum(hs_scr[...], axis=1, keepdims=True), (heads, width)
        )
        def move(r):
            if r < 0:
                if queue:
                    send_back(*queue.pop(0))
            elif moved[r] <= len(reductions[r]):
                reductions[r].advance(moved[r])
                moved[r] += 1

        if flips:
            pl.semaphore_wait(late_sem, len(flips))
        for r in third:
            move(r)

        def between():
            for r in BETWEEN if planned else first + second + third:
                move(r)

        bucket_totals(buckets_t_scr, st_scr, small.at[pl.ds(TABLE_ROWS, heads)], between)
        for r in TAIL if planned else ():
            move(r)
        left = third + [last] + second + first
        while any(moved[r] <= len(reductions[r]) for r in left):
            for r in left:
                move(r)
            move(-1)
        while queue:
            move(-1)
        for s in range(seqs):
            own_back(s).wait()
            if places > 1:
                all_in(s).wait_send()
                all_back(s).wait_send()
                all_back(s).wait_recv()


ACTS = (
    (),
    (),
    (),
    (),
    (),
    (),
    (),
    (),
    (),
    (),
    (),
    (),
    (),
    (),
    (),
    (),
    (),
    (),
    (),
    (),
    (),
    (0, 1, 2, 3),
    (0,),
    (1, 2, 3),
    (4, 5, 6, 7),
    (0, 4, 5, 6),
    (1, 7, 2),
    (),
    (0, 3),
    (),
    (),
    (0, 4, 2),
    (5, 3),
    (6,),
    (2, 1, 3, 0, 4),
    (5, 7),
)
SENDS = (0, 0, 0, 0, 0, 0, 0, 0, 0, 0, 0, 0, 0, 0, 0, 1, 0, 2, 2, 2, 1, 0, 2, 2, 0, 2, 0, 1, 0, 2, 0, 0, 2, 0, 0, 2)
BETWEEN = (0, 1, 2, 3, 4, 5, 6, 7, 8, 9, 10)
TAIL = (11, 11, 8, 10, 0, 1, 11, 9, 2, 3, 8, -1, 10, 4, 6, 5, 7, 9, 1, 0, 2, 11, 3, 8, 2, 10, 4, -1, -1, 6, 0, 3, 5, 9, 7, 1, 11, 0, 8, 10, 4, 2, 2, 5, 6, 4, -1, -1, 9, 7, 11, 3, 8, 6, 5, 10, 3, 1, 11, 6, -1, -1, 7, 9, 8, 4, 10, 1, 4, 5, 11, 1, 5, 11, 6, 9, 8, 6, 7, 9, 10, 8, 7, 8, 7, 9, 10, 9, 10)
MEMBERS = (('first', 0, 2), ('first', 1, 2), ('first', 0, 2), ('first', 0, 2), ('second', 0, 2), ('second', 0, 1), ('second', 0, 1), ('second', 0, 1), ('third', 1, 1), ('third', 1, 1), ('third', 0, 1))


def reduction_layout(sizes, width, hidden, spare):
    plain, _ = stage_orders(sizes)
    base = 2 * hidden
    members, at = [], {"first": 0, "second": 2 * hidden, "third": 0}
    for name, color, units in MEMBERS:
        rows = units * width
        out_start = at[name] + (base + 5 * width if name == "third" else 0)
        members.append(("kv" if name == "third" else "grads", at[name], rows, out_start, color))
        at[name] += rows
    used = {"first": 0, "second": 0, "key": 0, "value": 0, "land": 0}
    layout = []
    for buf, start, rows, out_start, color in members:
        lands = []
        for size in fold_sizes(rows, plain, 16):
            room = {"first": hidden, "second": hidden} if buf == "grads" else {"key": spare, "value": spare}
            name = next((n for n in room if used[n] + size <= room[n]), "land")
            lands.append((name, used[name]))
            used[name] += size
        layout.append((buf, start, rows, out_start, lands, color))
    return layout, max(used["land"], 16)


def whole_layer(sizes, tlen, mlen, head_scale, tokens, cotangent, mask, buckets, table, memory, w1, w2, vecs, wides, weights):
    seqs, length, width = tokens.shape
    places, _, piece, _ = memory.shape
    mem_total = places * piece
    heads, hidden = head_scale.shape[0], w1.shape[1]
    layout, land = reduction_layout(sizes, width, hidden, mem_total - length)
    plain, _ = stage_orders(sizes)
    small_land = max(sum(fold_sizes(SMALL_ROWS, plain, 8)), 8)
    slots = max(2 * len(plain), 1)
    several = places > 1 or sizes["rep"] > 1
    sds = jax.ShapeDtypeStruct
    anywhere = pl.BlockSpec(memory_space=pl.ANY)
    const = lambda a: pl.BlockSpec(a.shape, lambda t, *_: (0,) * a.ndim, pipeline_mode=pl.Buffered(1))
    seq = lambda idx: pl.BlockSpec((1, length, width), lambda t, *_: (idx(t), 0, 0))
    ends = lambda t: jnp.where(t < 3 * seqs, jnp.minimum(t, seqs - 1), t - 3 * seqs)
    middle = lambda t: jnp.clip((t - seqs) // 2, 0, seqs - 1)
    late = lambda t: jnp.maximum(t - 3 * seqs, 0)
    tall = heads * length
    scratch = [
        ((seqs, mem_total, width), BF16), ((hidden, width), BF16), ((hidden, width), BF16),
        ((2 * hidden + 5 * width, width), F32), ((heads, length, length), F32),
        ((length // 128, max(tall, 2 * mem_total, hidden * length * 128 // (length * 128)), 128), F32),
        ((seqs, length, width), BF16), ((seqs, length, width), BF16), ((seqs, length, width), BF16),
        ((seqs, heads, 1, length), F32), ((seqs, width, length), F32), ((seqs, length, width), F32),
        ((2 * mem_total, width), BF16), ((length, width), BF16), ((length, width), BF16),
        ((heads, 1, length), F32), ((heads, 1, length), F32),
        ((width, mem_total), BF16), ((width, length), F32), ((length, hidden), F32), ((length, hidden), F32),
        ((length, 128), F32), ((max(mem_total, hidden // width * length), width), BF16), ((mem_total, width), BF16),
        ((2 * hidden + 5 * width, width), BF16), ((land, width), BF16), ((SMALL_ROWS, width), F32), ((small_land, width), F32),
        ((24, hidden), F32), ((heads, length), F32), ((heads, 1, 512), F32), ((length, length), jnp.int32),
    ]
    dma = pltpu.SemaphoreType.DMA
    groups = len(layout) + 1
    return pl.pallas_call(
        functools.partial(layer_kernel, sizes, layout),
        out_shape=[
            sds(tokens.shape, BF16), sds(tokens.shape, BF16), sds(memory.shape, BF16),
            sds((2 * hidden + 8 * width, width), BF16), sds((SMALL_ROWS, width), F32),
        ],
        grid_spec=pltpu.PrefetchScalarGridSpec(
            num_scalar_prefetch=3,
            grid=(4 * seqs,),
            in_specs=[seq(ends), seq(middle), const(mask), anywhere, const(table), anywhere, anywhere, anywhere]
            + [const(a) for a in vecs + wides + weights],
            out_specs=[seq(middle), seq(late), anywhere, anywhere, anywhere],
            scratch_shapes=[pltpu.VMEM(shape, dtype) for shape, dtype in scratch] + [
                dma((hidden // width + 2,)), dma((seqs,)), dma((seqs,)), dma((seqs,)), dma((seqs,)), dma((seqs,)),
                dma((seqs,)), dma((groups, slots)), dma((groups, slots)), dma((groups,)), pltpu.SemaphoreType.REGULAR, pltpu.SemaphoreType.REGULAR,
            ],
        ),
        compiler_params=pltpu.CompilerParams(
            vmem_limit_bytes=VMEM_LIMIT, collective_id=0 if several else None, has_side_effects=True
        ),
        name="layer",
    )(tlen, mlen, head_scale, tokens, cotangent, mask, buckets, table, memory, w1, w2, *vecs, *wides, *weights)


def unpack_kernel(count, grads_hbm, small_ref, *refs):
    kept, refs = refs[:count], refs[count:]
    passed, refs = refs[:count], refs[count:]
    big, vectors, tail = refs[:10], refs[10:28], refs[28:]
    table_ref, scale_ref, rough, exact = tail[:4]
    holds, (in_sem, out_sem, hold_in, hold_out) = tail[4:-4], tail[-4:]
    dw1, dw2, rest = big[0], big[1], big[2:]
    width = grads_hbm.shape[1]
    parts = dw1.shape[1] // width
    targets = [dw1.at[:, pl.ds(c * width, width)] for c in range(parts)]
    targets += [dw2.at[pl.ds(c * width, width)] for c in range(parts)] + list(rest)
    rows = [pl.ds(k * width, width) for k in range(len(targets))]
    into = [pltpu.make_async_copy(grads_hbm.at[r], rough.at[r], in_sem.at[k]) for k, r in enumerate(rows)]
    out = [pltpu.make_async_copy(exact.at[r], target, out_sem.at[k]) for k, (r, target) in enumerate(zip(rows, targets))]
    take = [pltpu.make_async_copy(a, hold, hold_in.at[k]) for k, (a, hold) in enumerate(zip(kept, holds))]
    give = [pltpu.make_async_copy(hold, a, hold_out.at[k]) for k, (a, hold) in enumerate(zip(passed, holds))]
    for c in into + take:
        c.start()
    for row, ref in zip(VECTOR_ROWS, vectors):
        for c in range(ref.shape[1] // width):
            ref[:, c * width : (c + 1) * width] = small_ref[row + c : row + c + 1]
    heads = scale_ref.shape[1]
    table_ref[...] = small_ref[TABLE_ROWS : TABLE_ROWS + heads, : table_ref.shape[1]]
    block = small_ref[HEAD_ROWS : HEAD_ROWS + heads]
    diagonal = lax.broadcasted_iota(jnp.int32, block.shape, 0) == lax.broadcasted_iota(jnp.int32, block.shape, 1)
    scale_ref[...] = colsum(jnp.where(diagonal, block, 0.0))[:, :heads]
    step = 64
    for k in range(len(targets)):
        into[k].wait()

        @pl.loop(0, width // step)
        def _(b):
            part = pl.ds(pl.multiple_of(k * width + b * step, step), step)
            exact[part, :] = rough[part, :].astype(F32)

        out[k].start()
    for a, b in zip(take, give):
        a.wait()
        b.start()
    for c in out + give:
        c.wait()


VECTOR_ROWS = (24, 25, 26, 27, 28, 29, 30, 31, 32, 4, 5, 3, 1, 2, 0, 16, 8, 12)


def unpack(grads, small, kept, hidden, heads, buckets):
    total, width = grads.shape
    sds = jax.ShapeDtypeStruct
    big = [sds((width, hidden), F32), sds((hidden, width), F32)] + [sds((width, width), F32)] * 8
    vectors = [sds((1, width), F32)] * 15 + [sds((1, hidden), F32)] * 3
    tail = [sds((heads, buckets), F32), sds((1, heads), F32)]
    anywhere, inside = pl.BlockSpec(memory_space=pl.ANY), pl.BlockSpec(memory_space=pltpu.VMEM)
    dma = pltpu.SemaphoreType.DMA
    count = len(kept)
    outs = pl.pallas_call(
        functools.partial(unpack_kernel, count),
        out_shape=[sds(a.shape, a.dtype) for a in kept] + big + vectors + tail,
        in_specs=[anywhere, inside] + [anywhere] * count,
        out_specs=[anywhere] * (count + 10) + [inside] * (len(vectors) + len(tail)),
        scratch_shapes=[pltpu.VMEM((total, width), BF16), pltpu.VMEM((total, width), F32)]
        + [pltpu.VMEM(a.shape, a.dtype) for a in kept]
        + [dma((total // width,)), dma((total // width,)), dma((count,)), dma((count,))],
        compiler_params=pltpu.CompilerParams(vmem_limit_bytes=VMEM_LIMIT),
        name="unpack",
    )(grads, small, *kept)
    return outs[:count], outs[count:]


def local(
    tokens, cotangent, target_lengths, task_mask, memory_lengths, position_buckets, memory,
    self_gain, self_shift, query_weight, query_bias, key_weight, value_weight, value_bias, position_table, head_scale,
    output_weight, output_bias, cross_gain, cross_shift, cross_query, cross_query_bias, cross_key, cross_value,
    cross_value_bias, post_gain, post_shift, cross_output, cross_output_bias, feed_gain, feed_shift, inner_weight,
    inner_bias, inner_gain, inner_shift, outer_weight, outer_bias,
):
    heads = head_scale.shape[0]
    bucket_count = position_table.shape[0]
    hidden = inner_weight.shape[1]
    table_t = position_table.T
    row = lambda v: v.reshape(1, -1)
    vecs = [row(v) for v in (
        self_gain, self_shift, query_bias, value_bias, output_bias, output_bias, cross_gain, cross_shift,
        cross_query_bias, cross_value_bias, post_gain, post_shift, cross_output_bias, feed_gain, feed_shift, outer_bias,
    )]
    wides = [row(v) for v in (inner_bias, inner_gain, inner_shift)]
    sizes = {"dp": lax.axis_size("dp"), "rep": lax.axis_size("rep")}
    layer_output, dtok, memory_gradient, grads, small = whole_layer(
        sizes, target_lengths, memory_lengths, head_scale, tokens, cotangent, task_mask, position_buckets, table_t,
        memory, inner_weight, outer_weight, vecs, wides,
        [query_weight, key_weight, value_weight, output_weight, cross_query, cross_key, cross_value, cross_output],
    )
    (layer_output, dtok, memory_gradient), outs = unpack(
        grads, small, [layer_output, dtok, memory_gradient], hidden, heads, bucket_count
    )
    dw1, dw2, dwco, dwo, dwcq, dwck, dwcv, dwq, dwk, dwv = outs[:10]
    (
        d_self_gain, d_self_shift, d_query_bias, d_value_bias, d_output_bias, d_cross_gain, d_cross_shift,
        d_cross_query_bias, d_cross_value_bias, d_post_gain, d_post_shift, d_cross_output_bias, d_feed_gain,
        d_feed_shift, d_outer_bias, d_inner_bias, d_inner_gain, d_inner_shift,
    ) = [v.reshape(-1) for v in outs[10:28]]
    d_table, d_scale = outs[28].T, outs[29].reshape(-1)
    return (
        layer_output, dtok, memory_gradient,
        d_self_gain, d_self_shift, dwq, d_query_bias, dwk, dwv, d_value_bias, d_table, d_scale,
        dwo, d_output_bias, d_cross_gain, d_cross_shift, dwcq, d_cross_query_bias, dwck, dwcv, d_cross_value_bias,
        d_post_gain, d_post_shift, dwco, d_cross_output_bias, d_feed_gain, d_feed_shift, dw1, d_inner_bias,
        d_inner_gain, d_inner_shift, dw2, d_outer_bias,
    )


def solution(mesh):
    per_seq3, per_seq2, per_seq1 = P(("dp", "rep"), None, None), P(("dp", "rep"), None), P(("dp", "rep"))
    spread = P(None, "rep", "dp", None)
    in_specs = (per_seq3, per_seq3, per_seq1, per_seq2, per_seq1, P(), spread) + (P(),) * 30
    out_specs = (per_seq3, per_seq3, spread) + (P(),) * 30
    return jax.shard_map(local, mesh=mesh, in_specs=in_specs, out_specs=out_specs, check_vma=False)
```

```python
import functools

import jax
import jax.numpy as jnp
from jax import lax
from jax.experimental import pallas as pl
from jax.experimental.pallas import tpu as pltpu
from jax.sharding import PartitionSpec as P

NEG = -1e30
F32 = jnp.float32
BF16 = jnp.bfloat16
VMEM_LIMIT = 67043328

(
    SELF_GAIN,
    SELF_SHIFT,
    QUERY_BIAS,
    VALUE_BIAS,
    HEAD_SCALE,
    OUTPUT_BIAS,
    CROSS_GAIN,
    CROSS_SHIFT,
    CROSS_QUERY_BIAS,
    CROSS_VALUE_BIAS,
    POST_GAIN,
    POST_SHIFT,
    CROSS_OUTPUT_BIAS,
    FEED_GAIN,
    FEED_SHIFT,
    OUTER_BIAS,
) = range(16)


def mm(a, b):
    return jnp.dot(a, b, preferred_element_type=F32)


def mm_nt(a, b):
    return lax.dot_general(a, b, (((1,), (1,)), ((), ())), preferred_element_type=F32)


def mm_tn(a, b):
    return lax.dot_general(a, b, (((0,), (0,)), ((), ())), preferred_element_type=F32)


def normalize(x):
    center = x - jnp.mean(x, axis=-1, keepdims=True)
    spread = jnp.mean(center * center, axis=-1, keepdims=True)
    scale = lax.rsqrt(spread + 1e-05)
    return center * scale, scale


def norm_back(dy, hat, scale, gain):
    w = dy * gain
    first = jnp.mean(w, axis=-1, keepdims=True)
    second = jnp.mean(w * hat, axis=-1, keepdims=True)
    return (w - first - hat * second) * scale


def colsum(x):
    return jnp.sum(x, axis=0, keepdims=True)


def eight_rows(x):
    total = x[0:8]
    for k in range(8, x.shape[0], 8):
        total = total + x[k : k + 8]
    return total


def half_masks(rows):
    lane = lax.broadcasted_iota(jnp.int32, (rows, 128), 1)
    return (lane < 64, lane >= 64)


def pick(mask, x):
    return jnp.where(mask, x.astype(F32), 0.0).astype(BF16)


def pair_lanes(p):
    return pl.ds(pl.multiple_of(p * 128, 128), 128)


def head_rows(p, half):
    return pl.ds(pl.multiple_of(p * 128 + half * 64, 64), 64)


def fill_bias(buckets, table_rows, out_ref):
    length = buckets.shape[0]
    chunks = table_rows.shape[2] // 128
    low, high = buckets & 127, buckets >> 7
    key_place = lax.broadcasted_iota(jnp.int32, (length, 128), 0)
    lane = lax.broadcasted_iota(jnp.int32, (length, 128), 1)

    @pl.loop(0, out_ref.shape[0])
    def _(h):
        rows = [jnp.broadcast_to(table_rows[h, :, pl.ds(c * 128, 128)], (length, 128)) for c in range(chunks)]
        for tile in range(length // 128):
            cols, live = slice(tile * 128, (tile + 1) * 128), (tile + 1) * 128
            total = jnp.zeros((live, 128), F32)
            for c in range(chunks):
                got = jnp.take_along_axis(rows[c][:live], low[:live, cols], axis=1, mode="promise_in_bounds")
                total = jnp.where(high[:live, cols] == c, got, total)
            seen = jnp.where(key_place[:live] <= lane[:live] + tile * 128, total, NEG)
            out_ref[h, pl.ds(0, live), pl.ds(tile * 128, 128)] = seen
            if live < length:
                out_ref[h, pl.ds(live, length - live), pl.ds(tile * 128, 128)] = jnp.full((length - live, 128), NEG, F32)


def axis_bits(sizes):
    return [(axis, bit) for axis in ("rep", "dp") for bit in range(sizes[axis].bit_length() - 1)]


def stage_orders(sizes):
    plain = axis_bits(sizes)
    reps = sizes["rep"].bit_length() - 1
    swapped = list(plain)
    if reps >= 2 and len(plain) > reps:
        swapped = plain[: reps - 1] + [plain[reps], plain[reps - 1]] + plain[reps + 1 :]
    return plain, swapped


def flip(axis, bit):
    place = lax.axis_index(axis)
    return {axis: place + (1 - 2 * ((place // 2**bit) % 2)) * 2**bit}


def fold_sizes(rows, stages, tile):
    sizes, span = [], rows
    for _ in stages:
        span = span // 2 if span % (2 * tile) == 0 else span
        sizes.append(span)
    return sizes


class Reduction:
    def __init__(self, buf, start, rows, out, out_start, stages, tile, lands, send, recv, store):
        self.buf, self.out, self.tile, self.lands = buf, out, tile, lands
        self.send, self.recv, self.shift = send, recv, out_start - start
        folds, spreads = [], []
        base, span = start, rows
        for (axis, bit), size in zip(stages, fold_sizes(rows, stages, tile)):
            mine = (lax.axis_index(axis) // 2**bit) % 2
            peer = flip(axis, bit)
            halve = size < span
            keep = base + mine * size if halve else base
            give = base + (1 - mine) * size if halve else base
            folds.append((peer, give, keep, size))
            if halve:
                spreads.insert(0, (peer, keep, size))
            base, span = keep, size
        self.folds, self.spreads, self.own = folds, spreads, (base, span)
        self.store = pltpu.make_async_copy(self.part(buf, base, span), self.part(out, base + self.shift, span), store)

    def __len__(self):
        return len(self.folds) + len(self.spreads)

    def part(self, ref, start, size):
        return ref.at[pl.ds(start if isinstance(start, int) else pl.multiple_of(start, self.tile), size)]

    def copy(self, k):
        n = len(self.folds)
        if k < n:
            peer, give, keep, size = self.folds[k]
            land, at = self.lands[k]
            source, target = self.part(self.buf, give, size), land.at[pl.ds(at, size)]
        else:
            peer, base, size = self.spreads[k - n]
            target = self.part(self.out, base + self.shift, size)
            source = self.part(self.buf, base, size) if k == n else target
        return pltpu.make_async_remote_copy(
            src_ref=source, dst_ref=target, send_sem=self.send.at[k], recv_sem=self.recv.at[k],
            device_id=peer, device_id_type=pl.DeviceIdType.MESH,
        )

    def start(self, k):
        if k == len(self.folds):
            self.store.start()
        if k == min(len(self.folds) + 1, len(self)):
            self.store.wait()
        if k < len(self):
            self.copy(k).start()

    def finish(self, k):
        self.copy(k).wait()
        if k < len(self.folds):
            peer, give, keep, size = self.folds[k]
            land, at = self.lands[k]
            step = next(c for c in (128, 64, 48, 32, 16, 8) if size % c == 0)

            @pl.loop(0, size // step)
            def _(b):
                kept = pl.ds(pl.multiple_of(keep + b * step, self.tile), step)
                came = pl.ds(pl.multiple_of(at + b * step, self.tile), step)
                total = self.buf[kept, :].astype(F32) + land[came, :].astype(F32)
                self.buf[kept, :] = total.astype(self.buf.dtype)

    def advance(self, k):
        if 0 < k <= len(self):
            self.finish(k - 1)
        if k <= len(self):
            self.start(k)


def signal_all(sem, peers):
    for peer in peers:
        pl.semaphore_signal(sem, inc=1, device_id=peer, device_id_type=pl.DeviceIdType.MESH)


def scaled_heads(value_t, hs_ref):
    return jnp.concatenate([value_t[h * 64 : (h + 1) * 64] * hs_ref[h] for h in range(value_t.shape[0] // 64)], axis=0)


def self_forward(
    tlen, hs_ref, tok, bias_ref, vec_ref, wq, wk, wv, wo, q_ref, k_ref, v_ref, lse_ref, ot_ref, x1_ref, vt_ref
):
    length = tok.shape[0]
    x0 = tok.astype(F32)
    hat, _ = normalize(x0)
    h1 = (hat * vec_ref[SELF_GAIN][...] + vec_ref[SELF_SHIFT][...]).astype(BF16)
    q_ref[...] = ((mm(h1, wq[...]) + vec_ref[QUERY_BIAS][...]) * 0.125).astype(BF16)
    k_ref[...] = mm(h1, wk[...]).astype(BF16)
    value = (mm(h1, wv[...]) + vec_ref[VALUE_BIAS][...]).astype(BF16)
    v_ref[...] = value
    vt_ref[:, pl.ds(0, length)] = value.T
    key_place = lax.broadcasted_iota(jnp.int32, (length, length), 0)
    outside = jnp.where(key_place < tlen, 0.0, NEG)
    masks = half_masks(length)

    @pl.loop(0, q_ref.shape[1] // 128, unroll=4)
    def _(p):
        lanes = pair_lanes(p)
        kp, qp = k_ref[:, lanes], q_ref[:, lanes]
        for half in range(2):
            st = mm_nt(kp, pick(masks[half], qp)) + bias_ref[2 * p + half] + outside
            top = jnp.max(st, axis=0, keepdims=True)
            e = jnp.exp(st - top)
            total = colsum(e)
            ot = mm(vt_ref[head_rows(p, half), pl.ds(0, length)], e.astype(BF16))
            ot_ref[head_rows(p, half), :] = ot * (1.0 / total)
            lse_ref[2 * p + half] = top + jnp.log(total)

    c1 = scaled_heads(ot_ref[...], hs_ref).T.astype(BF16)
    x1_ref[...] = x0 + mm(c1, wo[...]) + vec_ref[OUTPUT_BIAS][...]


def cross_forward(mlen, mem_ref, vec_ref, x1, wcq, wck, wcv, q_ref, k_ref, v_ref, lse_ref, ot_ref, vt_ref, st_ref):
    length, mem_total = x1.shape[0], mem_ref.shape[0]
    hat, _ = normalize(x1)
    h2 = (hat * vec_ref[CROSS_GAIN][...] + vec_ref[CROSS_SHIFT][...]).astype(BF16)
    q_ref[...] = ((mm(h2, wcq[...]) + vec_ref[CROSS_QUERY_BIAS][...]) * 0.125).astype(BF16)
    step = 256

    @pl.loop(0, mem_total // step, unroll=4)
    def _(c):
        rows = pl.ds(pl.multiple_of(c * step, step), step)
        part = mem_ref[rows, :]
        k_ref[rows, :] = mm(part, wck[...]).astype(BF16)
        v_ref[rows, :] = (mm(part, wcv[...]) + vec_ref[CROSS_VALUE_BIAS][...]).astype(BF16)

    for c in range(mem_total // step):
        vt_ref[:, pl.ds(c * step, step)] = v_ref[pl.ds(c * step, step), :].T
    masks = half_masks(length)
    place = lax.broadcasted_iota(jnp.int32, (step, length), 0)
    tiles = length // 128

    @pl.loop(0, q_ref.shape[1] // 128, unroll=2)
    def _(p):
        lanes = pair_lanes(p)
        qp = q_ref[:, lanes]
        for half in range(2):
            qm = pick(masks[half], qp)
            top = jnp.full((1, length), -jnp.inf, F32)
            for c in range(mem_total // step):
                st = mm_nt(k_ref[pl.ds(c * step, step), lanes], qm)
                st = st + jnp.where(place < mlen - c * step, 0.0, NEG)
                for tile in range(tiles):
                    st_ref[tile, pl.ds(half * mem_total + c * step, step), :] = st[:, tile * 128 : (tile + 1) * 128]
                top = jnp.maximum(top, jnp.max(st, axis=0, keepdims=True))
            total = jnp.zeros((1, length), F32)
            ot = jnp.zeros((64, length), F32)
            for c in range(mem_total // step):
                rows = pl.ds(half * mem_total + c * step, step)
                st = jnp.concatenate([st_ref[tile, rows, :] for tile in range(tiles)], axis=1)
                e = jnp.exp(st - top)
                total = total + colsum(e)
                ot = ot + mm(vt_ref[head_rows(p, half), pl.ds(c * step, step)], e.astype(BF16))
            ot_ref[head_rows(p, half), :] = ot * (1.0 / total)
            lse_ref[2 * p + half] = top + jnp.log(total)


def feed_both(x2, g3, vec_ref, wide_ref, w1, w2, out_ref, acc, sums_ref, wide_sums_ref, u_ref, d_ref, df_ref, f_ref, r_ref, middle):
    length, hidden = u_ref.shape
    width = x2.shape[1]
    parts = hidden // width
    hat3, scale3 = normalize(x2)
    gain3 = vec_ref[FEED_GAIN][...]
    h3 = (hat3 * gain3 + vec_ref[FEED_SHIFT][...]).astype(BF16)
    cols = [pl.ds(c * width, width) for c in range(parts)]
    chunk = [pl.ds(c * length, length) for c in range(parts)]
    for c in range(parts):
        u_ref[:, cols[c]] = mm(h3, w1[cols[c], :])
    step = 64
    tiles = hidden // 128
    halves = d_ref.shape[0]

    def d_place(b, k):
        return k % halves, pl.ds(pl.multiple_of((k // halves) * length + b * step, step), step)

    @pl.loop(0, length // step)
    def _(b):
        rows = pl.ds(pl.multiple_of(b * step, step), step)
        u = u_ref[rows, :] + wide_ref[0][...]
        below = 0.5 * (1.0 + lax.erf(u * 0.7071067811865476))
        d = below + u * (jnp.exp(-0.5 * u * u) * 0.3989422804014327)
        for k in range(tiles):
            tile, place = d_place(b, k)
            d_ref[tile, place, :] = d[:, k * 128 : (k + 1) * 128]
        hat, scale = normalize(u * below)
        u_ref[rows, :] = hat
        f = (hat * wide_ref[1][...] + wide_ref[2][...]).astype(BF16)
        for c in range(parts):
            f_ref[pl.ds(pl.multiple_of(c * length + b * step, step), step), :] = f[:, c * width : (c + 1) * width]
        r_ref[rows, :] = jnp.broadcast_to(scale, (step, 128))

    x3 = x2 + vec_ref[OUTER_BIAS][...]
    for c in range(parts):
        x3 = x3 + mm(f_ref[chunk[c], :], w2[cols[c], :])
    out_ref[0] = x3.astype(BF16)
    sums_ref[0:1] += colsum(g3)
    e3 = g3.astype(BF16)
    for c in range(parts):
        acc[pl.ds(hidden + c * width, width), :] += mm_tn(f_ref[chunk[c], :], e3)
        df_ref[:, cols[c]] = mm_nt(e3, w2[cols[c], :])
    middle()

    @pl.loop(0, length // step)
    def _(b):
        rows = pl.ds(pl.multiple_of(b * step, step), step)
        dy, hat = df_ref[rows, :], u_ref[rows, :]
        part = dy * hat
        wide_sums_ref[0:8] += eight_rows(part)
        wide_sums_ref[8:16] += eight_rows(dy)
        da = norm_back(dy, hat, r_ref[rows, 0:1], wide_ref[1][...])
        pieces = []
        for k in range(tiles):
            tile, place = d_place(b, k)
            pieces.append(d_ref[tile, place, :])
        du = da * jnp.concatenate(pieces, axis=1)
        wide_sums_ref[16:24] += eight_rows(du)
        eu = du.astype(BF16)
        for c in range(parts):
            f_ref[pl.ds(pl.multiple_of(c * length + b * step, step), step), :] = eu[:, c * width : (c + 1) * width]

    dh3 = jnp.zeros(x2.shape, F32)
    h3t = h3.T
    for c in range(parts):
        acc[cols[c], :] += mm(h3t, f_ref[chunk[c], :])
        dh3 = dh3 + mm_nt(f_ref[chunk[c], :], w1[cols[c], :])
    sums_ref[1:2] += colsum(dh3 * hat3)
    sums_ref[2:3] += colsum(dh3)
    return g3 + norm_back(dh3, hat3, scale3, gain3)


def cross_backward(
    mlen, mem_ref, q_ref, k_ref, v_ref, lse_ref, delta_ref, do_ref, wck, wcv, dk_ref, dv_ref, dqt_ref, kt_ref,
    acc_key, acc_value, sums_ref, stage_ref, points,
):
    length, mem_total = q_ref.shape[0], mem_ref.shape[0]
    step = 256
    for c in range(mem_total // step):
        kt_ref[:, pl.ds(c * step, step)] = k_ref[pl.ds(c * step, step), :].T
    masks = half_masks(length)
    place = lax.broadcasted_iota(jnp.int32, (step, length), 0)
    pairs, chunks = q_ref.shape[1] // 128, mem_total // step

    @pl.loop(0, pairs)
    def _(p):
        @pl.when(p == pairs // 2)
        def _():
            points[0]()

        lanes = pair_lanes(p)
        qp, dop = q_ref[:, lanes], do_ref[:, lanes]
        qms = [pick(masks[half], qp) for half in range(2)]
        doms = [pick(masks[half], dop) for half in range(2)]
        lse = [lse_ref[2 * p + half] for half in range(2)]
        delta = [delta_ref[2 * p + half] for half in range(2)]
        for c in range(mem_total // step):
            rows = pl.ds(c * step, step)
            kp, vp = k_ref[rows, lanes], v_ref[rows, lanes]
            outside = jnp.where(place < mlen - c * step, 0.0, NEG)
            dv = jnp.zeros((step, 128), F32)
            dk = jnp.zeros((step, 128), F32)
            for half in range(2):
                st = mm_nt(kp, qms[half]) + outside
                pt = jnp.exp(st - lse[half])
                dpt = mm_nt(vp, doms[half])
                dst = (pt * (dpt - delta[half])).astype(BF16)
                stage_ref[:, pl.ds((half * chunks + c) * length, length)] = dst.astype(F32)
                dv = dv + mm(pt.astype(BF16), doms[half])
                dk = dk + mm(dst, qms[half])
            dv_ref[rows, lanes] = dv.astype(BF16)
            dk_ref[rows, lanes] = dk.astype(BF16)
        for half in range(2):
            staged = [stage_ref[:, pl.ds((half * chunks + c) * length, length)] for c in range(chunks)]
            dst = jnp.concatenate(staged, axis=0).astype(BF16)
            dqt_ref[head_rows(p, half), :] = mm(kt_ref[head_rows(p, half), :], dst)

    points[1]()
    acc_key[...] += mm_tn(mem_ref[...], dk_ref[...])
    acc_value[...] += mm_tn(mem_ref[...], dv_ref[...])

    @pl.loop(0, mem_total // step, unroll=4)
    def _(c):
        rows = pl.ds(pl.multiple_of(c * step, step), step)
        dk, dv = dk_ref[rows, :], dv_ref[rows, :]
        mem_ref[rows, :] = (mm_nt(dk, wck[...]) + mm_nt(dv, wcv[...])).astype(BF16)
        sums_ref[8:9] += colsum(dv.astype(F32))


def self_backward(tlen, bias_ref, q_ref, k_ref, v_ref, lse_ref, delta_ref, do_ref, dqt_ref, dk_ref, dv_ref, kt_ref, dbias_ref):
    length = q_ref.shape[0]
    kt_ref[:, pl.ds(0, length)] = k_ref[...].T
    key_place = lax.broadcasted_iota(jnp.int32, (length, length), 0)
    outside = jnp.where(key_place < tlen, 0.0, NEG)
    masks = half_masks(length)

    @pl.loop(0, q_ref.shape[1] // 128, unroll=4)
    def _(p):
        lanes = pair_lanes(p)
        qp, dop = q_ref[:, lanes], do_ref[:, lanes]
        kp, vp = k_ref[:, lanes], v_ref[:, lanes]
        dv = jnp.zeros((length, 128), F32)
        dk = jnp.zeros((length, 128), F32)
        for half in range(2):
            h = 2 * p + half
            qm, dom = pick(masks[half], qp), pick(masks[half], dop)
            st = mm_nt(kp, qm) + bias_ref[h] + outside
            pt = jnp.exp(st - lse_ref[h])
            dpt = mm_nt(vp, dom)
            dst = (pt * (dpt - delta_ref[h])).astype(BF16)
            rows = pl.ds(pl.multiple_of(h * length, length), length)
            wide_ds = dst.astype(F32)
            for tile in range(length // 128):
                dbias_ref[tile, rows, :] += wide_ds[:, tile * 128 : (tile + 1) * 128]
            dqt_ref[head_rows(p, half), :] = mm(kt_ref[head_rows(p, half), pl.ds(0, length)], dst)
            dv = dv + mm(pt.astype(BF16), dom)
            dk = dk + mm(dst, qm)
        dv_ref[:, lanes] = dv.astype(BF16)
        dk_ref[:, lanes] = dk.astype(BF16)


def bucket_totals(buckets_t, dbias_ref, out_ref, between):
    length = buckets_t.shape[0]
    heads = dbias_ref.shape[1] // length
    lo_places = lax.broadcasted_iota(jnp.int32, (32, 128), 0)
    group = 8

    def block(start, tiles, acc):
        rows = buckets_t[pl.ds(start, group), :]
        lefts, rights = [], []
        for k in range(group):
            for tile in tiles:
                ids = rows[k : k + 1, tile * 128 : (tile + 1) * 128]
                d = dbias_ref[tile, pl.ds(start + k, heads, stride=length), :]
                high = jnp.broadcast_to(ids >> 5, (heads, 128))
                lefts.append(jnp.concatenate([jnp.where(high == g, d, 0.0) for g in range(16)], axis=0).astype(BF16))
                rights.append(jnp.where(lo_places == (ids & 31), 1.0, 0.0).astype(BF16))
        return acc + mm_nt(jnp.concatenate(lefts, axis=1), jnp.concatenate(rights, axis=1))

    acc = jnp.zeros((16 * heads, 32), F32)
    tiles = length // 128
    for band in range(tiles):
        if band:
            between()
        live = range(band, tiles)

        def body(b, acc):
            return block(pl.multiple_of(band * 128 + b * group, group), live, acc)

        acc = lax.fori_loop(0, 128 // group, body, acc)
    for g in range(16):
        out_ref[:, g * 32 : (g + 1) * 32] = acc[g * heads : (g + 1) * heads]


SMALL_ROWS = 64
SUMS_B = 24
HEAD_ROWS = 40
TABLE_ROWS = 48


def piece_order(places):
    far, near = list(range(max(places // 2, 1), places)), list(range(1, places // 2))
    order = []
    for k in range(len(far)):
        order.append(far[k])
        if k < len(near):
            order.append(near[k])
    return order


def partner(me, places, k):
    if places & (places - 1):
        return lax.rem(me + k, places)
    for bit in range(places.bit_length() - 1):
        if (k >> bit) & 1:
            me = me + (1 - 2 * ((me // 2**bit) % 2)) * 2**bit
    return me


def layer_kernel(sizes, layout, tlen_ref, mlen_ref, hs_ref, tok_ref, cot_ref, mask_ref, buckets_ref, table_ref, *rest):
    mem_hbm, w1_hbm, w2_hbm = rest[:3]
    vec_ref, wide_ref = rest[3:19], rest[19:22]
    weights_hbm = rest[22:30]
    out_ref, dtok_ref, dmem_hbm, grads_hbm, small_hbm = rest[30:35]
    (
        mem_scr, w1s, w2s, acc, bias_ref, st_scr,
        q1_scr, k1_scr, v1_scr, lse1_scr, ot1_scr, x1_scr,
        kv_scr, q2_scr, do_scr, lse2_scr, delta_scr,
        vt_scr, ot_scr, u_scr, df_scr, r_scr, dk_scr, dv_scr,
        grads, land, small, small_land, wide_scr, hs_scr, table_scr, buckets_t_scr,
        load_sem, send_sem, recv_sem, own_sem, back_send, back_recv, back_own, group_send, group_recv, store_sem, ready_sem, late_sem,
        weight_sem, *weight_scr,
    ) = rest[35:]
    wq, wk, wv, wo, wcq, wck, wcv, wco = weight_scr
    seqs, mem_total, width = mem_scr.shape
    length, hidden, heads = tok_ref.shape[1], u_scr.shape[1], bias_ref.shape[0]
    places, piece = mem_hbm.shape[0], mem_hbm.shape[2]
    t = pl.program_id(0)
    me = lax.axis_index("dp")
    mine = pl.ds(pl.multiple_of(me * piece, piece), piece)
    k2_scr, v2_scr = kv_scr.at[pl.ds(0, mem_total)], kv_scr.at[pl.ds(mem_total, mem_total)]
    sums_a, sums_b = small.at[pl.ds(0, 8)], small.at[pl.ds(SUMS_B, 24)]
    base = 2 * hidden
    acc_at = lambda k: acc.at[pl.ds(base + k * width, width)]
    CROSS_OUT, OUT, QUERY, KEY, VALUE = range(5)
    order = piece_order(places)

    def own_in(s):
        return pltpu.make_async_copy(mem_hbm.at[me, s], mem_scr.at[s, mine], own_sem.at[s])

    def own_back(s):
        return pltpu.make_async_copy(mem_scr.at[s, mine], dmem_hbm.at[me, s], back_own.at[s])

    def loads():
        copies = []
        for c in range(hidden // width):
            cols = pl.ds(c * width, width)
            copies.append(pltpu.make_async_copy(w1_hbm.at[:, cols], w1s.at[cols], load_sem.at[c]))
        copies.append(pltpu.make_async_copy(w2_hbm, w2s, load_sem.at[hidden // width]))
        return copies

    def remote(source, target, send, recv, peer):
        return pltpu.make_async_remote_copy(
            src_ref=source, dst_ref=target, send_sem=send, recv_sem=recv, device_id={"dp": peer},
            device_id_type=pl.DeviceIdType.MESH,
        )

    def send_in(s, k):
        peer = partner(me, places, k)
        remote(mem_hbm.at[peer, s], mem_scr.at[s, mine], send_sem.at[s], recv_sem.at[s], peer).start()

    def send_back(s, k):
        peer = partner(me, places, k)
        rows = pl.ds(pl.multiple_of(peer * piece, piece), piece)
        remote(mem_scr.at[s, rows], dmem_hbm.at[me, s], back_send.at[s], back_recv.at[s], peer).start()

    def all_in(s):
        some = mem_scr.at[s, pl.ds(0, (places - 1) * piece)]
        return remote(some, some, send_sem.at[s], recv_sem.at[s], partner(me, places, 1))

    def all_back(s):
        some = dmem_hbm.at[pl.ds(0, places - 1), s]
        return remote(some, some, back_send.at[s], back_recv.at[s], partner(me, places, 1))

    plain, swapped = stage_orders(sizes)
    spare = pl.ds(length, mem_total - length)
    pools = {"first": w2s, "second": w1s, "key": dk_scr.at[spare], "value": dv_scr.at[spare], "land": land}
    buffers = {"grads": grads, "kv": kv_scr}
    reductions = []
    for r, (buf, start, rows, out_start, lands, color) in enumerate(layout):
        reductions.append(Reduction(
            buffers[buf], start, rows, grads_hbm, out_start, swapped if color == 1 else plain, 16,
            [(pools[name], at) for name, at in lands], group_send.at[r], group_recv.at[r], store_sem.at[r],
        ))
    last = len(layout)
    at, lands = 0, []
    for size in fold_sizes(SMALL_ROWS, plain, 8):
        lands.append((small_land, at))
        at += size
    reductions.append(Reduction(
        small, 0, SMALL_ROWS, small_hbm, 0, plain, 8, lands, group_send.at[last], group_recv.at[last], store_sem.at[last],
    ))
    first = [r for r, item in enumerate(layout) if item[0] == "grads" and item[1] < base]
    second = [r for r, item in enumerate(layout) if item[0] == "grads" and item[1] >= base]
    third = [r for r, item in enumerate(layout) if item[0] == "kv"]
    flips = [flip(axis, bit) for axis, bit in plain]

    steps = 4 * seqs
    begin_first, begin_second = 3 * (3 * seqs - 1), 3 * 3 * seqs
    planned = len(plain) == 5 and places == 8 and seqs == 4
    acts = {p: [] for p in range(3 * steps)}
    sends = {p: [] for p in range(3 * steps)}
    moved = [0] * len(reductions)
    queue = [(s, k) for s in range(seqs) for k in order]
    for p in range(3 * seqs, 3 * steps):
        if planned:
            count = SENDS[p - 3 * seqs]
        else:
            count = -(-len(order) * 2 // 7)
        while count and queue and p >= 3 * (seqs + 2 * queue[0][0] + 2):
            sends[p].append(queue.pop(0))
            count -= 1
        for r in ACTS[p - 3 * seqs] if planned else ():
            acts[p].append((r, moved[r]))
            moved[r] += 1

    def point(part, low, high):
        for step in range(low, high):
            p = 3 * step + part
            if acts[p] or sends[p] or (p == begin_first and flips):

                @pl.when(t == step)
                def _():
                    if p == begin_first and flips:
                        pl.semaphore_wait(ready_sem, len(flips))
                    for r, k in acts[p]:
                        reductions[r].advance(k)
                    for s, k in sends[p]:
                        send_back(s, k)

    @pl.when(t == 0)
    def _():
        bucket_load = pltpu.make_async_copy(buckets_ref, buckets_t_scr, load_sem.at[hidden // width + 1])
        bucket_load.start()
        for s in range(seqs):
            own_in(s).start()
        peers = [{"dp": partner(me, places, k)} for k in range(1, places)]
        peers += [flip(axis, bit) for axis, bit in plain if axis == "rep"]
        if peers:
            barrier = pltpu.get_barrier_semaphore()
            signal_all(barrier, peers)
        weight_loads = [
            pltpu.make_async_copy(a, b, weight_sem.at[k]) for k, (a, b) in enumerate(zip(weights_hbm, weight_scr))
        ]
        for c in weight_loads:
            c.start()
        if peers:
            pl.semaphore_wait(barrier, len(peers))
        for s in range(seqs):
            for k in order:
                send_in(s, k)
        for c in loads():
            c.start()
        for ref in (acc, small, wide_scr, hs_scr):
            ref[...] = jnp.zeros_like(ref)
        for h in range(heads):
            table_scr[h] = jnp.zeros(table_scr.shape[1:], F32)
            table_scr[h, :, : table_ref.shape[1]] = table_ref[h : h + 1, :]
        bucket_load.wait()
        buckets_t_scr[...] = buckets_t_scr[...].T
        fill_bias(buckets_t_scr[...], table_scr, bias_ref)
        for c in weight_loads:
            c.wait()

    @pl.when(t < seqs)
    def _():
        self_forward(
            tlen_ref[t], hs_ref, tok_ref[0], bias_ref, vec_ref, wq, wk, wv, wo,
            q1_scr.at[t], k1_scr.at[t], v1_scr.at[t], lse1_scr.at[t], ot1_scr.at[t], x1_scr.at[t], vt_scr,
        )

    @pl.when(t == seqs)
    def _():
        for c in loads():
            c.wait()

    inner = t - seqs
    s = inner // 2

    @pl.when((t >= seqs) & (t < 3 * seqs) & (inner % 2 == 0))
    def _():
        own_in(s).wait()
        if places > 1:
            all_in(s).wait_recv()
        point(0, seqs, 3 * seqs)
        x1 = x1_scr[s]
        cross_forward(
            mlen_ref[s], mem_scr.at[s], vec_ref, x1, wcq, wck, wcv,
            q2_scr, k2_scr, v2_scr, lse2_scr, ot_scr, vt_scr, st_scr,
        )
        point(1, seqs, 3 * seqs)
        hat, scale = normalize(ot_scr[...].T)
        gain = vec_ref[POST_GAIN][...]
        c2 = (hat * gain + vec_ref[POST_SHIFT][...]).astype(BF16)
        x2 = x1 + mm(c2, wco[...]) + vec_ref[CROSS_OUTPUT_BIAS][...]
        here = lax.broadcasted_iota(jnp.int32, mask_ref.shape, 0) == s
        row = jnp.sum(jnp.where(here, mask_ref[...], 0), axis=0, keepdims=True).astype(F32)
        row = jnp.where(lax.broadcasted_iota(jnp.int32, (1, length), 1) < tlen_ref[s], row, 0.0)
        g3 = cot_ref[0].astype(F32) * jnp.broadcast_to(row, (8, length)).T[:, 0:1]
        g2 = feed_both(
            x2, g3, vec_ref, wide_ref, w1s, w2s, out_ref, acc, sums_a, wide_scr,
            u_scr, st_scr, df_scr, dk_scr, r_scr, lambda: point(2, seqs, 3 * seqs),
        )
        df_scr[:, pl.ds(0, width)] = g2
        sums_a[3:4] += colsum(g2)
        e2 = g2.astype(BF16)
        acc_at(CROSS_OUT)[...] += mm_tn(c2, e2)
        dc2 = mm_nt(e2, wco[...])
        sums_a[4:5] += colsum(dc2 * hat)
        sums_a[5:6] += colsum(dc2)
        do2 = norm_back(dc2, hat, scale, gain).astype(BF16)
        do_scr[...] = do2
        prod = do2.astype(F32).T * ot_scr[...]
        for h in range(heads):
            delta_scr[h] = colsum(prod[h * 64 : (h + 1) * 64])

    @pl.when(t == 3 * seqs - 2)
    def _():
        signal_all(ready_sem, flips)
        for k in range(3):
            total = colsum(wide_scr[8 * k : 8 * k + 8])
            for c in range(hidden // width):
                row = 8 + k * (hidden // width) + c
                small[row : row + 1] = total[:, c * width : (c + 1) * width]

        @pl.loop(0, base // 256)
        def _(b):
            rows = pl.ds(pl.multiple_of(b * 256, 256), 256)
            grads[rows, :] = acc[rows, :].astype(BF16)

    @pl.when((t >= seqs) & (t < 3 * seqs) & (inner % 2 == 1))
    def _():
        point(0, seqs, 3 * seqs)
        cross_backward(
            mlen_ref[s], mem_scr.at[s], q2_scr, k2_scr, v2_scr, lse2_scr, delta_scr, do_scr, wck, wcv,
            dk_scr, dv_scr, ot_scr, vt_scr, acc_at(KEY), acc_at(VALUE), sums_b, u_scr,
            [lambda: point(1, seqs, 3 * seqs), lambda: point(2, seqs, 3 * seqs)],
        )
        own_back(s).start()
        dq2 = (ot_scr[...].T.astype(BF16).astype(F32) * 0.125).astype(BF16)
        hat2, scale2 = normalize(x1_scr[s])
        gain2 = vec_ref[CROSS_GAIN][...]
        h2 = (hat2 * gain2 + vec_ref[CROSS_SHIFT][...]).astype(BF16)
        acc_at(QUERY)[...] += mm_tn(h2, dq2)
        sums_b[7:8] += colsum(dq2.astype(F32))
        dh2 = mm_nt(dq2, wcq[...])
        sums_b[5:6] += colsum(dh2 * hat2)
        sums_b[6:7] += colsum(dh2)
        g1 = df_scr[:, pl.ds(0, width)] + norm_back(dh2, hat2, scale2, gain2)
        x1_scr[s] = g1
        sums_b[4:5] += colsum(g1)
        c1t = scaled_heads(ot1_scr[s], hs_ref).astype(BF16)
        acc_at(OUT)[...] += mm(c1t, g1.astype(BF16))

    @pl.when(t == 3 * seqs - 1)
    def _():
        @pl.loop(0, 5 * width // 256)
        def _(b):
            rows = pl.ds(pl.multiple_of(base + b * 256, 256), 256)
            grads[rows, :] = acc[rows, :].astype(BF16)

        signal_all(late_sem, flips)
        st_scr[...] = jnp.zeros_like(st_scr)
        acc[pl.ds(0, 3 * width), :] = jnp.zeros((3 * width, width), F32)

    @pl.when(t >= 3 * seqs)
    def _():
        point(0, 3 * seqs, steps)
        s = t - 3 * seqs
        g1 = x1_scr[s]
        dc1t = mm_nt(g1.astype(BF16), wo[...]).T
        do1t = scaled_heads(dc1t, hs_ref).astype(BF16)
        do_scr[...] = do1t.T
        for h in range(heads):
            rows = slice(h * 64, (h + 1) * 64)
            o = ot1_scr[s, rows, :]
            hs_scr[h : h + 1, :] += colsum(o * dc1t[rows])
            delta_scr[h] = colsum(o * do1t[rows].astype(F32))
        dk_ref, dv_ref = dk_scr.at[pl.ds(0, length)], dv_scr.at[pl.ds(0, length)]
        self_backward(
            tlen_ref[s], bias_ref, q1_scr.at[s], k1_scr.at[s], v1_scr.at[s], lse1_scr.at[s], delta_scr, do_scr,
            ot_scr, dk_ref, dv_ref, vt_scr, st_scr,
        )
        point(1, 3 * seqs, steps)
        dq1 = (ot_scr[...].T.astype(BF16).astype(F32) * 0.125).astype(BF16)
        dk1, dv1 = dk_ref[...], dv_ref[...]
        hat1, scale1 = normalize(tok_ref[0].astype(F32))
        gain1 = vec_ref[SELF_GAIN][...]
        h1t = (hat1 * gain1 + vec_ref[SELF_SHIFT][...]).astype(BF16).T
        for k, d in enumerate((dq1, dk1, dv1)):
            acc[pl.ds(k * width, width), :] += mm(h1t, d)
        point(2, 3 * seqs, steps)
        sums_b[2:3] += colsum(dq1.astype(F32))
        sums_b[3:4] += colsum(dv1.astype(F32))
        dh1 = mm_nt(dq1, wq[...]) + mm_nt(dk1, wk[...]) + mm_nt(dv1, wv[...])
        sums_b[0:1] += colsum(dh1 * hat1)
        sums_b[1:2] += colsum(dh1)
        dtok_ref[0] = (g1 + norm_back(dh1, hat1, scale1, gain1)).astype(BF16)

    @pl.when(t == steps - 1)
    def _():
        @pl.loop(0, 3 * width // 256)
        def _(b):
            rows = pl.ds(pl.multiple_of(b * 256, 256), 256)
            kv_scr[rows, :] = acc[rows, :].astype(BF16)

        small[HEAD_ROWS : HEAD_ROWS + heads] = jnp.broadcast_to(
            jnp.sum(hs_scr[...], axis=1, keepdims=True), (heads, width)
        )
        def move(r):
            if r < 0:
                if queue:
                    send_back(*queue.pop(0))
            elif moved[r] <= len(reductions[r]):
                reductions[r].advance(moved[r])
                moved[r] += 1

        if flips:
            pl.semaphore_wait(late_sem, len(flips))
        for r in third:
            move(r)

        def between():
            for r in BETWEEN if planned else first + second + third:
                move(r)

        bucket_totals(buckets_t_scr, st_scr, small.at[pl.ds(TABLE_ROWS, heads)], between)
        for r in TAIL if planned else ():
            move(r)
        left = third + [last] + second + first
        while any(moved[r] <= len(reductions[r]) for r in left):
            for r in left:
                move(r)
            move(-1)
        while queue:
            move(-1)
        for s in range(seqs):
            own_back(s).wait()
            if places > 1:
                all_in(s).wait_send()
                all_back(s).wait_send()
                all_back(s).wait_recv()


ACTS = (
    (),
    (),
    (),
    (),
    (),
    (),
    (),
    (),
    (),
    (),
    (),
    (),
    (),
    (),
    (),
    (),
    (),
    (),
    (),
    (),
    (),
    (0, 1),
    (2, 3, 0, 1),
    (2, 3),
    (4, 5, 0, 1),
    (4, 5, 2),
    (),
    (1,),
    (3, 2, 0),
    (1,),
    (),
    (2, 3, 0, 4, 1),
    (),
    (),
    (5, 3, 2, 4, 0),
    (1,),
)
SENDS = (0, 0, 0, 0, 0, 0, 0, 0, 0, 0, 0, 0, 0, 1, 2, 0, 2, 2, 1, 2, 0, 0, 2, 2, 0, 1, 0, 2, 0, 0, 2, 0, 0, 2, 0, 0)
BETWEEN = (2, 3, 4, 5, 6, 7, 8, -1)
TAIL = (0, 9, 1, 2, 3, 6, 9, 5, 4, 8, 7, 6, 0, 9, 1, 3, -1, -1, 7, 5, 2, 6, 4, 8, 9, 0, 7, 3, 4, -1, -1, 1, 8, 9, 5, 6, 7, 1, 0, 2, 0, -1, -1, 8, 4, 2, 5, 9, 3, 6, 7, 3, 6, 8, 7, 5, 4, 9, 8, 6, 7, 4, 8, 6, 5, 9, 6, 7, 5, 9, 8, 7, 8)
MEMBERS = (('first', 1, 2), ('first', 0, 2), ('first', 0, 2), ('first', 0, 2), ('second', 0, 3), ('second', 0, 2), ('third', 1, 1), ('third', 1, 1), ('third', 0, 1))


def reduction_layout(sizes, width, hidden, spare):
    plain, _ = stage_orders(sizes)
    base = 2 * hidden
    members, at = [], {"first": 0, "second": 2 * hidden, "third": 0}
    for name, color, units in MEMBERS:
        rows = units * width
        out_start = at[name] + (base + 5 * width if name == "third" else 0)
        members.append(("kv" if name == "third" else "grads", at[name], rows, out_start, color))
        at[name] += rows
    used = {"first": 0, "second": 0, "key": 0, "value": 0, "land": 0}
    layout = []
    for buf, start, rows, out_start, color in members:
        lands = []
        for size in fold_sizes(rows, plain, 16):
            room = {"first": hidden, "second": hidden} if buf == "grads" else {"key": spare, "value": spare}
            name = next((n for n in room if used[n] + size <= room[n]), "land")
            lands.append((name, used[name]))
            used[name] += size
        layout.append((buf, start, rows, out_start, lands, color))
    return layout, max(used["land"], 16)


def whole_layer(sizes, tlen, mlen, head_scale, tokens, cotangent, mask, buckets, table, memory, w1, w2, vecs, wides, weights):
    seqs, length, width = tokens.shape
    places, _, piece, _ = memory.shape
    mem_total = places * piece
    heads, hidden = head_scale.shape[0], w1.shape[1]
    layout, land = reduction_layout(sizes, width, hidden, mem_total - length)
    plain, _ = stage_orders(sizes)
    small_land = max(sum(fold_sizes(SMALL_ROWS, plain, 8)), 8)
    slots = max(2 * len(plain), 1)
    several = places > 1 or sizes["rep"] > 1
    sds = jax.ShapeDtypeStruct
    anywhere = pl.BlockSpec(memory_space=pl.ANY)
    const = lambda a: pl.BlockSpec(a.shape, lambda t, *_: (0,) * a.ndim, pipeline_mode=pl.Buffered(1))
    seq = lambda idx: pl.BlockSpec((1, length, width), lambda t, *_: (idx(t), 0, 0))
    ends = lambda t: jnp.where(t < 3 * seqs, jnp.minimum(t, seqs - 1), t - 3 * seqs)
    middle = lambda t: jnp.clip((t - seqs) // 2, 0, seqs - 1)
    late = lambda t: jnp.maximum(t - 3 * seqs, 0)
    tall = heads * length
    scratch = [
        ((seqs, mem_total, width), BF16), ((hidden, width), BF16), ((hidden, width), BF16),
        ((2 * hidden + 5 * width, width), F32), ((heads, length, length), F32),
        ((length // 128, max(tall, 2 * mem_total, hidden * length * 128 // (length * 128)), 128), F32),
        ((seqs, length, width), BF16), ((seqs, length, width), BF16), ((seqs, length, width), BF16),
        ((seqs, heads, 1, length), F32), ((seqs, width, length), F32), ((seqs, length, width), F32),
        ((2 * mem_total, width), BF16), ((length, width), BF16), ((length, width), BF16),
        ((heads, 1, length), F32), ((heads, 1, length), F32),
        ((width, mem_total), BF16), ((width, length), F32), ((length, hidden), F32), ((length, hidden), F32),
        ((length, 128), F32), ((max(mem_total, hidden // width * length), width), BF16), ((mem_total, width), BF16),
        ((2 * hidden + 5 * width, width), BF16), ((land, width), BF16), ((SMALL_ROWS, width), F32), ((small_land, width), F32),
        ((24, hidden), F32), ((heads, length), F32), ((heads, 1, 512), F32), ((length, length), jnp.int32),
    ]
    dma = pltpu.SemaphoreType.DMA
    groups = len(layout) + 1
    return pl.pallas_call(
        functools.partial(layer_kernel, sizes, layout),
        out_shape=[
            sds(tokens.shape, BF16), sds(tokens.shape, BF16), sds(memory.shape, BF16),
            sds((2 * hidden + 8 * width, width), BF16), sds((SMALL_ROWS, width), F32),
        ],
        grid_spec=pltpu.PrefetchScalarGridSpec(
            num_scalar_prefetch=3,
            grid=(4 * seqs,),
            in_specs=[seq(ends), seq(middle), const(mask), anywhere, const(table), anywhere, anywhere, anywhere]
            + [const(a) for a in vecs + wides] + [anywhere] * len(weights),
            out_specs=[seq(middle), seq(late), anywhere, anywhere, anywhere],
            scratch_shapes=[pltpu.VMEM(shape, dtype) for shape, dtype in scratch] + [
                dma((hidden // width + 2,)), dma((seqs,)), dma((seqs,)), dma((seqs,)), dma((seqs,)), dma((seqs,)),
                dma((seqs,)), dma((groups, slots)), dma((groups, slots)), dma((groups,)), pltpu.SemaphoreType.REGULAR, pltpu.SemaphoreType.REGULAR,
                dma((len(weights),)),
            ] + [pltpu.VMEM(a.shape, BF16) for a in weights],
        ),
        compiler_params=pltpu.CompilerParams(
            vmem_limit_bytes=VMEM_LIMIT, collective_id=0 if several else None, has_side_effects=True
        ),
        name="layer",
    )(tlen, mlen, head_scale, tokens, cotangent, mask, buckets, table, memory, w1, w2, *vecs, *wides, *weights)


def unpack_kernel(count, grads_hbm, small_ref, *refs):
    kept, refs = refs[:count], refs[count:]
    passed, refs = refs[:count], refs[count:]
    big, vectors, tail = refs[:10], refs[10:28], refs[28:]
    table_ref, scale_ref, rough, exact = tail[:4]
    holds, (in_sem, out_sem, hold_in, hold_out) = tail[4:-4], tail[-4:]
    dw1, dw2, rest = big[0], big[1], big[2:]
    width = grads_hbm.shape[1]
    parts = dw1.shape[1] // width
    targets = [dw1.at[:, pl.ds(c * width, width)] for c in range(parts)]
    targets += [dw2.at[pl.ds(c * width, width)] for c in range(parts)] + list(rest)
    rows = [pl.ds(k * width, width) for k in range(len(targets))]
    into = [pltpu.make_async_copy(grads_hbm.at[r], rough.at[r], in_sem.at[k]) for k, r in enumerate(rows)]
    out = [pltpu.make_async_copy(exact.at[r], target, out_sem.at[k]) for k, (r, target) in enumerate(zip(rows, targets))]
    take = [pltpu.make_async_copy(a, hold, hold_in.at[k]) for k, (a, hold) in enumerate(zip(kept, holds))]
    give = [pltpu.make_async_copy(hold, a, hold_out.at[k]) for k, (a, hold) in enumerate(zip(passed, holds))]
    for c in into + take:
        c.start()
    for row, ref in zip(VECTOR_ROWS, vectors):
        for c in range(ref.shape[1] // width):
            ref[:, c * width : (c + 1) * width] = small_ref[row + c : row + c + 1]
    heads = scale_ref.shape[1]
    table_ref[...] = small_ref[TABLE_ROWS : TABLE_ROWS + heads, : table_ref.shape[1]]
    block = small_ref[HEAD_ROWS : HEAD_ROWS + heads]
    diagonal = lax.broadcasted_iota(jnp.int32, block.shape, 0) == lax.broadcasted_iota(jnp.int32, block.shape, 1)
    scale_ref[...] = colsum(jnp.where(diagonal, block, 0.0))[:, :heads]
    step = 64
    for k in range(len(targets)):
        into[k].wait()

        @pl.loop(0, width // step)
        def _(b):
            part = pl.ds(pl.multiple_of(k * width + b * step, step), step)
            exact[part, :] = rough[part, :].astype(F32)

        out[k].start()
    for a, b in zip(take, give):
        a.wait()
        b.start()
    for c in out + give:
        c.wait()


VECTOR_ROWS = (24, 25, 26, 27, 28, 29, 30, 31, 32, 4, 5, 3, 1, 2, 0, 16, 8, 12)


def unpack(grads, small, kept, hidden, heads, buckets):
    total, width = grads.shape
    sds = jax.ShapeDtypeStruct
    big = [sds((width, hidden), F32), sds((hidden, width), F32)] + [sds((width, width), F32)] * 8
    vectors = [sds((1, width), F32)] * 15 + [sds((1, hidden), F32)] * 3
    tail = [sds((heads, buckets), F32), sds((1, heads), F32)]
    anywhere, inside = pl.BlockSpec(memory_space=pl.ANY), pl.BlockSpec(memory_space=pltpu.VMEM)
    dma = pltpu.SemaphoreType.DMA
    count = len(kept)
    outs = pl.pallas_call(
        functools.partial(unpack_kernel, count),
        out_shape=[sds(a.shape, a.dtype) for a in kept] + big + vectors + tail,
        in_specs=[anywhere, inside] + [anywhere] * count,
        out_specs=[anywhere] * (count + 10) + [inside] * (len(vectors) + len(tail)),
        scratch_shapes=[pltpu.VMEM((total, width), BF16), pltpu.VMEM((total, width), F32)]
        + [pltpu.VMEM(a.shape, a.dtype) for a in kept]
        + [dma((total // width,)), dma((total // width,)), dma((count,)), dma((count,))],
        compiler_params=pltpu.CompilerParams(vmem_limit_bytes=VMEM_LIMIT),
        name="unpack",
    )(grads, small, *kept)
    return outs[:count], outs[count:]


def local(
    tokens, cotangent, target_lengths, task_mask, memory_lengths, position_buckets, memory,
    self_gain, self_shift, query_weight, query_bias, key_weight, value_weight, value_bias, position_table, head_scale,
    output_weight, output_bias, cross_gain, cross_shift, cross_query, cross_query_bias, cross_key, cross_value,
    cross_value_bias, post_gain, post_shift, cross_output, cross_output_bias, feed_gain, feed_shift, inner_weight,
    inner_bias, inner_gain, inner_shift, outer_weight, outer_bias,
):
    heads = head_scale.shape[0]
    bucket_count = position_table.shape[0]
    hidden = inner_weight.shape[1]
    table_t = position_table.T
    row = lambda v: v.reshape(1, -1)
    vecs = [row(v) for v in (
        self_gain, self_shift, query_bias, value_bias, output_bias, output_bias, cross_gain, cross_shift,
        cross_query_bias, cross_value_bias, post_gain, post_shift, cross_output_bias, feed_gain, feed_shift, outer_bias,
    )]
    wides = [row(v) for v in (inner_bias, inner_gain, inner_shift)]
    sizes = {"dp": lax.axis_size("dp"), "rep": lax.axis_size("rep")}
    layer_output, dtok, memory_gradient, grads, small = whole_layer(
        sizes, target_lengths, memory_lengths, head_scale, tokens, cotangent, task_mask, position_buckets, table_t,
        memory, inner_weight, outer_weight, vecs, wides,
        [query_weight, key_weight, value_weight, output_weight, cross_query, cross_key, cross_value, cross_output],
    )
    (layer_output, dtok, memory_gradient), outs = unpack(
        grads, small, [layer_output, dtok, memory_gradient], hidden, heads, bucket_count
    )
    dw1, dw2, dwco, dwo, dwcq, dwck, dwcv, dwq, dwk, dwv = outs[:10]
    (
        d_self_gain, d_self_shift, d_query_bias, d_value_bias, d_output_bias, d_cross_gain, d_cross_shift,
        d_cross_query_bias, d_cross_value_bias, d_post_gain, d_post_shift, d_cross_output_bias, d_feed_gain,
        d_feed_shift, d_outer_bias, d_inner_bias, d_inner_gain, d_inner_shift,
    ) = [v.reshape(-1) for v in outs[10:28]]
    d_table, d_scale = outs[28].T, outs[29].reshape(-1)
    return (
        layer_output, dtok, memory_gradient,
        d_self_gain, d_self_shift, dwq, d_query_bias, dwk, dwv, d_value_bias, d_table, d_scale,
        dwo, d_output_bias, d_cross_gain, d_cross_shift, dwcq, d_cross_query_bias, dwck, dwcv, d_cross_value_bias,
        d_post_gain, d_post_shift, dwco, d_cross_output_bias, d_feed_gain, d_feed_shift, dw1, d_inner_bias,
        d_inner_gain, d_inner_shift, dw2, d_outer_bias,
    )


def solution(mesh):
    per_seq3, per_seq2, per_seq1 = P(("dp", "rep"), None, None), P(("dp", "rep"), None), P(("dp", "rep"))
    spread = P(None, "rep", "dp", None)
    in_specs = (per_seq3, per_seq3, per_seq1, per_seq2, per_seq1, P(), spread) + (P(),) * 30
    out_specs = (per_seq3, per_seq3, spread) + (P(),) * 30
    return jax.shard_map(local, mesh=mesh, in_specs=in_specs, out_specs=out_specs, check_vma=False)
```

```python
import functools

import jax
import jax.numpy as jnp
from jax import lax
from jax.experimental import pallas as pl
from jax.experimental.pallas import tpu as pltpu
from jax.sharding import PartitionSpec as P

NEG = -1e30
F32 = jnp.float32
BF16 = jnp.bfloat16
VMEM_LIMIT = 67043328

(
    SELF_GAIN,
    SELF_SHIFT,
    QUERY_BIAS,
    VALUE_BIAS,
    HEAD_SCALE,
    OUTPUT_BIAS,
    CROSS_GAIN,
    CROSS_SHIFT,
    CROSS_QUERY_BIAS,
    CROSS_VALUE_BIAS,
    POST_GAIN,
    POST_SHIFT,
    CROSS_OUTPUT_BIAS,
    FEED_GAIN,
    FEED_SHIFT,
    OUTER_BIAS,
) = range(16)


def mm(a, b):
    return jnp.dot(a, b, preferred_element_type=F32)


def mm_nt(a, b):
    return lax.dot_general(a, b, (((1,), (1,)), ((), ())), preferred_element_type=F32)


def mm_tn(a, b):
    return lax.dot_general(a, b, (((0,), (0,)), ((), ())), preferred_element_type=F32)


def normalize(x):
    center = x - jnp.mean(x, axis=-1, keepdims=True)
    spread = jnp.mean(center * center, axis=-1, keepdims=True)
    scale = lax.rsqrt(spread + 1e-05)
    return center * scale, scale


def norm_back(dy, hat, scale, gain):
    w = dy * gain
    first = jnp.mean(w, axis=-1, keepdims=True)
    second = jnp.mean(w * hat, axis=-1, keepdims=True)
    return (w - first - hat * second) * scale


def colsum(x):
    return jnp.sum(x, axis=0, keepdims=True)


def eight_rows(x):
    total = x[0:8]
    for k in range(8, x.shape[0], 8):
        total = total + x[k : k + 8]
    return total


def half_masks(rows):
    lane = lax.broadcasted_iota(jnp.int32, (rows, 128), 1)
    return (lane < 64, lane >= 64)


def pick(mask, x):
    return jnp.where(mask, x.astype(F32), 0.0).astype(BF16)


def pair_lanes(p):
    return pl.ds(pl.multiple_of(p * 128, 128), 128)


def head_rows(p, half):
    return pl.ds(pl.multiple_of(p * 128 + half * 64, 64), 64)


def fill_bias(buckets, table_rows, out_ref):
    length = buckets.shape[0]
    chunks = table_rows.shape[2] // 128
    low, high = buckets & 127, buckets >> 7
    key_place = lax.broadcasted_iota(jnp.int32, (length, 128), 0)
    lane = lax.broadcasted_iota(jnp.int32, (length, 128), 1)

    @pl.loop(0, out_ref.shape[0])
    def _(h):
        rows = [jnp.broadcast_to(table_rows[h, :, pl.ds(c * 128, 128)], (length, 128)) for c in range(chunks)]
        for tile in range(length // 128):
            cols, live = slice(tile * 128, (tile + 1) * 128), (tile + 1) * 128
            total = jnp.zeros((live, 128), F32)
            for c in range(chunks):
                got = jnp.take_along_axis(rows[c][:live], low[:live, cols], axis=1, mode="promise_in_bounds")
                total = jnp.where(high[:live, cols] == c, got, total)
            seen = jnp.where(key_place[:live] <= lane[:live] + tile * 128, total, NEG)
            out_ref[h, pl.ds(0, live), pl.ds(tile * 128, 128)] = seen
            if live < length:
                out_ref[h, pl.ds(live, length - live), pl.ds(tile * 128, 128)] = jnp.full((length - live, 128), NEG, F32)


def axis_bits(sizes):
    return [(axis, bit) for axis in ("rep", "dp") for bit in range(sizes[axis].bit_length() - 1)]


def stage_orders(sizes):
    plain = axis_bits(sizes)
    reps = sizes["rep"].bit_length() - 1
    swapped = list(plain)
    if reps >= 2 and len(plain) > reps:
        swapped = plain[: reps - 1] + [plain[reps], plain[reps - 1]] + plain[reps + 1 :]
    return plain, swapped


def flip(axis, bit):
    place = lax.axis_index(axis)
    return {axis: place + (1 - 2 * ((place // 2**bit) % 2)) * 2**bit}


def fold_sizes(rows, stages, tile):
    sizes, span = [], rows
    for _ in stages:
        span = span // 2 if span % (2 * tile) == 0 else span
        sizes.append(span)
    return sizes


class Reduction:
    def __init__(self, buf, start, rows, out, out_start, stages, tile, lands, send, recv, store):
        self.buf, self.out, self.tile, self.lands = buf, out, tile, lands
        self.send, self.recv, self.shift = send, recv, out_start - start
        folds, spreads = [], []
        base, span = start, rows
        for (axis, bit), size in zip(stages, fold_sizes(rows, stages, tile)):
            mine = (lax.axis_index(axis) // 2**bit) % 2
            peer = flip(axis, bit)
            halve = size < span
            keep = base + mine * size if halve else base
            give = base + (1 - mine) * size if halve else base
            folds.append((peer, give, keep, size))
            if halve:
                spreads.insert(0, (peer, keep, size))
            base, span = keep, size
        self.folds, self.spreads, self.own = folds, spreads, (base, span)
        self.store = pltpu.make_async_copy(self.part(buf, base, span), self.part(out, base + self.shift, span), store)

    def __len__(self):
        return len(self.folds) + len(self.spreads)

    def part(self, ref, start, size):
        return ref.at[pl.ds(start if isinstance(start, int) else pl.multiple_of(start, self.tile), size)]

    def copy(self, k):
        n = len(self.folds)
        if k < n:
            peer, give, keep, size = self.folds[k]
            land, at = self.lands[k]
            source, target = self.part(self.buf, give, size), land.at[pl.ds(at, size)]
        else:
            peer, base, size = self.spreads[k - n]
            target = self.part(self.out, base + self.shift, size)
            source = self.part(self.buf, base, size) if k == n else target
        return pltpu.make_async_remote_copy(
            src_ref=source, dst_ref=target, send_sem=self.send.at[k], recv_sem=self.recv.at[k],
            device_id=peer, device_id_type=pl.DeviceIdType.MESH,
        )

    def start(self, k):
        if k == len(self.folds):
            self.store.start()
        if k == min(len(self.folds) + 1, len(self)):
            self.store.wait()
        if k < len(self):
            self.copy(k).start()

    def finish(self, k):
        self.copy(k).wait()
        if k < len(self.folds):
            peer, give, keep, size = self.folds[k]
            land, at = self.lands[k]
            step = next(c for c in (128, 64, 48, 32, 16, 8) if size % c == 0)

            @pl.loop(0, size // step)
            def _(b):
                kept = pl.ds(pl.multiple_of(keep + b * step, self.tile), step)
                came = pl.ds(pl.multiple_of(at + b * step, self.tile), step)
                total = self.buf[kept, :].astype(F32) + land[came, :].astype(F32)
                self.buf[kept, :] = total.astype(self.buf.dtype)

    def advance(self, k):
        if 0 < k <= len(self):
            self.finish(k - 1)
        if k <= len(self):
            self.start(k)


def signal_all(sem, peers):
    for peer in peers:
        pl.semaphore_signal(sem, inc=1, device_id=peer, device_id_type=pl.DeviceIdType.MESH)


def scaled_heads(value_t, hs_ref):
    return jnp.concatenate([value_t[h * 64 : (h + 1) * 64] * hs_ref[h] for h in range(value_t.shape[0] // 64)], axis=0)


def self_forward(
    tlen, hs_ref, tok, bias_ref, vec_ref, wq, wk, wv, wo, q_ref, k_ref, v_ref, lse_ref, ot_ref, x1_ref, vt_ref
):
    length = tok.shape[0]
    x0 = tok.astype(F32)
    hat, _ = normalize(x0)
    h1 = (hat * vec_ref[SELF_GAIN][...] + vec_ref[SELF_SHIFT][...]).astype(BF16)
    q_ref[...] = ((mm(h1, wq[...]) + vec_ref[QUERY_BIAS][...]) * 0.125).astype(BF16)
    k_ref[...] = mm(h1, wk[...]).astype(BF16)
    value = (mm(h1, wv[...]) + vec_ref[VALUE_BIAS][...]).astype(BF16)
    v_ref[...] = value
    vt_ref[:, pl.ds(0, length)] = value.T
    key_place = lax.broadcasted_iota(jnp.int32, (length, length), 0)
    outside = jnp.where(key_place < tlen, 0.0, NEG)
    masks = half_masks(length)

    @pl.loop(0, q_ref.shape[1] // 128, unroll=4)
    def _(p):
        lanes = pair_lanes(p)
        kp, qp = k_ref[:, lanes], q_ref[:, lanes]
        for half in range(2):
            st = mm_nt(kp, pick(masks[half], qp)) + bias_ref[2 * p + half] + outside
            top = jnp.max(st, axis=0, keepdims=True)
            e = jnp.exp(st - top)
            total = colsum(e)
            ot = mm(vt_ref[head_rows(p, half), pl.ds(0, length)], e.astype(BF16))
            ot_ref[head_rows(p, half), :] = ot * (1.0 / total)
            lse_ref[2 * p + half] = top + jnp.log(total)

    c1 = scaled_heads(ot_ref[...], hs_ref).T.astype(BF16)
    x1_ref[...] = x0 + mm(c1, wo[...]) + vec_ref[OUTPUT_BIAS][...]


def cross_forward(mlen, mem_ref, vec_ref, x1, wcq, wck, wcv, q_ref, k_ref, v_ref, lse_ref, ot_ref, vt_ref, st_ref, arrive):
    length, mem_total = x1.shape[0], mem_ref.shape[0]
    hat, _ = normalize(x1)
    h2 = (hat * vec_ref[CROSS_GAIN][...] + vec_ref[CROSS_SHIFT][...]).astype(BF16)
    q_ref[...] = ((mm(h2, wcq[...]) + vec_ref[CROSS_QUERY_BIAS][...]) * 0.125).astype(BF16)
    arrive()
    step = 256

    @pl.loop(0, mem_total // step, unroll=4)
    def _(c):
        rows = pl.ds(pl.multiple_of(c * step, step), step)
        part = mem_ref[rows, :]
        k_ref[rows, :] = mm(part, wck[...]).astype(BF16)
        v_ref[rows, :] = (mm(part, wcv[...]) + vec_ref[CROSS_VALUE_BIAS][...]).astype(BF16)

    for c in range(mem_total // step):
        vt_ref[:, pl.ds(c * step, step)] = v_ref[pl.ds(c * step, step), :].T
    masks = half_masks(length)
    place = lax.broadcasted_iota(jnp.int32, (step, length), 0)
    tiles = length // 128

    @pl.loop(0, q_ref.shape[1] // 128, unroll=2)
    def _(p):
        lanes = pair_lanes(p)
        qp = q_ref[:, lanes]
        for half in range(2):
            qm = pick(masks[half], qp)
            top = jnp.full((1, length), -jnp.inf, F32)
            for c in range(mem_total // step):
                st = mm_nt(k_ref[pl.ds(c * step, step), lanes], qm)
                st = st + jnp.where(place < mlen - c * step, 0.0, NEG)
                for tile in range(tiles):
                    st_ref[tile, pl.ds(half * mem_total + c * step, step), :] = st[:, tile * 128 : (tile + 1) * 128]
                top = jnp.maximum(top, jnp.max(st, axis=0, keepdims=True))
            total = jnp.zeros((1, length), F32)
            ot = jnp.zeros((64, length), F32)
            for c in range(mem_total // step):
                rows = pl.ds(half * mem_total + c * step, step)
                st = jnp.concatenate([st_ref[tile, rows, :] for tile in range(tiles)], axis=1)
                e = jnp.exp(st - top)
                total = total + colsum(e)
                ot = ot + mm(vt_ref[head_rows(p, half), pl.ds(c * step, step)], e.astype(BF16))
            ot_ref[head_rows(p, half), :] = ot * (1.0 / total)
            lse_ref[2 * p + half] = top + jnp.log(total)


def feed_both(x2, g3, vec_ref, wide_ref, w1, w2, out_ref, acc, sums_ref, wide_sums_ref, u_ref, d_ref, df_ref, f_ref, r_ref, middle):
    length, hidden = u_ref.shape
    width = x2.shape[1]
    parts = hidden // width
    hat3, scale3 = normalize(x2)
    gain3 = vec_ref[FEED_GAIN][...]
    h3 = (hat3 * gain3 + vec_ref[FEED_SHIFT][...]).astype(BF16)
    cols = [pl.ds(c * width, width) for c in range(parts)]
    chunk = [pl.ds(c * length, length) for c in range(parts)]
    for c in range(parts):
        u_ref[:, cols[c]] = mm(h3, w1[cols[c], :])
    step = 64
    tiles = hidden // 128
    halves = d_ref.shape[0]

    def d_place(b, k):
        return k % halves, pl.ds(pl.multiple_of((k // halves) * length + b * step, step), step)

    @pl.loop(0, length // step)
    def _(b):
        rows = pl.ds(pl.multiple_of(b * step, step), step)
        u = u_ref[rows, :] + wide_ref[0][...]
        below = 0.5 * (1.0 + lax.erf(u * 0.7071067811865476))
        d = below + u * (jnp.exp(-0.5 * u * u) * 0.3989422804014327)
        for k in range(tiles):
            tile, place = d_place(b, k)
            d_ref[tile, place, :] = d[:, k * 128 : (k + 1) * 128]
        hat, scale = normalize(u * below)
        u_ref[rows, :] = hat
        f = (hat * wide_ref[1][...] + wide_ref[2][...]).astype(BF16)
        for c in range(parts):
            f_ref[pl.ds(pl.multiple_of(c * length + b * step, step), step), :] = f[:, c * width : (c + 1) * width]
        r_ref[rows, :] = jnp.broadcast_to(scale, (step, 128))

    x3 = x2 + vec_ref[OUTER_BIAS][...]
    for c in range(parts):
        x3 = x3 + mm(f_ref[chunk[c], :], w2[cols[c], :])
    out_ref[0] = x3.astype(BF16)
    sums_ref[0:1] += colsum(g3)
    e3 = g3.astype(BF16)
    for c in range(parts):
        acc[pl.ds(hidden + c * width, width), :] += mm_tn(f_ref[chunk[c], :], e3)
        df_ref[:, cols[c]] = mm_nt(e3, w2[cols[c], :])
    middle()

    @pl.loop(0, length // step)
    def _(b):
        rows = pl.ds(pl.multiple_of(b * step, step), step)
        dy, hat = df_ref[rows, :], u_ref[rows, :]
        part = dy * hat
        wide_sums_ref[0:8] += eight_rows(part)
        wide_sums_ref[8:16] += eight_rows(dy)
        da = norm_back(dy, hat, r_ref[rows, 0:1], wide_ref[1][...])
        pieces = []
        for k in range(tiles):
            tile, place = d_place(b, k)
            pieces.append(d_ref[tile, place, :])
        du = da * jnp.concatenate(pieces, axis=1)
        wide_sums_ref[16:24] += eight_rows(du)
        eu = du.astype(BF16)
        for c in range(parts):
            f_ref[pl.ds(pl.multiple_of(c * length + b * step, step), step), :] = eu[:, c * width : (c + 1) * width]

    dh3 = jnp.zeros(x2.shape, F32)
    h3t = h3.T
    for c in range(parts):
        acc[cols[c], :] += mm(h3t, f_ref[chunk[c], :])
        dh3 = dh3 + mm_nt(f_ref[chunk[c], :], w1[cols[c], :])
    sums_ref[1:2] += colsum(dh3 * hat3)
    sums_ref[2:3] += colsum(dh3)
    return g3 + norm_back(dh3, hat3, scale3, gain3)


def cross_backward(
    mlen, mem_ref, q_ref, k_ref, v_ref, lse_ref, delta_ref, do_ref, wck, wcv, dk_ref, dv_ref, dqt_ref, kt_ref,
    acc_key, acc_value, sums_ref, stage_ref, points,
):
    length, mem_total = q_ref.shape[0], mem_ref.shape[0]
    step = 256
    for c in range(mem_total // step):
        kt_ref[:, pl.ds(c * step, step)] = k_ref[pl.ds(c * step, step), :].T
    masks = half_masks(length)
    place = lax.broadcasted_iota(jnp.int32, (step, length), 0)
    pairs, chunks = q_ref.shape[1] // 128, mem_total // step

    @pl.loop(0, pairs)
    def _(p):
        @pl.when(p == pairs // 2)
        def _():
            points[0]()

        lanes = pair_lanes(p)
        qp, dop = q_ref[:, lanes], do_ref[:, lanes]
        qms = [pick(masks[half], qp) for half in range(2)]
        doms = [pick(masks[half], dop) for half in range(2)]
        lse = [lse_ref[2 * p + half] for half in range(2)]
        delta = [delta_ref[2 * p + half] for half in range(2)]
        for c in range(mem_total // step):
            rows = pl.ds(c * step, step)
            kp, vp = k_ref[rows, lanes], v_ref[rows, lanes]
            outside = jnp.where(place < mlen - c * step, 0.0, NEG)
            dv = jnp.zeros((step, 128), F32)
            dk = jnp.zeros((step, 128), F32)
            for half in range(2):
                st = mm_nt(kp, qms[half]) + outside
                pt = jnp.exp(st - lse[half])
                dpt = mm_nt(vp, doms[half])
                dst = (pt * (dpt - delta[half])).astype(BF16)
                stage_ref[:, pl.ds((half * chunks + c) * length, length)] = dst.astype(F32)
                dv = dv + mm(pt.astype(BF16), doms[half])
                dk = dk + mm(dst, qms[half])
            dv_ref[rows, lanes] = dv.astype(BF16)
            dk_ref[rows, lanes] = dk.astype(BF16)
        for half in range(2):
            staged = [stage_ref[:, pl.ds((half * chunks + c) * length, length)] for c in range(chunks)]
            dst = jnp.concatenate(staged, axis=0).astype(BF16)
            dqt_ref[head_rows(p, half), :] = mm(kt_ref[head_rows(p, half), :], dst)

    points[1]()
    acc_key[...] += mm_tn(mem_ref[...], dk_ref[...])
    acc_value[...] += mm_tn(mem_ref[...], dv_ref[...])

    @pl.loop(0, mem_total // step, unroll=4)
    def _(c):
        rows = pl.ds(pl.multiple_of(c * step, step), step)
        dk, dv = dk_ref[rows, :], dv_ref[rows, :]
        mem_ref[rows, :] = (mm_nt(dk, wck[...]) + mm_nt(dv, wcv[...])).astype(BF16)
        sums_ref[8:9] += colsum(dv.astype(F32))


def self_backward(tlen, bias_ref, q_ref, k_ref, v_ref, lse_ref, delta_ref, do_ref, dqt_ref, dk_ref, dv_ref, kt_ref, dbias_ref):
    length = q_ref.shape[0]
    kt_ref[:, pl.ds(0, length)] = k_ref[...].T
    key_place = lax.broadcasted_iota(jnp.int32, (length, length), 0)
    outside = jnp.where(key_place < tlen, 0.0, NEG)
    masks = half_masks(length)

    @pl.loop(0, q_ref.shape[1] // 128, unroll=4)
    def _(p):
        lanes = pair_lanes(p)
        qp, dop = q_ref[:, lanes], do_ref[:, lanes]
        kp, vp = k_ref[:, lanes], v_ref[:, lanes]
        dv = jnp.zeros((length, 128), F32)
        dk = jnp.zeros((length, 128), F32)
        for half in range(2):
            h = 2 * p + half
            qm, dom = pick(masks[half], qp), pick(masks[half], dop)
            st = mm_nt(kp, qm) + bias_ref[h] + outside
            pt = jnp.exp(st - lse_ref[h])
            dpt = mm_nt(vp, dom)
            dst = (pt * (dpt - delta_ref[h])).astype(BF16)
            rows = pl.ds(pl.multiple_of(h * length, length), length)
            wide_ds = dst.astype(F32)
            for tile in range(length // 128):
                dbias_ref[tile, rows, :] += wide_ds[:, tile * 128 : (tile + 1) * 128]
            dqt_ref[head_rows(p, half), :] = mm(kt_ref[head_rows(p, half), pl.ds(0, length)], dst)
            dv = dv + mm(pt.astype(BF16), dom)
            dk = dk + mm(dst, qm)
        dv_ref[:, lanes] = dv.astype(BF16)
        dk_ref[:, lanes] = dk.astype(BF16)


def bucket_totals(buckets_t, dbias_ref, out_ref, between):
    length = buckets_t.shape[0]
    heads = dbias_ref.shape[1] // length
    lo_places = lax.broadcasted_iota(jnp.int32, (32, 128), 0)
    group = 8

    def block(start, tiles, acc):
        rows = buckets_t[pl.ds(start, group), :]
        lefts, rights = [], []
        for k in range(group):
            for tile in tiles:
                ids = rows[k : k + 1, tile * 128 : (tile + 1) * 128]
                d = dbias_ref[tile, pl.ds(start + k, heads, stride=length), :]
                high = jnp.broadcast_to(ids >> 5, (heads, 128))
                lefts.append(jnp.concatenate([jnp.where(high == g, d, 0.0) for g in range(16)], axis=0).astype(BF16))
                rights.append(jnp.where(lo_places == (ids & 31), 1.0, 0.0).astype(BF16))
        return acc + mm_nt(jnp.concatenate(lefts, axis=1), jnp.concatenate(rights, axis=1))

    acc = jnp.zeros((16 * heads, 32), F32)
    tiles = length // 128
    for band in range(tiles):
        if band:
            between()
        live = range(band, tiles)

        def body(b, acc):
            return block(pl.multiple_of(band * 128 + b * group, group), live, acc)

        acc = lax.fori_loop(0, 128 // group, body, acc)
    for g in range(16):
        out_ref[:, g * 32 : (g + 1) * 32] = acc[g * heads : (g + 1) * heads]


SMALL_ROWS = 64
SUMS_B = 24
HEAD_ROWS = 40
TABLE_ROWS = 48


def piece_order(places):
    far, near = list(range(max(places // 2, 1), places)), list(range(1, places // 2))
    order = []
    for k in range(len(far)):
        order.append(far[k])
        if k < len(near):
            order.append(near[k])
    return order


def partner(me, places, k):
    if places & (places - 1):
        return lax.rem(me + k, places)
    for bit in range(places.bit_length() - 1):
        if (k >> bit) & 1:
            me = me + (1 - 2 * ((me // 2**bit) % 2)) * 2**bit
    return me


def layer_kernel(sizes, layout, tlen_ref, mlen_ref, hs_ref, tok_ref, cot_ref, mask_ref, buckets_ref, table_ref, *rest):
    mem_hbm, w1_hbm, w2_hbm = rest[:3]
    vec_ref, wide_ref = rest[3:19], rest[19:22]
    weights_hbm = rest[22:30]
    out_ref, dtok_ref, dmem_hbm, grads_hbm, small_hbm = rest[30:35]
    (
        mem_scr, w1s, w2s, acc, bias_ref, st_scr,
        q1_scr, k1_scr, v1_scr, lse1_scr, ot1_scr, x1_scr,
        kv_scr, q2_scr, do_scr, lse2_scr, delta_scr,
        vt_scr, ot_scr, u_scr, df_scr, r_scr, dk_scr, dv_scr,
        grads, land, small, small_land, wide_scr, hs_scr, table_scr, buckets_t_scr,
        load_sem, send_sem, recv_sem, own_sem, back_send, back_recv, back_own, group_send, group_recv, store_sem, ready_sem, late_sem,
        weight_sem, *weight_scr,
    ) = rest[35:]
    wq, wk, wv, wo, wcq, wck, wcv, wco = weight_scr
    seqs, mem_total, width = mem_scr.shape
    length, hidden, heads = tok_ref.shape[1], u_scr.shape[1], bias_ref.shape[0]
    places, piece = mem_hbm.shape[0], mem_hbm.shape[2]
    t = pl.program_id(0)
    me = lax.axis_index("dp")
    mine = pl.ds(pl.multiple_of(me * piece, piece), piece)
    k2_scr, v2_scr = kv_scr.at[pl.ds(0, mem_total)], kv_scr.at[pl.ds(mem_total, mem_total)]
    sums_a, sums_b = small.at[pl.ds(0, 8)], small.at[pl.ds(SUMS_B, 24)]
    base = 2 * hidden
    acc_at = lambda k: acc.at[pl.ds(base + k * width, width)]
    CROSS_OUT, OUT, QUERY, KEY, VALUE = range(5)
    order = piece_order(places)

    def own_in(s):
        return pltpu.make_async_copy(mem_hbm.at[me, s], mem_scr.at[s, mine], own_sem.at[s])

    def own_back(s):
        return pltpu.make_async_copy(mem_scr.at[s, mine], dmem_hbm.at[me, s], back_own.at[s])

    def loads():
        copies = []
        for c in range(hidden // width):
            cols = pl.ds(c * width, width)
            copies.append(pltpu.make_async_copy(w1_hbm.at[:, cols], w1s.at[cols], load_sem.at[c]))
        copies.append(pltpu.make_async_copy(w2_hbm, w2s, load_sem.at[hidden // width]))
        return copies

    def remote(source, target, send, recv, peer):
        return pltpu.make_async_remote_copy(
            src_ref=source, dst_ref=target, send_sem=send, recv_sem=recv, device_id={"dp": peer},
            device_id_type=pl.DeviceIdType.MESH,
        )

    def send_in(s, k):
        peer = partner(me, places, k)
        remote(mem_hbm.at[peer, s], mem_scr.at[s, mine], send_sem.at[s], recv_sem.at[s], peer).start()

    def send_back(s, k):
        peer = partner(me, places, k)
        rows = pl.ds(pl.multiple_of(peer * piece, piece), piece)
        remote(mem_scr.at[s, rows], dmem_hbm.at[me, s], back_send.at[s], back_recv.at[s], peer).start()

    def all_in(s):
        some = mem_scr.at[s, pl.ds(0, (places - 1) * piece)]
        return remote(some, some, send_sem.at[s], recv_sem.at[s], partner(me, places, 1))

    def all_back(s):
        some = dmem_hbm.at[pl.ds(0, places - 1), s]
        return remote(some, some, back_send.at[s], back_recv.at[s], partner(me, places, 1))

    plain, swapped = stage_orders(sizes)
    spare = pl.ds(length, mem_total - length)
    pools = {"first": w2s, "second": w1s, "key": dk_scr.at[spare], "value": dv_scr.at[spare], "land": land}
    buffers = {"grads": grads, "kv": kv_scr}
    reductions = []
    for r, (buf, start, rows, out_start, lands, color) in enumerate(layout):
        reductions.append(Reduction(
            buffers[buf], start, rows, grads_hbm, out_start, swapped if color == 1 else plain, 16,
            [(pools[name], at) for name, at in lands], group_send.at[r], group_recv.at[r], store_sem.at[r],
        ))
    last = len(layout)
    at, lands = 0, []
    for size in fold_sizes(SMALL_ROWS, plain, 8):
        lands.append((small_land, at))
        at += size
    reductions.append(Reduction(
        small, 0, SMALL_ROWS, small_hbm, 0, plain, 8, lands, group_send.at[last], group_recv.at[last], store_sem.at[last],
    ))
    first = [r for r, item in enumerate(layout) if item[0] == "grads" and item[1] < base]
    second = [r for r, item in enumerate(layout) if item[0] == "grads" and item[1] >= base]
    third = [r for r, item in enumerate(layout) if item[0] == "kv"]
    flips = [flip(axis, bit) for axis, bit in plain]

    steps = 4 * seqs
    begin_first, begin_second = 3 * (3 * seqs - 1), 3 * 3 * seqs
    planned = len(plain) == 5 and places == 8 and seqs == 4
    acts = {p: [] for p in range(3 * steps)}
    sends = {p: [] for p in range(3 * steps)}
    moved = [0] * len(reductions)
    queue = [(s, k) for s in range(seqs) for k in order]
    for p in range(3 * seqs, 3 * steps):
        if planned:
            count = SENDS[p - 3 * seqs]
        else:
            count = -(-len(order) * 2 // 7)
        while count and queue and p >= 3 * (seqs + 2 * queue[0][0] + 2):
            sends[p].append(queue.pop(0))
            count -= 1
        for r in ACTS[p - 3 * seqs] if planned else ():
            acts[p].append((r, moved[r]))
            moved[r] += 1

    def point(part, low, high):
        for step in range(low, high):
            p = 3 * step + part
            if acts[p] or sends[p] or (p == begin_first and flips):

                @pl.when(t == step)
                def _():
                    if p == begin_first and flips:
                        pl.semaphore_wait(ready_sem, len(flips))
                    for r, k in acts[p]:
                        reductions[r].advance(k)
                    for s, k in sends[p]:
                        send_back(s, k)

    @pl.when(t == 0)
    def _():
        bucket_load = pltpu.make_async_copy(buckets_ref, buckets_t_scr, load_sem.at[hidden // width + 1])
        bucket_load.start()
        for s in range(seqs):
            own_in(s).start()
        peers = [{"dp": partner(me, places, k)} for k in range(1, places)]
        peers += [flip(axis, bit) for axis, bit in plain if axis == "rep"]
        if peers:
            barrier = pltpu.get_barrier_semaphore()
            signal_all(barrier, peers)
        weight_loads = [
            pltpu.make_async_copy(a, b, weight_sem.at[k]) for k, (a, b) in enumerate(zip(weights_hbm, weight_scr))
        ]
        for c in weight_loads:
            c.start()
        if peers:
            pl.semaphore_wait(barrier, len(peers))
        for s in range(seqs):
            for k in order:
                send_in(s, k)
        for c in loads():
            c.start()
        for ref in (acc, small, wide_scr, hs_scr):
            ref[...] = jnp.zeros_like(ref)
        for h in range(heads):
            table_scr[h] = jnp.zeros(table_scr.shape[1:], F32)
            table_scr[h, :, : table_ref.shape[1]] = table_ref[h : h + 1, :]
        bucket_load.wait()
        buckets_t_scr[...] = buckets_t_scr[...].T
        fill_bias(buckets_t_scr[...], table_scr, bias_ref)
        for c in weight_loads:
            c.wait()

    @pl.when(t < seqs)
    def _():
        self_forward(
            tlen_ref[t], hs_ref, tok_ref[0], bias_ref, vec_ref, wq, wk, wv, wo,
            q1_scr.at[t], k1_scr.at[t], v1_scr.at[t], lse1_scr.at[t], ot1_scr.at[t], x1_scr.at[t], vt_scr,
        )

    @pl.when(t == seqs)
    def _():
        for c in loads():
            c.wait()

    inner = t - seqs
    s = inner // 2

    @pl.when((t >= seqs) & (t < 3 * seqs) & (inner % 2 == 0))
    def _():
        def arrive():
            own_in(s).wait()
            if places > 1:
                all_in(s).wait_recv()
            point(0, seqs, 3 * seqs)

        x1 = x1_scr[s]
        cross_forward(
            mlen_ref[s], mem_scr.at[s], vec_ref, x1, wcq, wck, wcv,
            q2_scr, k2_scr, v2_scr, lse2_scr, ot_scr, vt_scr, st_scr, arrive,
        )
        point(1, seqs, 3 * seqs)
        hat, scale = normalize(ot_scr[...].T)
        gain = vec_ref[POST_GAIN][...]
        c2 = (hat * gain + vec_ref[POST_SHIFT][...]).astype(BF16)
        x2 = x1 + mm(c2, wco[...]) + vec_ref[CROSS_OUTPUT_BIAS][...]
        here = lax.broadcasted_iota(jnp.int32, mask_ref.shape, 0) == s
        row = jnp.sum(jnp.where(here, mask_ref[...], 0), axis=0, keepdims=True).astype(F32)
        row = jnp.where(lax.broadcasted_iota(jnp.int32, (1, length), 1) < tlen_ref[s], row, 0.0)
        g3 = cot_ref[0].astype(F32) * jnp.broadcast_to(row, (8, length)).T[:, 0:1]
        g2 = feed_both(
            x2, g3, vec_ref, wide_ref, w1s, w2s, out_ref, acc, sums_a, wide_scr,
            u_scr, st_scr, df_scr, dk_scr, r_scr, lambda: point(2, seqs, 3 * seqs),
        )
        df_scr[:, pl.ds(0, width)] = g2
        sums_a[3:4] += colsum(g2)
        e2 = g2.astype(BF16)
        acc_at(CROSS_OUT)[...] += mm_tn(c2, e2)
        dc2 = mm_nt(e2, wco[...])
        sums_a[4:5] += colsum(dc2 * hat)
        sums_a[5:6] += colsum(dc2)
        do2 = norm_back(dc2, hat, scale, gain).astype(BF16)
        do_scr[...] = do2
        prod = do2.astype(F32).T * ot_scr[...]
        for h in range(heads):
            delta_scr[h] = colsum(prod[h * 64 : (h + 1) * 64])

    @pl.when(t == 3 * seqs - 2)
    def _():
        signal_all(ready_sem, flips)
        for k in range(3):
            total = colsum(wide_scr[8 * k : 8 * k + 8])
            for c in range(hidden // width):
                row = 8 + k * (hidden // width) + c
                small[row : row + 1] = total[:, c * width : (c + 1) * width]

        @pl.loop(0, base // 256)
        def _(b):
            rows = pl.ds(pl.multiple_of(b * 256, 256), 256)
            grads[rows, :] = acc[rows, :].astype(BF16)

    @pl.when((t >= seqs) & (t < 3 * seqs) & (inner % 2 == 1))
    def _():
        point(0, seqs, 3 * seqs)
        cross_backward(
            mlen_ref[s], mem_scr.at[s], q2_scr, k2_scr, v2_scr, lse2_scr, delta_scr, do_scr, wck, wcv,
            dk_scr, dv_scr, ot_scr, vt_scr, acc_at(KEY), acc_at(VALUE), sums_b, u_scr,
            [lambda: point(1, seqs, 3 * seqs), lambda: point(2, seqs, 3 * seqs)],
        )
        own_back(s).start()
        dq2 = (ot_scr[...].T.astype(BF16).astype(F32) * 0.125).astype(BF16)
        hat2, scale2 = normalize(x1_scr[s])
        gain2 = vec_ref[CROSS_GAIN][...]
        h2 = (hat2 * gain2 + vec_ref[CROSS_SHIFT][...]).astype(BF16)
        acc_at(QUERY)[...] += mm_tn(h2, dq2)
        sums_b[7:8] += colsum(dq2.astype(F32))
        dh2 = mm_nt(dq2, wcq[...])
        sums_b[5:6] += colsum(dh2 * hat2)
        sums_b[6:7] += colsum(dh2)
        g1 = df_scr[:, pl.ds(0, width)] + norm_back(dh2, hat2, scale2, gain2)
        x1_scr[s] = g1
        sums_b[4:5] += colsum(g1)
        c1t = scaled_heads(ot1_scr[s], hs_ref).astype(BF16)
        acc_at(OUT)[...] += mm(c1t, g1.astype(BF16))

    @pl.when(t == 3 * seqs - 1)
    def _():
        @pl.loop(0, 5 * width // 256)
        def _(b):
            rows = pl.ds(pl.multiple_of(base + b * 256, 256), 256)
            grads[rows, :] = acc[rows, :].astype(BF16)

        signal_all(late_sem, flips)
        st_scr[...] = jnp.zeros_like(st_scr)
        acc[pl.ds(0, 3 * width), :] = jnp.zeros((3 * width, width), F32)

    @pl.when(t >= 3 * seqs)
    def _():
        point(0, 3 * seqs, steps)
        s = t - 3 * seqs
        g1 = x1_scr[s]
        dc1t = mm_nt(g1.astype(BF16), wo[...]).T
        do1t = scaled_heads(dc1t, hs_ref).astype(BF16)
        do_scr[...] = do1t.T
        for h in range(heads):
            rows = slice(h * 64, (h + 1) * 64)
            o = ot1_scr[s, rows, :]
            hs_scr[h : h + 1, :] += colsum(o * dc1t[rows])
            delta_scr[h] = colsum(o * do1t[rows].astype(F32))
        dk_ref, dv_ref = dk_scr.at[pl.ds(0, length)], dv_scr.at[pl.ds(0, length)]
        self_backward(
            tlen_ref[s], bias_ref, q1_scr.at[s], k1_scr.at[s], v1_scr.at[s], lse1_scr.at[s], delta_scr, do_scr,
            ot_scr, dk_ref, dv_ref, vt_scr, st_scr,
        )
        point(1, 3 * seqs, steps)
        dq1 = (ot_scr[...].T.astype(BF16).astype(F32) * 0.125).astype(BF16)
        dk1, dv1 = dk_ref[...], dv_ref[...]
        hat1, scale1 = normalize(tok_ref[0].astype(F32))
        gain1 = vec_ref[SELF_GAIN][...]
        h1t = (hat1 * gain1 + vec_ref[SELF_SHIFT][...]).astype(BF16).T
        for k, d in enumerate((dq1, dk1, dv1)):
            acc[pl.ds(k * width, width), :] += mm(h1t, d)
        point(2, 3 * seqs, steps)
        sums_b[2:3] += colsum(dq1.astype(F32))
        sums_b[3:4] += colsum(dv1.astype(F32))
        dh1 = mm_nt(dq1, wq[...]) + mm_nt(dk1, wk[...]) + mm_nt(dv1, wv[...])
        sums_b[0:1] += colsum(dh1 * hat1)
        sums_b[1:2] += colsum(dh1)
        dtok_ref[0] = (g1 + norm_back(dh1, hat1, scale1, gain1)).astype(BF16)

    @pl.when(t == steps - 1)
    def _():
        @pl.loop(0, 3 * width // 256)
        def _(b):
            rows = pl.ds(pl.multiple_of(b * 256, 256), 256)
            kv_scr[rows, :] = acc[rows, :].astype(BF16)

        small[HEAD_ROWS : HEAD_ROWS + heads] = jnp.broadcast_to(
            jnp.sum(hs_scr[...], axis=1, keepdims=True), (heads, width)
        )
        def move(r):
            if r < 0:
                if queue:
                    send_back(*queue.pop(0))
            elif moved[r] <= len(reductions[r]):
                reductions[r].advance(moved[r])
                moved[r] += 1

        if flips:
            pl.semaphore_wait(late_sem, len(flips))
        for r in third:
            move(r)

        def between():
            for r in BETWEEN if planned else first + second + third:
                move(r)

        bucket_totals(buckets_t_scr, st_scr, small.at[pl.ds(TABLE_ROWS, heads)], between)
        for r in TAIL if planned else ():
            move(r)
        left = third + [last] + second + first
        while any(moved[r] <= len(reductions[r]) for r in left):
            for r in left:
                move(r)
            move(-1)
        while queue:
            move(-1)
        for s in range(seqs):
            own_back(s).wait()
            if places > 1:
                all_in(s).wait_send()
                all_back(s).wait_send()
                all_back(s).wait_recv()


ACTS = (
    (),
    (),
    (),
    (),
    (),
    (),
    (),
    (),
    (),
    (),
    (),
    (),
    (),
    (),
    (),
    (),
    (),
    (),
    (),
    (),
    (),
    (0, 1),
    (2, 3, 0, 1),
    (2, 3),
    (4, 5, 0, 1),
    (4, 5, 2),
    (),
    (1,),
    (3, 2, 0),
    (1,),
    (),
    (2, 3, 0, 4, 1),
    (),
    (),
    (5, 3, 2, 4, 0),
    (1,),
)
SENDS = (0, 0, 0, 0, 0, 0, 0, 0, 0, 0, 0, 0, 0, 1, 2, 0, 2, 2, 1, 2, 0, 0, 2, 2, 0, 1, 0, 2, 0, 0, 2, 0, 0, 2, 0, 0)
BETWEEN = (2, 3, 4, 5, 6, 7, 8, -1)
TAIL = (0, 9, 1, 2, 3, 6, 9, 5, 4, 8, 7, 6, 0, 9, 1, 3, -1, -1, 7, 5, 2, 6, 4, 8, 9, 0, 7, 3, 4, -1, -1, 1, 8, 9, 5, 6, 7, 1, 0, 2, 0, -1, -1, 8, 4, 2, 5, 9, 3, 6, 7, 3, 6, 8, 7, 5, 4, 9, 8, 6, 7, 4, 8, 6, 5, 9, 6, 7, 5, 9, 8, 7, 8)
MEMBERS = (('first', 1, 2), ('first', 0, 2), ('first', 0, 2), ('first', 0, 2), ('second', 0, 3), ('second', 0, 2), ('third', 1, 1), ('third', 1, 1), ('third', 0, 1))


def reduction_layout(sizes, width, hidden, spare):
    plain, _ = stage_orders(sizes)
    base = 2 * hidden
    members, at = [], {"first": 0, "second": 2 * hidden, "third": 0}
    for name, color, units in MEMBERS:
        rows = units * width
        out_start = at[name] + (base + 5 * width if name == "third" else 0)
        members.append(("kv" if name == "third" else "grads", at[name], rows, out_start, color))
        at[name] += rows
    used = {"first": 0, "second": 0, "key": 0, "value": 0, "land": 0}
    layout = []
    for buf, start, rows, out_start, color in members:
        lands = []
        for size in fold_sizes(rows, plain, 16):
            room = {"first": hidden, "second": hidden} if buf == "grads" else {"key": spare, "value": spare}
            name = next((n for n in room if used[n] + size <= room[n]), "land")
            lands.append((name, used[name]))
            used[name] += size
        layout.append((buf, start, rows, out_start, lands, color))
    return layout, max(used["land"], 16)


def whole_layer(sizes, tlen, mlen, head_scale, tokens, cotangent, mask, buckets, table, memory, w1, w2, vecs, wides, weights):
    seqs, length, width = tokens.shape
    places, _, piece, _ = memory.shape
    mem_total = places * piece
    heads, hidden = head_scale.shape[0], w1.shape[1]
    layout, land = reduction_layout(sizes, width, hidden, mem_total - length)
    plain, _ = stage_orders(sizes)
    small_land = max(sum(fold_sizes(SMALL_ROWS, plain, 8)), 8)
    slots = max(2 * len(plain), 1)
    several = places > 1 or sizes["rep"] > 1
    sds = jax.ShapeDtypeStruct
    anywhere = pl.BlockSpec(memory_space=pl.ANY)
    const = lambda a: pl.BlockSpec(a.shape, lambda t, *_: (0,) * a.ndim, pipeline_mode=pl.Buffered(1))
    seq = lambda idx: pl.BlockSpec((1, length, width), lambda t, *_: (idx(t), 0, 0))
    ends = lambda t: jnp.where(t < 3 * seqs, jnp.minimum(t, seqs - 1), t - 3 * seqs)
    middle = lambda t: jnp.clip((t - seqs) // 2, 0, seqs - 1)
    late = lambda t: jnp.maximum(t - 3 * seqs, 0)
    tall = heads * length
    scratch = [
        ((seqs, mem_total, width), BF16), ((hidden, width), BF16), ((hidden, width), BF16),
        ((2 * hidden + 5 * width, width), F32), ((heads, length, length), F32),
        ((length // 128, max(tall, 2 * mem_total, hidden * length * 128 // (length * 128)), 128), F32),
        ((seqs, length, width), BF16), ((seqs, length, width), BF16), ((seqs, length, width), BF16),
        ((seqs, heads, 1, length), F32), ((seqs, width, length), F32), ((seqs, length, width), F32),
        ((2 * mem_total, width), BF16), ((length, width), BF16), ((length, width), BF16),
        ((heads, 1, length), F32), ((heads, 1, length), F32),
        ((width, mem_total), BF16), ((width, length), F32), ((length, hidden), F32), ((length, hidden), F32),
        ((length, 128), F32), ((max(mem_total, hidden // width * length), width), BF16), ((mem_total, width), BF16),
        ((2 * hidden + 5 * width, width), BF16), ((land, width), BF16), ((SMALL_ROWS, width), F32), ((small_land, width), F32),
        ((24, hidden), F32), ((heads, length), F32), ((heads, 1, 512), F32), ((length, length), jnp.int32),
    ]
    dma = pltpu.SemaphoreType.DMA
    groups = len(layout) + 1
    return pl.pallas_call(
        functools.partial(layer_kernel, sizes, layout),
        out_shape=[
            sds(tokens.shape, BF16), sds(tokens.shape, BF16), sds(memory.shape, BF16),
            sds((2 * hidden + 8 * width, width), BF16), sds((SMALL_ROWS, width), F32),
        ],
        grid_spec=pltpu.PrefetchScalarGridSpec(
            num_scalar_prefetch=3,
            grid=(4 * seqs,),
            in_specs=[seq(ends), seq(middle), const(mask), anywhere, const(table), anywhere, anywhere, anywhere]
            + [const(a) for a in vecs + wides] + [anywhere] * len(weights),
            out_specs=[seq(middle), seq(late), anywhere, anywhere, anywhere],
            scratch_shapes=[pltpu.VMEM(shape, dtype) for shape, dtype in scratch] + [
                dma((hidden // width + 2,)), dma((seqs,)), dma((seqs,)), dma((seqs,)), dma((seqs,)), dma((seqs,)),
                dma((seqs,)), dma((groups, slots)), dma((groups, slots)), dma((groups,)), pltpu.SemaphoreType.REGULAR, pltpu.SemaphoreType.REGULAR,
                dma((len(weights),)),
            ] + [pltpu.VMEM(a.shape, BF16) for a in weights],
        ),
        compiler_params=pltpu.CompilerParams(
            vmem_limit_bytes=VMEM_LIMIT, collective_id=0 if several else None, has_side_effects=True
        ),
        name="layer",
    )(tlen, mlen, head_scale, tokens, cotangent, mask, buckets, table, memory, w1, w2, *vecs, *wides, *weights)


def unpack_kernel(count, grads_hbm, small_ref, *refs):
    kept, refs = refs[:count], refs[count:]
    passed, refs = refs[:count], refs[count:]
    big, vectors, tail = refs[:10], refs[10:28], refs[28:]
    table_ref, scale_ref, rough, exact = tail[:4]
    holds, (in_sem, out_sem, hold_in, hold_out) = tail[4:-4], tail[-4:]
    dw1, dw2, rest = big[0], big[1], big[2:]
    width = grads_hbm.shape[1]
    parts = dw1.shape[1] // width
    targets = [dw1.at[:, pl.ds(c * width, width)] for c in range(parts)]
    targets += [dw2.at[pl.ds(c * width, width)] for c in range(parts)] + list(rest)
    rows = [pl.ds(k * width, width) for k in range(len(targets))]
    into = [pltpu.make_async_copy(grads_hbm.at[r], rough.at[r], in_sem.at[k]) for k, r in enumerate(rows)]
    out = [pltpu.make_async_copy(exact.at[r], target, out_sem.at[k]) for k, (r, target) in enumerate(zip(rows, targets))]
    take = [pltpu.make_async_copy(a, hold, hold_in.at[k]) for k, (a, hold) in enumerate(zip(kept, holds))]
    give = [pltpu.make_async_copy(hold, a, hold_out.at[k]) for k, (a, hold) in enumerate(zip(passed, holds))]
    for c in into + take:
        c.start()
    for row, ref in zip(VECTOR_ROWS, vectors):
        for c in range(ref.shape[1] // width):
            ref[:, c * width : (c + 1) * width] = small_ref[row + c : row + c + 1]
    heads = scale_ref.shape[1]
    table_ref[...] = small_ref[TABLE_ROWS : TABLE_ROWS + heads, : table_ref.shape[1]]
    block = small_ref[HEAD_ROWS : HEAD_ROWS + heads]
    diagonal = lax.broadcasted_iota(jnp.int32, block.shape, 0) == lax.broadcasted_iota(jnp.int32, block.shape, 1)
    scale_ref[...] = colsum(jnp.where(diagonal, block, 0.0))[:, :heads]
    step = 64
    for k in range(len(targets)):
        into[k].wait()

        @pl.loop(0, width // step)
        def _(b):
            part = pl.ds(pl.multiple_of(k * width + b * step, step), step)
            exact[part, :] = rough[part, :].astype(F32)

        out[k].start()
    for a, b in zip(take, give):
        a.wait()
        b.start()
    for c in out + give:
        c.wait()


VECTOR_ROWS = (24, 25, 26, 27, 28, 29, 30, 31, 32, 4, 5, 3, 1, 2, 0, 16, 8, 12)


def unpack(grads, small, kept, hidden, heads, buckets):
    total, width = grads.shape
    sds = jax.ShapeDtypeStruct
    big = [sds((width, hidden), F32), sds((hidden, width), F32)] + [sds((width, width), F32)] * 8
    vectors = [sds((1, width), F32)] * 15 + [sds((1, hidden), F32)] * 3
    tail = [sds((heads, buckets), F32), sds((1, heads), F32)]
    anywhere, inside = pl.BlockSpec(memory_space=pl.ANY), pl.BlockSpec(memory_space=pltpu.VMEM)
    dma = pltpu.SemaphoreType.DMA
    count = len(kept)
    outs = pl.pallas_call(
        functools.partial(unpack_kernel, count),
        out_shape=[sds(a.shape, a.dtype) for a in kept] + big + vectors + tail,
        in_specs=[anywhere, inside] + [anywhere] * count,
        out_specs=[anywhere] * (count + 10) + [inside] * (len(vectors) + len(tail)),
        scratch_shapes=[pltpu.VMEM((total, width), BF16), pltpu.VMEM((total, width), F32)]
        + [pltpu.VMEM(a.shape, a.dtype) for a in kept]
        + [dma((total // width,)), dma((total // width,)), dma((count,)), dma((count,))],
        compiler_params=pltpu.CompilerParams(vmem_limit_bytes=VMEM_LIMIT),
        name="unpack",
    )(grads, small, *kept)
    return outs[:count], outs[count:]


def local(
    tokens, cotangent, target_lengths, task_mask, memory_lengths, position_buckets, memory,
    self_gain, self_shift, query_weight, query_bias, key_weight, value_weight, value_bias, position_table, head_scale,
    output_weight, output_bias, cross_gain, cross_shift, cross_query, cross_query_bias, cross_key, cross_value,
    cross_value_bias, post_gain, post_shift, cross_output, cross_output_bias, feed_gain, feed_shift, inner_weight,
    inner_bias, inner_gain, inner_shift, outer_weight, outer_bias,
):
    heads = head_scale.shape[0]
    bucket_count = position_table.shape[0]
    hidden = inner_weight.shape[1]
    table_t = position_table.T
    row = lambda v: v.reshape(1, -1)
    vecs = [row(v) for v in (
        self_gain, self_shift, query_bias, value_bias, output_bias, output_bias, cross_gain, cross_shift,
        cross_query_bias, cross_value_bias, post_gain, post_shift, cross_output_bias, feed_gain, feed_shift, outer_bias,
    )]
    wides = [row(v) for v in (inner_bias, inner_gain, inner_shift)]
    sizes = {"dp": lax.axis_size("dp"), "rep": lax.axis_size("rep")}
    layer_output, dtok, memory_gradient, grads, small = whole_layer(
        sizes, target_lengths, memory_lengths, head_scale, tokens, cotangent, task_mask, position_buckets, table_t,
        memory, inner_weight, outer_weight, vecs, wides,
        [query_weight, key_weight, value_weight, output_weight, cross_query, cross_key, cross_value, cross_output],
    )
    (layer_output, dtok, memory_gradient), outs = unpack(
        grads, small, [layer_output, dtok, memory_gradient], hidden, heads, bucket_count
    )
    dw1, dw2, dwco, dwo, dwcq, dwck, dwcv, dwq, dwk, dwv = outs[:10]
    (
        d_self_gain, d_self_shift, d_query_bias, d_value_bias, d_output_bias, d_cross_gain, d_cross_shift,
        d_cross_query_bias, d_cross_value_bias, d_post_gain, d_post_shift, d_cross_output_bias, d_feed_gain,
        d_feed_shift, d_outer_bias, d_inner_bias, d_inner_gain, d_inner_shift,
    ) = [v.reshape(-1) for v in outs[10:28]]
    d_table, d_scale = outs[28].T, outs[29].reshape(-1)
    return (
        layer_output, dtok, memory_gradient,
        d_self_gain, d_self_shift, dwq, d_query_bias, dwk, dwv, d_value_bias, d_table, d_scale,
        dwo, d_output_bias, d_cross_gain, d_cross_shift, dwcq, d_cross_query_bias, dwck, dwcv, d_cross_value_bias,
        d_post_gain, d_post_shift, dwco, d_cross_output_bias, d_feed_gain, d_feed_shift, dw1, d_inner_bias,
        d_inner_gain, d_inner_shift, dw2, d_outer_bias,
    )


def solution(mesh):
    per_seq3, per_seq2, per_seq1 = P(("dp", "rep"), None, None), P(("dp", "rep"), None), P(("dp", "rep"))
    spread = P(None, "rep", "dp", None)
    in_specs = (per_seq3, per_seq3, per_seq1, per_seq2, per_seq1, P(), spread) + (P(),) * 30
    out_specs = (per_seq3, per_seq3, spread) + (P(),) * 30
    return jax.shard_map(local, mesh=mesh, in_specs=in_specs, out_specs=out_specs, check_vma=False)
```
